256 devices in a mesh: ctx: 4 (over y_lo, core), exp: 64 (over z, x, y_hi).
Axes of the slice: x: 4, y: 4 (y_hi: 2, y_lo: 2; y = y_hi * 2 + y_lo), z: 8, core: 2. Of those that a mesh axis runs over, the one named last changes fastest.
Arguments:
- residual_in: bfloat16 [2048, 3584], P(('ctx', 'exp')), may hold values from -1.5 to 1.5
- norm_gain: float32 [3584], replicated, may hold values from 0.25 to 1.75
- q_nope: bfloat16 [2048, 128, 512], P('ctx', 'exp'), may hold values from -64 to 64
- q_rope: bfloat16 [2048, 8192], P('ctx', 'exp'), may hold values from -6 to 6
- latent: bfloat16 [2048, 512], P('ctx'), may hold values from -6 to 6
- k_rope: bfloat16 [2048, 64], P('ctx'), may hold values from -6 to 6
- doc_ids: int32 [2048], P('ctx'), may hold values from 0 to 3, never falling along the last dimension, each value on 1 to 1024 neighbouring positions
- uv_weight: bfloat16 [128, 512, 128], P('exp'), may hold values from -0.25 to 0.25
- out_weight: bfloat16 [16384, 3584], P('exp'), may hold values from -0.046875 to 0.046875
- expert_ids: int32 [2048, 8], P(('ctx', 'exp')), may hold values from 0 to 63, all different within a row; in each aligned block of 8 rows (0 to 7, 8 to 15, ...) at most 2 rows name the same one
- gate_levels: int32 [2048, 8], P(('ctx', 'exp')), may hold values from 1 to 255
- bin_ids: int32 [2048, 8], P(('ctx', 'exp')), may hold values from 0 to 2047
- gate_weight: bfloat16 [64, 3584, 1024], P('exp', None, 'ctx'), may hold values from -0.09375 to 0.09375
- up_weight: bfloat16 [64, 3584, 1024], P('exp', None, 'ctx'), may hold values from -0.09375 to 0.09375
- down_weight: bfloat16 [64, 1024, 3584], P('exp', 'ctx'), may hold values from -0.1875 to 0.1875
Outputs:
- layer_out: bfloat16 [2048, 3584], P(('ctx', 'exp'))
- histogram: float32 [64, 2048], P('exp', 'ctx')
The draws below stay inside these ranges and needn't reach their ends.
Inputs may be any that keep to these rules, and one draw needn't show every extreme that they name: `expert_ids`: each row names 8 different experts; within the rows of one device (aligned blocks of 8 rows) no expert is named more than 2 times, a bound that some block reaches. `doc_ids`: document numbers never fall along the sequence; each document has 1 to 1024 tokens, one exactly 1024.
All inputs are finite; a program needn't handle non-finite values.
Results may differ from the reference program's by a relative error of at most 0.03.
Values may be sent and summed in bfloat16 or wider, within the bound.
A program may use at most 128 MiB of HBM per device.

```python
import math
import jax
import jax.numpy as jnp
import numpy as np
from jax import lax

D = 3584
LAT = 512
ROPE = 64
VDIM = 128
HID = 1024
TOPK = 8
NBINS = 2048
BLOCK = 512
SEQ = 2048
HEADS = 128
EXPERTS = 64
TOK = 8
CAP = 2
N_CTX = 4
N_EXP = 64


def shared_latent(key):
    return jax.random.normal(jax.random.fold_in(key, 11), (SEQ, LAT), jnp.float32)


def draw_latent(key, part):
    base = shared_latent(key)
    return jnp.clip(base, -6.0, 6.0).astype(jnp.bfloat16)


def draw_q_nope(key, part):
    values = jax.random.normal(jax.random.fold_in(key, 23), (SEQ, HEADS, LAT), jnp.float32)
    return jnp.clip(values, -64.0, 64.0).astype(jnp.bfloat16)


def set_ends(array, own_key, low, top_value):
    dims = array.shape
    place = [jax.random.randint(jax.random.fold_in(own_key, axis), (), 0, dims[axis]) for axis in range(len(dims))]
    array = array.at[tuple(place)].set(low)
    longest = dims.index(max(dims))
    place[longest] = (place[longest] + 1) % dims[longest]
    return array.at[tuple(place)].set(top_value)


def shard_levels(rng, dims, split, least, top_value):
    loudness = 1.0
    for axis_at, blocks in split:
        heights = jax.random.uniform(jax.random.fold_in(jax.random.fold_in(rng, 6), axis_at), (blocks,), jnp.float32, least / len(split), top_value / len(split))
        loudness = loudness * jnp.repeat(jnp.exp(heights), dims[axis_at] // blocks).reshape((-1,) + (1,) * (len(dims) - 1 - axis_at))
    return loudness


def profile(amount, total, bound, slope):
    weights = [(1 << 20) // math.isqrt(standing ** slope) + 1 for standing in range(2, amount + 1)]
    surplus, given = total - bound - (amount - 1), [1] * (amount - 1)
    while surplus > 0:
        movable = [i for i in range(amount - 1) if given[i] < bound]
        pool, remaining = sum([weights[i] for i in movable]), surplus
        for i in movable:
            extra = min(bound - given[i], max(1, remaining * weights[i] // pool), surplus)
            given[i] = given[i] + extra
            surplus = surplus - extra
    return np.array([bound] + given)


def uneven_parts(own_key, count, total, most, slope):
    if count == 2:
        one = jax.random.randint(own_key, (), max(1, total - most), min(most, total - 1) + 1)
        return jnp.stack([one, total - one])
    lengths = jnp.asarray(profile(count, total, most, slope), jnp.int32)
    twos = (count - 1) // 2
    giver, taker = lengths[1:1 + 2 * twos:2], lengths[2:2 + 2 * twos:2]
    room = jnp.minimum(giver - 1, most - taker)
    moved = jax.random.randint(jax.random.fold_in(own_key, 1), (twos,), 0, 1 << 20) % (room + 1)
    lengths = lengths.at[1:1 + 2 * twos:2].set(giver - moved).at[2:2 + 2 * twos:2].set(taker + moved)
    return lengths[jax.random.permutation(jax.random.fold_in(own_key, 2), count)]


def routed_block(own_key, own, number, rows, amount, top, bound, skew):
    order = jax.random.permutation(own_key, amount)
    crowded, usual = shares(amount, rows * top, bound, skew, True), shares(amount, rows * top, bound, skew, False)
    places = jnp.arange(amount)

    def named(tallies, offset_by):
        used = int((tallies > 0).sum())
        fixed = max(1, used // 4)
        moved = fixed + (places - fixed + offset_by * (used - fixed)) % max(1, amount - fixed)
        return jnp.zeros((amount,), jnp.int32).at[order[jnp.where(places < fixed, places, moved)]].set(jnp.asarray(tallies, jnp.int32))

    tallies = jnp.where(number % 4 == 0, named(crowded, number // 4), named(usual, number - number // 4 - 1))
    mixed = jax.random.permutation(jax.random.fold_in(own, 3), amount)
    donor, sink = mixed[0:amount // 2 * 2:2], mixed[1:amount // 2 * 2:2]
    room = jnp.minimum(tallies[donor] - 1, bound - tallies[sink]) // 2
    room = jnp.where((donor == order[0]) | (sink == order[0]) | (tallies[sink] == 0), 0, jnp.maximum(room, 0))
    moved = jax.random.randint(jax.random.fold_in(own, 4), (amount // 2,), 0, 1 << 20) % (room + 1)
    tallies = tallies.at[donor].add(-moved).at[sink].add(moved)
    labels = jnp.searchsorted(jnp.cumsum(tallies), jnp.arange(rows * top), side="right").astype(jnp.int32)
    listing = labels.reshape(top, rows).T
    listing = listing[jax.random.permutation(jax.random.fold_in(own, 1), rows)]
    offset_by = jax.random.randint(jax.random.fold_in(own, 2), (rows, 1), 0, top)
    return jnp.take_along_axis(listing, (jnp.arange(top)[None, :] + offset_by) % top, axis=1)


def shares(number_of, total, reach, slope, full):
    weights = [(1 << 20) // math.isqrt(grade ** slope) + 1 for grade in range(1, number_of + 1)]
    largest = reach if full else min(reach, max(-(-total // number_of), total * weights[0] // sum(weights)))
    least = 1 if total - largest >= number_of - 1 else 0
    given, rest = [largest] + [least] * (number_of - 1), total - largest - least * (number_of - 1)
    while rest > 0:
        candidates = [i for i in range(1, number_of) if given[i] < largest] or [i for i in range(1, number_of) if given[i] < reach]
        mass, budget = sum([weights[i] for i in candidates]), rest
        for i in candidates:
            addition = min(reach - given[i], max(1, budget * weights[i] // mass), rest)
            given[i] = given[i] + addition
            rest = rest - addition
    return np.array(given)


def bell_draw(rng, extent, spread, reach, split=(), held_as=jnp.bfloat16):
    loudness = shard_levels(rng, extent, split, -0.22, 0.18) if split else 1.0
    values = jax.random.normal(rng, extent, jnp.float32) * spread * loudness
    return jnp.minimum(jnp.maximum(values, -reach), reach).astype(held_as)


def setup_inputs(seed: int = 0) -> dict:
    key_of = jax.random.split(jax.random.key(seed), 16)
    residual_in = bell_draw(key_of[0], (SEQ, D), 0.25, 1.5, ((0, 256),))
    norm_gain = jnp.clip(1.0 + 0.15 * jax.random.normal(key_of[1], (D,), jnp.float32), 0.25, 1.75)
    q_nope = draw_q_nope(jax.random.fold_in(key_of[15], 71), 0)
    q_rope = bell_draw(key_of[3], (SEQ, HEADS * ROPE), 1.0, 6.0, ((0, 4), (1, 64)))
    latent = draw_latent(jax.random.fold_in(key_of[15], 71), 0)
    k_rope = bell_draw(key_of[5], (SEQ, ROPE), 1.0, 6.0, ((0, 4),))
    doc_ids = jnp.searchsorted(jnp.cumsum(uneven_parts(key_of[6], N_CTX, SEQ, 2 * BLOCK, 0)), jnp.arange(SEQ), side="right").astype(jnp.int32)
    uv_weight = bell_draw(key_of[7], (HEADS, LAT, VDIM), LAT ** -0.5, 0.25, ((0, 64),))
    out_weight = bell_draw(key_of[8], (HEADS * VDIM, D), (HEADS * VDIM) ** -0.5, 0.046875, ((0, 64),))
    expert_ids_keys = jax.random.split(jax.random.fold_in(key_of[9], 1), SEQ // TOK)
    expert_ids_turns = jax.random.permutation(jax.random.fold_in(key_of[9], 3), SEQ // TOK)
    expert_ids = jax.vmap(lambda own, number: routed_block(jax.random.fold_in(key_of[9], 2), own, number, TOK, EXPERTS, TOPK, CAP, 2))(expert_ids_keys, expert_ids_turns).reshape((SEQ, TOPK))
    gate_levels = set_ends(jax.random.randint(key_of[10], (SEQ, TOPK), 1, 256), jax.random.fold_in(key_of[10], 1), 1, 255).astype(jnp.int32)
    bin_ids = set_ends(jax.random.randint(key_of[11], (SEQ, TOPK), 0, NBINS), jax.random.fold_in(key_of[11], 1), 0, NBINS - 1).astype(jnp.int32)
    gate_weight = bell_draw(key_of[12], (EXPERTS, D, HID), D ** -0.5, 0.09375, ((0, 64), (2, 4)))
    up_weight = bell_draw(key_of[13], (EXPERTS, D, HID), D ** -0.5, 0.09375, ((0, 64), (2, 4)))
    down_weight = bell_draw(key_of[14], (EXPERTS, HID, D), HID ** -0.5, 0.1875, ((0, 64), (1, 4)))
    return dict(residual_in=residual_in, norm_gain=norm_gain, q_nope=q_nope, q_rope=q_rope, latent=latent, k_rope=k_rope, doc_ids=doc_ids, uv_weight=uv_weight, out_weight=out_weight, expert_ids=expert_ids, gate_levels=gate_levels, bin_ids=bin_ids, gate_weight=gate_weight, up_weight=up_weight, down_weight=down_weight)


softmax_scale = 192.0 ** (-0.5)
norm_eps = 1e-06

def route_slots(expert_ids, experts, capacity):
    flat_ids = expert_ids.reshape(-1)
    onehot = (flat_ids[:, None] == jnp.arange(experts, dtype=jnp.int32)[None, :]).astype(jnp.int32)
    before = jnp.cumsum(onehot, axis=0) - onehot
    slot_rank = lax.optimization_barrier(jnp.sum(before * onehot, axis=1))
    return (flat_ids * capacity + slot_rank).reshape(expert_ids.shape)

def reference(residual_in, norm_gain, q_nope, q_rope, latent, k_rope, doc_ids, uv_weight, out_weight, expert_ids, gate_levels, bin_ids, gate_weight, up_weight, down_weight):
    positions = jnp.arange(SEQ, dtype=jnp.int32)
    allowed = (positions[None, :] <= positions[:, None]) & (doc_ids[None, :] == doc_ids[:, None])
    query_rope = q_rope.reshape(SEQ, HEADS, ROPE)

    def attend_head(head_index):
        head_nope = q_nope[:, head_index, :]
        head_rope = query_rope[:, head_index, :]
        scores = jnp.dot(head_nope, latent.T, preferred_element_type=jnp.float32)
        scores = (scores + jnp.dot(head_rope, k_rope.T, preferred_element_type=jnp.float32)) * softmax_scale
        scores = jnp.where(allowed, scores, -jnp.inf)
        row_max = lax.optimization_barrier(jnp.max(scores, axis=1, keepdims=True))
        exp_terms = jnp.where(allowed, jnp.exp(scores - row_max), 0.0)
        weights = (exp_terms / lax.optimization_barrier(jnp.sum(exp_terms, axis=1, keepdims=True))).astype(jnp.bfloat16)
        context = jnp.dot(weights, latent, preferred_element_type=jnp.float32).astype(jnp.bfloat16)
        return jnp.dot(context, uv_weight[head_index], preferred_element_type=jnp.float32).astype(jnp.bfloat16)
    values = lax.map(attend_head, jnp.arange(HEADS, dtype=jnp.int32))
    values = values.transpose(1, 0, 2).reshape(SEQ, HEADS * VDIM)
    attended = jnp.dot(values, out_weight, preferred_element_type=jnp.float32)
    stream_state = residual_in.astype(jnp.float32) + attended
    normed = (stream_state * lax.rsqrt(lax.optimization_barrier(jnp.mean(stream_state * stream_state, axis=1, keepdims=True)) + norm_eps) * norm_gain).astype(jnp.bfloat16)
    device_count = N_CTX * N_EXP
    slot_total = EXPERTS * CAP
    slot_index = jnp.arange(slot_total, dtype=jnp.int32)
    block_ids = expert_ids.reshape(device_count, TOK, TOPK)
    destination = jax.vmap(lambda ids_block: route_slots(ids_block, EXPERTS, CAP))(block_ids)

    def pack_slots(dest_block, row_block, bin_block):
        slot_match = dest_block[:, :, None] == slot_index[None, None, :]
        selector = lax.optimization_barrier(jnp.sum(slot_match.astype(jnp.int32), axis=1)).astype(jnp.bfloat16)
        outgoing = jnp.einsum('ts,td->sd', selector, row_block, preferred_element_type=jnp.float32).astype(jnp.bfloat16)
        slot_bins = lax.optimization_barrier(jnp.sum(jnp.where(slot_match, bin_block[:, :, None], 0), axis=(0, 1))).astype(jnp.int32)
        return (outgoing, slot_bins)
    sends, send_bins = jax.vmap(pack_slots)(destination, normed.reshape(device_count, TOK, D), bin_ids.reshape(device_count, TOK, TOPK))
    sends = sends.reshape(device_count, EXPERTS, CAP, D)
    send_bins = send_bins.reshape(device_count, EXPERTS, CAP)

    def run_expert(expert_index):
        row_data = sends[:, expert_index].reshape(device_count * CAP, D)
        slot_bins = send_bins[:, expert_index].reshape(device_count * CAP)
        gate_part = jnp.dot(row_data, gate_weight[expert_index], preferred_element_type=jnp.float32)
        up_part = jnp.dot(row_data, up_weight[expert_index], preferred_element_type=jnp.float32)
        activation = jax.nn.silu(gate_part) * up_part
        hidden = activation.astype(jnp.bfloat16)
        energy = lax.optimization_barrier(jnp.sum(activation * activation, axis=1)) / HID
        onehot = (slot_bins[:, None] == jnp.arange(NBINS, dtype=jnp.int32)[None, :]).astype(jnp.float32)
        bin_sums = jnp.dot(energy[None, :], onehot, precision=lax.Precision.HIGHEST)[0]
        expert_rows = jnp.dot(hidden, down_weight[expert_index], preferred_element_type=jnp.float32).astype(jnp.bfloat16)
        return (expert_rows.reshape(device_count, CAP, D), bin_sums)
    expert_out, histogram = lax.map(run_expert, jnp.arange(EXPERTS, dtype=jnp.int32))
    levels = gate_levels.astype(jnp.float32)
    route_weights = levels / lax.optimization_barrier(jnp.sum(levels, axis=1, keepdims=True))

    def combine_rows(dest_block, weight_block, returned):
        slot_match = dest_block[:, :, None] == slot_index[None, None, :]
        combiner = lax.optimization_barrier(jnp.sum(jnp.where(slot_match, weight_block[:, :, None], 0.0), axis=1))
        return jnp.dot(combiner, returned.reshape(slot_total, D).astype(jnp.float32), precision=lax.Precision.HIGHEST)
    mixture = jax.vmap(combine_rows)(destination, route_weights.reshape(device_count, TOK, TOPK), expert_out.transpose(1, 0, 2, 3))
    layer_out = (stream_state + mixture.reshape(SEQ, D)).astype(jnp.bfloat16)
    return (layer_out, histogram)
```

```python
import functools

import jax
import jax.numpy as jnp
from jax import lax
from jax.experimental import pallas as pl
from jax.experimental.pallas import tpu as pltpu
from jax.sharding import PartitionSpec as P

HID = 1024
NBINS = 2048


softmax_scale = 192.0 ** (-0.5)
norm_eps = 1e-06
masked_score = -1e30

NZ, NX, NY = 8, 4, 2
NQ = NX * NY
NR = NZ * NY
TOK = 8
CAP = 2
N_CTX = 4
N_EXPERTS = 64
MESH = pl.DeviceIdType.MESH


def remote(src, dst, send_sem, recv_sem, target):
    copy = pltpu.make_async_remote_copy(
        src_ref=src,
        dst_ref=dst,
        send_sem=send_sem,
        recv_sem=recv_sem,
        device_id=target,
        device_id_type=MESH,
    )
    copy.start()
    return copy


def greet(targets):
    barrier = pltpu.get_barrier_semaphore()
    for target in targets:
        pl.semaphore_signal(barrier, inc=1, device_id=target, device_id_type=MESH)
    pl.semaphore_wait(barrier, len(targets))


def project_sum_kernel(
    part_a,
    values_ref,
    weight_ref,
    out_ref,
    a_first,
    a_slots,
    b_first,
    b_slots,
    a_push,
    a_got,
    b_push,
    b_got,
    a_send_sem,
    a_recv_sem,
    b_send_sem,
    b_recv_sem,
    ap_send_sem,
    ap_recv_sem,
    bp_send_sem,
    bp_recv_sem,
):
    width = weight_ref.shape[1]
    half_a, half_b = part_a // 2, (width - part_a) // 2
    me = lax.axis_index("exp")
    z, x, y = me // NQ, (me // NY) % NX, me % NY
    q, r = x * NY + y, z * NY + y

    def at(z_at, x_at, y_at):
        return {"exp": (z_at * NX + x_at) * NY + y_at}

    q_peers = [(q + j) % NQ for j in range(NQ)]
    r_peers = [(r + j) % NR for j in range(NR)]
    z_next = [at((z + 1) % NZ, x, y), at((z + NZ - 1) % NZ, x, y)]
    x_next = [at(z, (x + 1) % NX, y), at(z, (x + NX - 1) % NX, y)]
    greet(
        [at(z, p // NY, p % NY) for p in q_peers[1:]]
        + [at(p // NY, x, p % NY) for p in r_peers[1:]]
    )

    def a_own(way, chunk):
        rows = values_ref[chunk].reshape(NX * NY * TOK, values_ref.shape[3])
        return jnp.dot(
            rows,
            weight_ref[:, way * half_a : (way + 1) * half_a],
            preferred_element_type=jnp.float32,
        )

    def b_own(way, chunk):
        rows = values_ref[:, chunk].reshape(NZ * NY * TOK, values_ref.shape[3])
        return jnp.dot(
            rows,
            weight_ref[:, part_a + way * half_b : part_a + (way + 1) * half_b],
            preferred_element_type=jnp.float32,
        )

    a_flight, b_flight, pushes = {}, {}, []

    def a_step(step):
        for way in range(2):
            sign = -1 if way == 0 else 1
            own = a_own(way, (z + sign * (1 + step) + 2 * NZ) % NZ)
            if step == 0:
                src = a_first.at[way]
                a_first[way] = own.astype(jnp.bfloat16)
            else:
                src = a_slots.at[way, step - 1]
                a_flight[way, step - 1].wait_recv()
                a_slots[way, step - 1] = (
                    a_slots[way, step - 1].astype(jnp.float32) + own
                ).astype(jnp.bfloat16)
            a_flight[way, step] = remote(
                src,
                a_slots.at[way, step],
                a_send_sem.at[way, step],
                a_recv_sem.at[way, step],
                z_next[way],
            )

    def b_step(step):
        for way in range(2):
            sign = -1 if way == 0 else 1
            own = b_own(way, (x + sign * (1 + step) + 2 * NX) % NX)
            if step == 0:
                src = b_first.at[way]
                b_first[way] = own.astype(jnp.bfloat16)
            else:
                src = b_slots.at[way, step - 1]
                b_flight[way, step - 1].wait_recv()
                b_slots[way, step - 1] = (
                    b_slots[way, step - 1].astype(jnp.float32) + own
                ).astype(jnp.bfloat16)
            b_flight[way, step] = remote(
                src,
                b_slots.at[way, step],
                b_send_sem.at[way, step],
                b_recv_sem.at[way, step],
                x_next[way],
            )

    def a_push_out():
        for way in range(2):
            own = a_own(way, z)
            a_flight[way, NZ - 2].wait_recv()
            own = own + a_slots[way, NZ - 2].astype(jnp.float32)
            a_push[:, :, way * half_a : (way + 1) * half_a] = own.reshape(
                NQ, TOK, half_a
            ).astype(jnp.bfloat16)
        for j in range(1, NQ):
            p = q_peers[j]
            pushes.append(
                remote(
                    a_push.at[p],
                    a_got.at[j - 1],
                    ap_send_sem.at[j - 1],
                    ap_recv_sem.at[j - 1],
                    at(z, p // NY, p % NY),
                )
            )

    def b_push_out():
        for way in range(2):
            own = b_own(way, x)
            b_flight[way, NX - 2].wait_recv()
            own = own + b_slots[way, NX - 2].astype(jnp.float32)
            b_push[:, :, way * half_b : (way + 1) * half_b] = own.reshape(
                NR, TOK, half_b
            ).astype(jnp.bfloat16)
        for j in range(1, NR):
            p = r_peers[j]
            pushes.append(
                remote(
                    b_push.at[p],
                    b_got.at[j - 1],
                    bp_send_sem.at[j - 1],
                    bp_recv_sem.at[j - 1],
                    at(p // NY, x, p % NY),
                )
            )

    a_step(0)
    b_step(0)
    a_step(1)
    a_step(2)
    b_step(1)
    a_step(3)
    b_step(2)
    a_step(4)
    b_push_out()
    a_step(5)
    a_step(6)
    a_push_out()
    for copy in pushes:
        copy.wait_recv()
    total = b_push[r].astype(jnp.float32)
    for j in range(NR - 1):
        total = total + b_got[j].astype(jnp.float32)
    out_ref[:, part_a:] = total
    total = a_push[q].astype(jnp.float32)
    for j in range(NQ - 1):
        total = total + a_got[j].astype(jnp.float32)
    out_ref[:, :part_a] = total
    for copy in [*a_flight.values(), *b_flight.values(), *pushes]:
        copy.wait_send()


def project_sum(values, weight, part_a=2048):
    rows, depth = values.shape
    width = weight.shape[1]
    part_b = width - part_a
    bf16 = jnp.bfloat16
    dma = pltpu.SemaphoreType.DMA
    return pl.pallas_call(
        functools.partial(project_sum_kernel, part_a),
        out_shape=jax.ShapeDtypeStruct((TOK, width), jnp.float32),
        in_specs=[pl.BlockSpec(memory_space=pltpu.VMEM)] * 2,
        out_specs=pl.BlockSpec(memory_space=pltpu.VMEM),
        scratch_shapes=[
            pltpu.VMEM((2, NQ * TOK, part_a // 2), bf16),
            pltpu.VMEM((2, NZ - 1, NQ * TOK, part_a // 2), bf16),
            pltpu.VMEM((2, NR * TOK, part_b // 2), bf16),
            pltpu.VMEM((2, NX - 1, NR * TOK, part_b // 2), bf16),
            pltpu.VMEM((NQ, TOK, part_a), bf16),
            pltpu.VMEM((NQ - 1, TOK, part_a), bf16),
            pltpu.VMEM((NR, TOK, part_b), bf16),
            pltpu.VMEM((NR - 1, TOK, part_b), bf16),
            dma((2, NZ - 1)),
            dma((2, NZ - 1)),
            dma((2, NX - 1)),
            dma((2, NX - 1)),
            dma((NQ - 1,)),
            dma((NQ - 1,)),
            dma((NR - 1,)),
            dma((NR - 1,)),
        ],
        compiler_params=pltpu.CompilerParams(
            collective_id=0, has_side_effects=True, vmem_limit_bytes=40 << 20
        ),
        name="project_sum",
    )(values.reshape(NZ, NX, NY * TOK, depth), weight)


def small(cond):
    return cond.astype(jnp.float32).astype(jnp.bfloat16)


def split3(v):
    first = v.astype(jnp.bfloat16)
    rest = v - first.astype(jnp.float32)
    second = rest.astype(jnp.bfloat16)
    third = (rest - second.astype(jnp.float32)).astype(jnp.bfloat16)
    return first, second, third


def mm(a, b):
    return jnp.dot(a, b, preferred_element_type=jnp.float32)


def mm_t(a, b):
    return lax.dot_general(
        a, b, (((0,), (0,)), ((), ())), preferred_element_type=jnp.float32
    )


def experts_kernel(
    rows_ref,
    state_ref,
    scale_ref,
    gate_hbm,
    up_hbm,
    down_hbm,
    out_ref,
    hist_ref,
    gate_ref,
    up_ref,
    down_ref,
    near,
    weigh,
    slots,
    inbox,
    kept,
    to_mate,
    from_mate,
    back,
    returned,
    to_y,
    from_y,
    to_z,
    from_z,
    hist_out,
    hist_in,
    load_sem,
    z_send,
    z_recv,
    y_send,
    y_recv,
    q_send,
    q_recv,
    m_send,
    m_recv,
    o_send,
    o_recv,
    b_send,
    b_recv,
    ys_send,
    ys_recv,
    zs_send,
    zs_recv,
    h_send,
    h_recv,
):
    width = state_ref.shape[1]
    sent = width + 2 * N_EXPERTS
    half_rows, half_slots = NZ * TOK, NQ * NZ * CAP
    piece = NZ * CAP
    ctx, me = lax.axis_index("ctx"), lax.axis_index("exp")
    y_lo, core = ctx // 2, ctx % 2
    z, q = me // NQ, me % NQ

    def z_peer(z_at):
        return {"ctx": ctx, "exp": z_at * NQ + q}

    def q_peer(q_at):
        return {"ctx": ctx, "exp": z * NQ + q_at}

    y_peer = {"ctx": (1 - y_lo) * 2 + core, "exp": me}
    mate = {"ctx": y_lo * 2 + 1 - core, "exp": me}

    def c_peer(j):
        return {"ctx": (ctx + j) % N_CTX, "exp": me}

    loads = [
        pltpu.make_async_copy(src, dst, load_sem.at[i])
        for i, (src, dst) in enumerate(
            ((gate_hbm, gate_ref), (up_hbm, up_ref), (down_hbm, down_ref))
        )
    ]
    for load in loads:
        load.start()
    greet(
        [z_peer((z + j) % NZ) for j in range(1, NZ)]
        + [q_peer((q + j) % NQ) for j in range(1, NQ)]
        + [c_peer(j) for j in range(1, N_CTX)]
    )
    pending = []

    order = (1, 7, 2, 6, 3, 5, 4)
    arrivals = {}
    for j in order:
        arrivals[j] = remote(
            rows_ref, near.at[y_lo, z], z_send.at[j], z_recv.at[j], z_peer((z + j) % NZ)
        )
        pending.append(arrivals[j])
    near[y_lo, z] = rows_ref[...]
    crossings = [remote(rows_ref, near.at[y_lo, z], y_send.at[0], y_recv.at[0], y_peer)]
    for j in order:
        z_from = (z + NZ - j) % NZ
        arrivals[j].wait_recv()
        crossings.append(
            remote(
                near.at[y_lo, z_from],
                near.at[y_lo, z_from],
                y_send.at[j],
                y_recv.at[j],
                y_peer,
            )
        )
    pending += crossings

    lane = lax.broadcasted_iota(jnp.int32, (2 * N_EXPERTS, half_slots), 0)
    wanted = z * NQ + (
        lax.broadcasted_iota(jnp.int32, (2 * N_EXPERTS, half_slots), 1) // piece
    )
    pick_level, pick_rank = small(lane == wanted), small(lane == wanted + N_EXPERTS)
    row = lax.broadcasted_iota(jnp.int32, (half_rows, half_slots), 0)
    col = lax.broadcasted_iota(jnp.int32, (half_rows, half_slots), 1)
    same_source = (row // TOK) == ((col // CAP) % NZ)
    slot_rank = (col % CAP).astype(jnp.float32)

    slot_flight = {}
    for half in range(2):
        if half == 1:
            for copy in crossings:
                copy.wait_recv()
        y_at = y_lo if half == 0 else 1 - y_lo
        held = (
            near[y_at]
            .astype(jnp.float32)
            .reshape(half_rows, sent + 2 * N_EXPERTS)
            .astype(jnp.bfloat16)
        )
        route = held[:, sent:]
        level, rank = mm(route, pick_level), mm(route, pick_rank)
        chosen = (level > 0.5) & (rank == slot_rank) & same_source
        weigh[half] = jnp.where(chosen, level, 0.0).astype(jnp.bfloat16)
        picked = mm_t(small(chosen), held[:, :sent])
        slots[half] = picked.astype(jnp.bfloat16).reshape(NQ, piece, sent)
        for j in order:
            p = (q + j) % NQ
            slot_flight[half, j] = remote(
                slots.at[half, p],
                inbox.at[0, half, q],
                q_send.at[half, j],
                q_recv.at[half, j],
                q_peer(p),
            )
        inbox[0, half, q] = slots[half, q]
    pending += slot_flight.values()

    mate_flight = []
    for half in range(2):
        for j in (0,) + order:
            q_from = (q + NQ - j) % NQ
            if j:
                slot_flight[half, j].wait_recv()
            mate_flight.append(
                remote(
                    inbox.at[0, half, q_from],
                    inbox.at[1, half, q_from],
                    m_send.at[half, j],
                    m_recv.at[half, j],
                    mate,
                )
            )
    pending += mate_flight

    bin_lane = lax.broadcasted_iota(jnp.int32, (2 * half_slots, 2 * N_EXPERTS), 1)
    bins_at = bin_lane.astype(jnp.float32)

    def run_block(which):
        block = inbox[which].reshape(2 * half_slots, sent)
        x = block[:, :width]
        gate_part, up_part = mm(x, gate_ref[...]), mm(x, up_ref[...])
        activation = gate_part / (1.0 + jnp.exp(-gate_part)) * up_part
        energy = jnp.sum(activation * activation, axis=1, keepdims=True) * (1.0 / HID)
        tail = block[:, width:].astype(jnp.float32)
        high = jnp.sum(jnp.where(bin_lane == me, tail, 0.0), axis=1, keepdims=True)
        low = jnp.sum(
            jnp.where(bin_lane == me + N_EXPERTS, tail, 0.0), axis=1, keepdims=True
        )
        at_high = jnp.where(high == bins_at, energy, 0.0)
        at_low = small(low == bins_at)
        first, second, third = split3(at_high)
        hist = mm_t(first, at_low) + mm_t(second, at_low) + mm_t(third, at_low)
        return activation.astype(jnp.bfloat16), hist

    for load in loads:
        load.wait()
    hidden, hist = run_block(0)
    kept[...] = mm(hidden, down_ref[...])
    for copy in mate_flight:
        copy.wait_recv()
    hidden, more = run_block(1)
    to_mate[...] = (
        mm(hidden, down_ref[...]).astype(jnp.bfloat16).reshape(to_mate.shape)
    )
    mate_out = {}
    for half in (1, 0):
        mate_out[half] = remote(
            to_mate.at[half], from_mate.at[half], o_send.at[half], o_recv.at[half], mate
        )
    pending += mate_out.values()

    hist_out[...] = (hist + more)[: N_CTX * 8].reshape(N_CTX, 8, 2 * N_EXPERTS)
    hist_flight = [
        remote(
            hist_out.at[(ctx + j) % N_CTX],
            hist_in.at[j - 1],
            h_send.at[j - 1],
            h_recv.at[j - 1],
            c_peer(j),
        )
        for j in range(1, N_CTX)
    ]
    pending += hist_flight

    back_flight = {}
    for half in (1, 0):
        mate_out[half].wait_recv()
        total = kept[half * half_slots : (half + 1) * half_slots] + from_mate[
            half
        ].reshape(half_slots, width).astype(jnp.float32)
        back[half] = total.astype(jnp.bfloat16).reshape(NQ, piece, width)
        for j in order:
            p = (q + j) % NQ
            back_flight[half, j] = remote(
                back.at[half, p],
                returned.at[half, q],
                b_send.at[half, j],
                b_recv.at[half, j],
                q_peer(p),
            )
        returned[half, q] = back[half, q]
    pending += back_flight.values()

    def mixed(half):
        for j in order:
            back_flight[half, j].wait_recv()
        return mm(weigh[half], returned[half].reshape(half_slots, width))

    to_y[...] = mixed(1).reshape(NZ, TOK, width).astype(jnp.bfloat16)
    y_flight = [
        remote(to_y.at[j], from_y.at[j], ys_send.at[j], ys_recv.at[j], y_peer)
        for j in range(NZ)
    ]
    pending += y_flight
    own = mixed(0).reshape(NZ, TOK, width)
    for copy in y_flight:
        copy.wait_recv()
    to_z[...] = (own + from_y[...].astype(jnp.float32)).astype(jnp.bfloat16)
    z_flight = []
    for j in order:
        z_to = (z + j) % NZ
        z_flight.append(
            remote(
                to_z.at[z_to],
                from_z.at[j - 1],
                zs_send.at[j - 1],
                zs_recv.at[j - 1],
                z_peer(z_to),
            )
        )
    pending += z_flight
    for copy in hist_flight:
        copy.wait_recv()
    hist = hist_out[ctx]
    for j in range(N_CTX - 1):
        hist = hist + hist_in[j]
    hist_ref[...] = hist
    for copy in z_flight:
        copy.wait_recv()
    total = to_z[z].astype(jnp.float32)
    for j in range(NZ - 1):
        total = total + from_z[j].astype(jnp.float32)
    out_ref[...] = (state_ref[...] + total * scale_ref[:, :1]).astype(jnp.bfloat16)
    for copy in pending:
        copy.wait_send()


def run_experts(rows, state, scale, gate, up, down):
    width = state.shape[1]
    sent = width + 2 * N_EXPERTS
    half_slots, piece = NQ * NZ * CAP, NZ * CAP
    bf16, f32 = jnp.bfloat16, jnp.float32
    dma = pltpu.SemaphoreType.DMA
    vmem = pl.BlockSpec(memory_space=pltpu.VMEM)
    hbm = pl.BlockSpec(memory_space=pl.ANY)
    return pl.pallas_call(
        experts_kernel,
        out_shape=(
            jax.ShapeDtypeStruct((TOK, width), bf16),
            jax.ShapeDtypeStruct((8, 2 * N_EXPERTS), f32),
        ),
        in_specs=[vmem, vmem, vmem, hbm, hbm, hbm],
        out_specs=(vmem, vmem),
        scratch_shapes=[
            pltpu.VMEM(gate.shape, bf16),
            pltpu.VMEM(up.shape, bf16),
            pltpu.VMEM(down.shape, bf16),
            pltpu.VMEM((2, NZ, TOK, rows.shape[1]), bf16),
            pltpu.VMEM((2, NZ * TOK, half_slots), bf16),
            pltpu.VMEM((2, NQ, piece, sent), bf16),
            pltpu.VMEM((2, 2, NQ, piece, sent), bf16),
            pltpu.VMEM((2 * half_slots, width), f32),
            pltpu.VMEM((2, NQ, piece, width), bf16),
            pltpu.VMEM((2, NQ, piece, width), bf16),
            pltpu.VMEM((2, NQ, piece, width), bf16),
            pltpu.VMEM((2, NQ, piece, width), bf16),
            pltpu.VMEM((NZ, TOK, width), bf16),
            pltpu.VMEM((NZ, TOK, width), bf16),
            pltpu.VMEM((NZ, TOK, width), bf16),
            pltpu.VMEM((NZ - 1, TOK, width), bf16),
            pltpu.VMEM((N_CTX, 8, 2 * N_EXPERTS), f32),
            pltpu.VMEM((N_CTX - 1, 8, 2 * N_EXPERTS), f32),
            dma((3,)),
            dma((NZ,)),
            dma((NZ,)),
            dma((NZ,)),
            dma((NZ,)),
            dma((2, NQ)),
            dma((2, NQ)),
            dma((2, NQ)),
            dma((2, NQ)),
            dma((2,)),
            dma((2,)),
            dma((2, NQ)),
            dma((2, NQ)),
            dma((NZ,)),
            dma((NZ,)),
            dma((NZ - 1,)),
            dma((NZ - 1,)),
            dma((N_CTX - 1,)),
            dma((N_CTX - 1,)),
        ],
        compiler_params=pltpu.CompilerParams(
            collective_id=1, has_side_effects=True, vmem_limit_bytes=50 << 20
        ),
        name="experts",
    )(rows, state, scale, gate, up, down)


def route_lanes(expert_ids, gate_levels, bin_ids):
    onehot = expert_ids[:, :, None] == jnp.arange(N_EXPERTS, dtype=jnp.int32)

    def spread(v):
        return jnp.sum(jnp.where(onehot, v[:, :, None], 0), axis=1)

    named = jnp.sum(onehot.astype(jnp.int32), axis=1)
    earlier = jnp.arange(TOK)[:, None] > jnp.arange(TOK)[None, :]
    rank = jnp.sum(jnp.where(earlier[:, :, None], named[None, :, :], 0), axis=1)
    lanes = (spread(bin_ids // 64), spread(bin_ids % 64), spread(gate_levels), rank)
    return jnp.concatenate(lanes, axis=1).astype(jnp.bfloat16)


def key_scores(query_nope, query_rope, lat_rows, rope_rows):
    scores = jnp.einsum("qhl,kl->hqk", query_nope, lat_rows, preferred_element_type=jnp.float32)
    scores = scores + jnp.einsum(
        "qhr,kr->hqk", query_rope, rope_rows, preferred_element_type=jnp.float32
    )
    return scores * softmax_scale


def attend_piece(running, key_piece, query_nope, query_rope, query_pos, query_docs):
    lat_rows, rope_rows, doc_rows = key_piece
    key_pos = jnp.arange(lat_rows.shape[0], dtype=jnp.int32)
    allowed = (key_pos[None, :] <= query_pos[:, None]) & (doc_rows[None, :] == query_docs[:, None])
    scores = jnp.where(
        allowed[None], key_scores(query_nope, query_rope, lat_rows, rope_rows), masked_score
    )
    run_max, run_sum, accum = running
    new_max = jnp.maximum(run_max, jnp.max(scores, axis=2))
    probs = jnp.where(allowed[None], jnp.exp(scores - new_max[:, :, None]), 0.0)
    run_sum = jnp.sum(probs, axis=2)
    accum = jnp.einsum(
        "hqk,kl->hql", probs.astype(jnp.bfloat16), lat_rows, preferred_element_type=jnp.float32
    )
    return (new_max, run_sum, accum)


def project_values(context, uv_weight):
    values = jnp.einsum(
        "hql,hlv->qhv", context, uv_weight, preferred_element_type=jnp.float32
    ).astype(jnp.bfloat16)
    return values.reshape(values.shape[0], values.shape[1] * values.shape[2])


def head_values(running, uv_weight):
    context = (running[2] / running[1][:, :, None]).astype(jnp.bfloat16)
    return project_values(context, uv_weight)


def on_device(
    residual_in,
    norm_gain,
    q_nope,
    q_rope,
    latent,
    k_rope,
    doc_ids,
    uv_weight,
    out_weight,
    expert_ids,
    gate_levels,
    bin_ids,
    gate_weight,
    up_weight,
    down_weight,
):
    block_len, head_count, lat_width = q_nope.shape
    rope_width = k_rope.shape[1]
    query_first = lax.axis_index("ctx") * block_len
    query_pos = query_first + jnp.arange(block_len, dtype=jnp.int32)
    query_rope = q_rope.reshape(block_len, head_count, rope_width)
    keys_local = (latent, k_rope, doc_ids)
    initial = (
        jnp.full((head_count, block_len), masked_score, jnp.float32),
        jnp.zeros((head_count, block_len), jnp.float32),
        jnp.zeros((head_count, block_len, lat_width), jnp.float32),
    )
    running = attend_piece(
        initial,
        (
            lax.all_gather(keys_local[0], "ctx", axis=0, tiled=True),
            lax.all_gather(keys_local[1], "ctx", axis=0, tiled=True),
            lax.all_gather(keys_local[2], "ctx", axis=0, tiled=True),
        ),
        q_nope,
        query_rope,
        query_pos,
        doc_ids,
    )
    attended = project_sum(head_values(running, uv_weight), out_weight)
    stream_state = residual_in.astype(jnp.float32) + attended
    normed = (
        stream_state
        * lax.rsqrt(jnp.mean(stream_state * stream_state, axis=1, keepdims=True) + norm_eps)
        * norm_gain
    ).astype(jnp.bfloat16)
    rows = jnp.concatenate(
        (normed, route_lanes(expert_ids, gate_levels, bin_ids)), axis=1
    )
    scale = 1.0 / jnp.sum(gate_levels.astype(jnp.float32), axis=1, keepdims=True)
    layer_out, hist = run_experts(
        rows,
        stream_state,
        jnp.broadcast_to(scale, (TOK, 128)),
        gate_weight[0],
        up_weight[0],
        down_weight[0],
    )
    histogram = hist[:, : NBINS // 32].reshape(1, NBINS // N_CTX)
    return (layer_out, histogram)


def solution(mesh):
    return jax.shard_map(
        on_device,
        mesh=mesh,
        in_specs=(
            P(("ctx", "exp"), None),
            P(),
            P("ctx", "exp", None),
            P("ctx", "exp"),
            P("ctx", None),
            P("ctx", None),
            P("ctx"),
            P("exp", None, None),
            P("exp", None),
            P(("ctx", "exp"), None),
            P(("ctx", "exp"), None),
            P(("ctx", "exp"), None),
            P("exp", None, "ctx"),
            P("exp", None, "ctx"),
            P("exp", "ctx", None),
        ),
        out_specs=(P(("ctx", "exp"), None), P("exp", "ctx")),
        check_vma=False,
    )
```

```python
import functools
import math

import jax
import jax.numpy as jnp
from jax import lax
from jax.experimental import pallas as pl
from jax.experimental.pallas import tpu as pltpu
from jax.sharding import PartitionSpec as P

HID = 1024
NBINS = 2048


exponent_scale = 192.0 ** (-0.5) * math.log2(math.e)
norm_eps = 1e-06
masked_score = -1e30

NZ, NX, NY = 8, 4, 2
NQ = NX * NY
NR = NZ * NY
TOK = 8
CAP = 2
N_CTX = 4
N_EXPERTS = 64
ROPE = 64
VDIM = 128
KEY_TAIL = 128
KEY_PIECES = 2
MESH = pl.DeviceIdType.MESH


def remote(src, dst, send_sem, recv_sem, target):
    copy = pltpu.make_async_remote_copy(
        src_ref=src,
        dst_ref=dst,
        send_sem=send_sem,
        recv_sem=recv_sem,
        device_id=target,
        device_id_type=MESH,
    )
    copy.start()
    return copy


def greet(targets):
    barrier = pltpu.get_barrier_semaphore()
    for target in targets:
        pl.semaphore_signal(barrier, inc=1, device_id=target, device_id_type=MESH)
    pl.semaphore_wait(barrier, len(targets))


def small(cond):
    return cond.astype(jnp.float32).astype(jnp.bfloat16)


def split3(v):
    first = v.astype(jnp.bfloat16)
    rest = v - first.astype(jnp.float32)
    second = rest.astype(jnp.bfloat16)
    third = (rest - second.astype(jnp.float32)).astype(jnp.bfloat16)
    return first, second, third


def mm(a, b):
    return jnp.dot(a, b, preferred_element_type=jnp.float32)


def mm_t(a, b):
    return lax.dot_general(
        a, b, (((0,), (0,)), ((), ())), preferred_element_type=jnp.float32
    )


def attend_sum_kernel(
    part_a,
    query_ref,
    key_ref,
    uv_hbm,
    weight_hbm,
    out_ref,
    uv_ref,
    weight_ref,
    keys,
    top,
    denominator,
    accum,
    values_ref,
    a_first,
    a_slots,
    b_first,
    b_slots,
    a_push,
    a_got,
    b_push,
    b_got,
    k_send_sem,
    k_recv_sem,
    a_send_sem,
    a_recv_sem,
    b_send_sem,
    b_recv_sem,
    ap_send_sem,
    ap_recv_sem,
    bp_send_sem,
    bp_recv_sem,
    load_sem,
):
    loads = [
        pltpu.make_async_copy(uv_hbm, uv_ref, load_sem.at[0]),
        pltpu.make_async_copy(weight_hbm, weight_ref, load_sem.at[1]),
    ]
    for load in loads:
        load.start()
    width = weight_ref.shape[1]
    half_a, half_b = part_a // 2, (width - part_a) // 2
    me = lax.axis_index("exp")
    z, x, y = me // NQ, (me // NY) % NX, me % NY
    q, r = x * NY + y, z * NY + y

    def at(z_at, x_at, y_at):
        return {"exp": (z_at * NX + x_at) * NY + y_at}

    q_peers = [(q + j) % NQ for j in range(NQ)]
    r_peers = [(r + j) % NR for j in range(NR)]
    z_next = [at((z + 1) % NZ, x, y), at((z + NZ - 1) % NZ, x, y)]
    x_next = [at(z, (x + 1) % NX, y), at(z, (x + NX - 1) % NX, y)]
    ctx = lax.axis_index("ctx")
    y_lo, core = ctx // 2, ctx % 2
    mate = {"ctx": y_lo * 2 + 1 - core, "exp": me}
    across = {"ctx": (1 - y_lo) * 2 + core, "exp": me}
    greet(
        [at(z, p // NY, p % NY) for p in q_peers[1:]]
        + [at(p // NY, x, p % NY) for p in r_peers[1:]]
        + [mate, across]
    )

    piece = key_ref.shape[0] // KEY_PIECES

    def key_copy(back, i, src, target):
        return pltpu.make_async_remote_copy(
            src_ref=src,
            dst_ref=keys.at[back, i],
            send_sem=k_send_sem.at[back, i],
            recv_sem=k_recv_sem.at[back, i],
            device_id=target,
            device_id_type=MESH,
        )

    def own_piece(i):
        return key_ref.at[i * piece : (i + 1) * piece]

    for i in range(KEY_PIECES):

        @pl.when(y_lo == 0)
        def _():
            key_copy(1, i, own_piece(i), across).start()

    for i in range(KEY_PIECES):

        @pl.when(core == 0)
        def _():
            key_copy(0, i, own_piece(i), mate).start()

    lat = uv_ref.shape[1]
    doc_lane = key_ref.shape[1] - KEY_TAIL + ROPE
    query_docs = key_ref[:, doc_lane : doc_lane + 1].astype(jnp.float32)
    doc_pick = small(lax.broadcasted_iota(jnp.int32, (8, KEY_TAIL), 1) == ROPE)

    def nt(a, b):
        return lax.dot_general(
            a, b, (((1,), (1,)), ((), ())), preferred_element_type=jnp.float32
        )

    def fold(block, first):
        docs = nt(doc_pick, block[:, lat:])[:1]
        allowed = query_docs == docs
        if first:
            shape = (query_ref.shape[1], block.shape[0])
            query_at = lax.broadcasted_iota(jnp.int32, shape, 0)
            key_at = lax.broadcasted_iota(jnp.int32, shape, 1)
            allowed = allowed & (key_at <= query_at)
        for head in range(query_ref.shape[0]):
            scores = jnp.where(allowed, nt(query_ref[head], block), masked_score)
            peak = jnp.max(scores, axis=1, keepdims=True)
            if not first:
                old = top[head][:, :1]
                peak = jnp.maximum(old, peak)
                fade = jnp.exp2((old - peak) * exponent_scale)
            probs = jnp.exp2((scores - peak) * exponent_scale)
            mass = jnp.sum(probs, axis=1, keepdims=True)
            mixed = mm(probs.astype(jnp.bfloat16), block[:, :lat])
            if not first:
                mass = mass + denominator[head][:, :1] * fade
                mixed = mixed + accum[head] * fade
            top[head] = jnp.broadcast_to(peak, top.shape[1:])
            denominator[head] = jnp.broadcast_to(mass, denominator.shape[1:])
            accum[head] = mixed

    fold(key_ref[...], True)

    @pl.when(core == 1)
    def _():
        for i in range(KEY_PIECES):
            key_copy(0, i, own_piece(i), mate).wait_recv()
            fold(keys[0, i], False)

    @pl.when(y_lo == 1)
    def _():
        for i in range(KEY_PIECES):
            key_copy(1, i, own_piece(i), across).wait_recv()

            @pl.when(core == 1)
            def _():
                key_copy(0, i, keys.at[1, i], mate).start()

            fold(keys[1, i], False)

    @pl.when(ctx == 2)
    def _():
        for i in range(KEY_PIECES):
            key_copy(0, i, own_piece(i), mate).wait_recv()
            fold(keys[0, i], False)

    for load in loads:
        load.wait()
    for head in range(query_ref.shape[0]):
        context = (accum[head] / denominator[head][:, :1]).astype(jnp.bfloat16)
        values_ref[:, :, :, head * VDIM : (head + 1) * VDIM] = (
            mm(context, uv_ref[head])
            .astype(jnp.bfloat16)
            .reshape(NZ, NX, NY * TOK, VDIM)
        )

    def a_own(way, chunk):
        rows = values_ref[chunk].reshape(NX * NY * TOK, values_ref.shape[3])
        return jnp.dot(
            rows,
            weight_ref[:, way * half_a : (way + 1) * half_a],
            preferred_element_type=jnp.float32,
        )

    def b_own(way, chunk):
        rows = values_ref[:, chunk].reshape(NZ * NY * TOK, values_ref.shape[3])
        return jnp.dot(
            rows,
            weight_ref[:, part_a + way * half_b : part_a + (way + 1) * half_b],
            preferred_element_type=jnp.float32,
        )

    a_flight, b_flight, pushes = {}, {}, []

    def a_step(step):
        for way in range(2):
            sign = -1 if way == 0 else 1
            own = a_own(way, (z + sign * (1 + step) + 2 * NZ) % NZ)
            if step == 0:
                src = a_first.at[way]
                a_first[way] = own.astype(jnp.bfloat16)
            else:
                src = a_slots.at[way, step - 1]
                a_flight[way, step - 1].wait_recv()
                a_slots[way, step - 1] = (
                    a_slots[way, step - 1].astype(jnp.float32) + own
                ).astype(jnp.bfloat16)
            a_flight[way, step] = remote(
                src,
                a_slots.at[way, step],
                a_send_sem.at[way, step],
                a_recv_sem.at[way, step],
                z_next[way],
            )

    def b_step(step):
        for way in range(2):
            sign = -1 if way == 0 else 1
            own = b_own(way, (x + sign * (1 + step) + 2 * NX) % NX)
            if step == 0:
                src = b_first.at[way]
                b_first[way] = own.astype(jnp.bfloat16)
            else:
                src = b_slots.at[way, step - 1]
                b_flight[way, step - 1].wait_recv()
                b_slots[way, step - 1] = (
                    b_slots[way, step - 1].astype(jnp.float32) + own
                ).astype(jnp.bfloat16)
            b_flight[way, step] = remote(
                src,
                b_slots.at[way, step],
                b_send_sem.at[way, step],
                b_recv_sem.at[way, step],
                x_next[way],
            )

    def a_push_out():
        for way in range(2):
            own = a_own(way, z)
            a_flight[way, NZ - 2].wait_recv()
            own = own + a_slots[way, NZ - 2].astype(jnp.float32)
            a_push[:, :, way * half_a : (way + 1) * half_a] = own.reshape(
                NQ, TOK, half_a
            ).astype(jnp.bfloat16)
        for j in range(1, NQ):
            p = q_peers[j]
            pushes.append(
                remote(
                    a_push.at[p],
                    a_got.at[j - 1],
                    ap_send_sem.at[j - 1],
                    ap_recv_sem.at[j - 1],
                    at(z, p // NY, p % NY),
                )
            )

    def b_push_out():
        for way in range(2):
            own = b_own(way, x)
            b_flight[way, NX - 2].wait_recv()
            own = own + b_slots[way, NX - 2].astype(jnp.float32)
            b_push[:, :, way * half_b : (way + 1) * half_b] = own.reshape(
                NR, TOK, half_b
            ).astype(jnp.bfloat16)
        for j in range(1, NR):
            p = r_peers[j]
            pushes.append(
                remote(
                    b_push.at[p],
                    b_got.at[j - 1],
                    bp_send_sem.at[j - 1],
                    bp_recv_sem.at[j - 1],
                    at(p // NY, x, p % NY),
                )
            )

    a_step(0)
    b_step(0)
    a_step(1)
    a_step(2)
    b_step(1)
    a_step(3)
    b_step(2)
    a_step(4)
    b_push_out()
    a_step(5)
    a_step(6)
    a_push_out()
    for copy in pushes:
        copy.wait_recv()
    total = b_push[r].astype(jnp.float32)
    for j in range(NR - 1):
        total = total + b_got[j].astype(jnp.float32)
    out_ref[:, part_a:] = total
    total = a_push[q].astype(jnp.float32)
    for j in range(NQ - 1):
        total = total + a_got[j].astype(jnp.float32)
    out_ref[:, :part_a] = total
    for copy in [*a_flight.values(), *b_flight.values(), *pushes]:
        copy.wait_send()
    for i in range(KEY_PIECES):

        @pl.when(y_lo == 0)
        def _():
            key_copy(1, i, own_piece(i), across).wait_send()

        @pl.when((core == 0) | (y_lo == 1))
        def _():
            key_copy(0, i, own_piece(i), mate).wait_send()


def attend_sum(queries, keys, uv_weight, weight, part_a=2048):
    heads, rows, depth = queries.shape
    width = weight.shape[1]
    part_b = width - part_a
    bf16 = jnp.bfloat16
    dma = pltpu.SemaphoreType.DMA
    return pl.pallas_call(
        functools.partial(attend_sum_kernel, part_a),
        out_shape=jax.ShapeDtypeStruct((TOK, width), jnp.float32),
        in_specs=[pl.BlockSpec(memory_space=pltpu.VMEM)] * 2
        + [pl.BlockSpec(memory_space=pltpu.HBM)] * 2,
        out_specs=pl.BlockSpec(memory_space=pltpu.VMEM),
        scratch_shapes=[
            pltpu.VMEM(uv_weight.shape, bf16),
            pltpu.VMEM(weight.shape, bf16),
            pltpu.VMEM((2, KEY_PIECES, rows // KEY_PIECES, depth), bf16),
            pltpu.VMEM((heads, rows, 128), jnp.float32),
            pltpu.VMEM((heads, rows, 128), jnp.float32),
            pltpu.VMEM((heads, rows, uv_weight.shape[1]), jnp.float32),
            pltpu.VMEM((NZ, NX, NY * TOK, heads * VDIM), bf16),
            pltpu.VMEM((2, NQ * TOK, part_a // 2), bf16),
            pltpu.VMEM((2, NZ - 1, NQ * TOK, part_a // 2), bf16),
            pltpu.VMEM((2, NR * TOK, part_b // 2), bf16),
            pltpu.VMEM((2, NX - 1, NR * TOK, part_b // 2), bf16),
            pltpu.VMEM((NQ, TOK, part_a), bf16),
            pltpu.VMEM((NQ - 1, TOK, part_a), bf16),
            pltpu.VMEM((NR, TOK, part_b), bf16),
            pltpu.VMEM((NR - 1, TOK, part_b), bf16),
            dma((2, KEY_PIECES)),
            dma((2, KEY_PIECES)),
            dma((2, NZ - 1)),
            dma((2, NZ - 1)),
            dma((2, NX - 1)),
            dma((2, NX - 1)),
            dma((NQ - 1,)),
            dma((NQ - 1,)),
            dma((NR - 1,)),
            dma((NR - 1,)),
            dma((2,)),
        ],
        compiler_params=pltpu.CompilerParams(
            collective_id=0, has_side_effects=True, vmem_limit_bytes=50 << 20
        ),
        name="attend_sum",
    )(queries, keys, uv_weight, weight)


def experts_kernel(
    rows_ref,
    state_ref,
    scale_ref,
    gate_hbm,
    up_hbm,
    down_hbm,
    out_ref,
    hist_ref,
    gate_ref,
    up_ref,
    down_ref,
    near,
    weigh,
    slots,
    inbox,
    kept,
    to_mate,
    from_mate,
    back,
    returned,
    to_y,
    from_y,
    to_z,
    from_z,
    hist_out,
    hist_in,
    load_sem,
    z_send,
    z_recv,
    y_send,
    y_recv,
    q_send,
    q_recv,
    m_send,
    m_recv,
    o_send,
    o_recv,
    b_send,
    b_recv,
    ys_send,
    ys_recv,
    zs_send,
    zs_recv,
    h_send,
    h_recv,
):
    width = state_ref.shape[1]
    sent = width + 2 * N_EXPERTS
    half_rows, half_slots = NZ * TOK, NQ * NZ * CAP
    piece = NZ * CAP
    ctx, me = lax.axis_index("ctx"), lax.axis_index("exp")
    y_lo, core = ctx // 2, ctx % 2
    z, q = me // NQ, me % NQ

    def z_peer(z_at):
        return {"ctx": ctx, "exp": z_at * NQ + q}

    def q_peer(q_at):
        return {"ctx": ctx, "exp": z * NQ + q_at}

    y_peer = {"ctx": (1 - y_lo) * 2 + core, "exp": me}
    mate = {"ctx": y_lo * 2 + 1 - core, "exp": me}

    def c_peer(j):
        return {"ctx": (ctx + j) % N_CTX, "exp": me}

    loads = [
        pltpu.make_async_copy(src, dst, load_sem.at[i])
        for i, (src, dst) in enumerate(
            ((gate_hbm, gate_ref), (up_hbm, up_ref), (down_hbm, down_ref))
        )
    ]
    for load in loads:
        load.start()
    greet(
        [z_peer((z + j) % NZ) for j in range(1, NZ)]
        + [q_peer((q + j) % NQ) for j in range(1, NQ)]
        + [c_peer(j) for j in range(1, N_CTX)]
    )
    pending = []

    order = (1, 7, 2, 6, 3, 5, 4)
    arrivals = {}
    for j in order:
        arrivals[j] = remote(
            rows_ref, near.at[y_lo, z], z_send.at[j], z_recv.at[j], z_peer((z + j) % NZ)
        )
        pending.append(arrivals[j])
    near[y_lo, z] = rows_ref[...]
    crossings = [remote(rows_ref, near.at[y_lo, z], y_send.at[0], y_recv.at[0], y_peer)]
    for j in order:
        z_from = (z + NZ - j) % NZ
        arrivals[j].wait_recv()
        crossings.append(
            remote(
                near.at[y_lo, z_from],
                near.at[y_lo, z_from],
                y_send.at[j],
                y_recv.at[j],
                y_peer,
            )
        )
    pending += crossings

    lane = lax.broadcasted_iota(jnp.int32, (2 * N_EXPERTS, half_slots), 0)
    wanted = z * NQ + (
        lax.broadcasted_iota(jnp.int32, (2 * N_EXPERTS, half_slots), 1) // piece
    )
    pick_level, pick_rank = small(lane == wanted), small(lane == wanted + N_EXPERTS)
    row = lax.broadcasted_iota(jnp.int32, (half_rows, half_slots), 0)
    col = lax.broadcasted_iota(jnp.int32, (half_rows, half_slots), 1)
    same_source = (row // TOK) == ((col // CAP) % NZ)
    slot_rank = (col % CAP).astype(jnp.float32)

    slot_flight = {}
    for half in range(2):
        if half == 1:
            for copy in crossings:
                copy.wait_recv()
        y_at = y_lo if half == 0 else 1 - y_lo
        held = (
            near[y_at]
            .astype(jnp.float32)
            .reshape(half_rows, sent + 2 * N_EXPERTS)
            .astype(jnp.bfloat16)
        )
        route = held[:, sent:]
        level, rank = mm(route, pick_level), mm(route, pick_rank)
        chosen = (level > 0.5) & (rank == slot_rank) & same_source
        weigh[half] = jnp.where(chosen, level, 0.0).astype(jnp.bfloat16)
        picked = mm_t(small(chosen), held[:, :sent])
        slots[half] = picked.astype(jnp.bfloat16).reshape(NQ, piece, sent)
        for j in order:
            p = (q + j) % NQ
            slot_flight[half, j] = remote(
                slots.at[half, p],
                inbox.at[0, half, q],
                q_send.at[half, j],
                q_recv.at[half, j],
                q_peer(p),
            )
        inbox[0, half, q] = slots[half, q]
    pending += slot_flight.values()

    mate_flight = []
    for half in range(2):
        for j in (0,) + order:
            q_from = (q + NQ - j) % NQ
            if j:
                slot_flight[half, j].wait_recv()
            mate_flight.append(
                remote(
                    inbox.at[0, half, q_from],
                    inbox.at[1, half, q_from],
                    m_send.at[half, j],
                    m_recv.at[half, j],
                    mate,
                )
            )
    pending += mate_flight

    bin_lane = lax.broadcasted_iota(jnp.int32, (2 * half_slots, 2 * N_EXPERTS), 1)
    bins_at = bin_lane.astype(jnp.float32)

    def run_block(which):
        block = inbox[which].reshape(2 * half_slots, sent)
        x = block[:, :width]
        gate_part, up_part = mm(x, gate_ref[...]), mm(x, up_ref[...])
        activation = gate_part / (1.0 + jnp.exp(-gate_part)) * up_part
        energy = jnp.sum(activation * activation, axis=1, keepdims=True) * (1.0 / HID)
        tail = block[:, width:].astype(jnp.float32)
        high = jnp.sum(jnp.where(bin_lane == me, tail, 0.0), axis=1, keepdims=True)
        low = jnp.sum(
            jnp.where(bin_lane == me + N_EXPERTS, tail, 0.0), axis=1, keepdims=True
        )
        at_high = jnp.where(high == bins_at, energy, 0.0)
        at_low = small(low == bins_at)
        first, second, third = split3(at_high)
        hist = mm_t(first, at_low) + mm_t(second, at_low) + mm_t(third, at_low)
        return activation.astype(jnp.bfloat16), hist

    for load in loads:
        load.wait()
    hidden, hist = run_block(0)
    kept[...] = mm(hidden, down_ref[...])
    for copy in mate_flight:
        copy.wait_recv()
    hidden, more = run_block(1)
    to_mate[...] = (
        mm(hidden, down_ref[...]).astype(jnp.bfloat16).reshape(to_mate.shape)
    )
    mate_out = {}
    for half in (1, 0):
        mate_out[half] = remote(
            to_mate.at[half], from_mate.at[half], o_send.at[half], o_recv.at[half], mate
        )
    pending += mate_out.values()

    hist_out[...] = (hist + more)[: N_CTX * 8].reshape(N_CTX, 8, 2 * N_EXPERTS)
    hist_flight = [
        remote(
            hist_out.at[(ctx + j) % N_CTX],
            hist_in.at[j - 1],
            h_send.at[j - 1],
            h_recv.at[j - 1],
            c_peer(j),
        )
        for j in range(1, N_CTX)
    ]
    pending += hist_flight

    back_flight = {}
    for half in (1, 0):
        mate_out[half].wait_recv()
        total = kept[half * half_slots : (half + 1) * half_slots] + from_mate[
            half
        ].reshape(half_slots, width).astype(jnp.float32)
        back[half] = total.astype(jnp.bfloat16).reshape(NQ, piece, width)
        for j in order:
            p = (q + j) % NQ
            back_flight[half, j] = remote(
                back.at[half, p],
                returned.at[half, q],
                b_send.at[half, j],
                b_recv.at[half, j],
                q_peer(p),
            )
        returned[half, q] = back[half, q]
    pending += back_flight.values()

    def mixed(half):
        for j in order:
            back_flight[half, j].wait_recv()
        return mm(weigh[half], returned[half].reshape(half_slots, width))

    to_y[...] = mixed(1).reshape(NZ, TOK, width).astype(jnp.bfloat16)
    y_flight = [
        remote(to_y.at[j], from_y.at[j], ys_send.at[j], ys_recv.at[j], y_peer)
        for j in range(NZ)
    ]
    pending += y_flight
    own = mixed(0).reshape(NZ, TOK, width)
    for copy in y_flight:
        copy.wait_recv()
    to_z[...] = (own + from_y[...].astype(jnp.float32)).astype(jnp.bfloat16)
    z_flight = []
    for j in order:
        z_to = (z + j) % NZ
        z_flight.append(
            remote(
                to_z.at[z_to],
                from_z.at[j - 1],
                zs_send.at[j - 1],
                zs_recv.at[j - 1],
                z_peer(z_to),
            )
        )
    pending += z_flight
    for copy in hist_flight:
        copy.wait_recv()
    hist = hist_out[ctx]
    for j in range(N_CTX - 1):
        hist = hist + hist_in[j]
    hist_ref[...] = hist
    for copy in z_flight:
        copy.wait_recv()
    total = to_z[z].astype(jnp.float32)
    for j in range(NZ - 1):
        total = total + from_z[j].astype(jnp.float32)
    out_ref[...] = (state_ref[...] + total * scale_ref[:, :1]).astype(jnp.bfloat16)
    for copy in pending:
        copy.wait_send()


def run_experts(rows, state, scale, gate, up, down):
    width = state.shape[1]
    sent = width + 2 * N_EXPERTS
    half_slots, piece = NQ * NZ * CAP, NZ * CAP
    bf16, f32 = jnp.bfloat16, jnp.float32
    dma = pltpu.SemaphoreType.DMA
    vmem = pl.BlockSpec(memory_space=pltpu.VMEM)
    hbm = pl.BlockSpec(memory_space=pltpu.HBM)
    return pl.pallas_call(
        experts_kernel,
        out_shape=(
            jax.ShapeDtypeStruct((TOK, width), bf16),
            jax.ShapeDtypeStruct((8, 2 * N_EXPERTS), f32),
        ),
        in_specs=[vmem, vmem, vmem, hbm, hbm, hbm],
        out_specs=(vmem, vmem),
        scratch_shapes=[
            pltpu.VMEM(gate.shape, bf16),
            pltpu.VMEM(up.shape, bf16),
            pltpu.VMEM(down.shape, bf16),
            pltpu.VMEM((2, NZ, TOK, rows.shape[1]), bf16),
            pltpu.VMEM((2, NZ * TOK, half_slots), bf16),
            pltpu.VMEM((2, NQ, piece, sent), bf16),
            pltpu.VMEM((2, 2, NQ, piece, sent), bf16),
            pltpu.VMEM((2 * half_slots, width), f32),
            pltpu.VMEM((2, NQ, piece, width), bf16),
            pltpu.VMEM((2, NQ, piece, width), bf16),
            pltpu.VMEM((2, NQ, piece, width), bf16),
            pltpu.VMEM((2, NQ, piece, width), bf16),
            pltpu.VMEM((NZ, TOK, width), bf16),
            pltpu.VMEM((NZ, TOK, width), bf16),
            pltpu.VMEM((NZ, TOK, width), bf16),
            pltpu.VMEM((NZ - 1, TOK, width), bf16),
            pltpu.VMEM((N_CTX, 8, 2 * N_EXPERTS), f32),
            pltpu.VMEM((N_CTX - 1, 8, 2 * N_EXPERTS), f32),
            dma((3,)),
            dma((NZ,)),
            dma((NZ,)),
            dma((NZ,)),
            dma((NZ,)),
            dma((2, NQ)),
            dma((2, NQ)),
            dma((2, NQ)),
            dma((2, NQ)),
            dma((2,)),
            dma((2,)),
            dma((2, NQ)),
            dma((2, NQ)),
            dma((NZ,)),
            dma((NZ,)),
            dma((NZ - 1,)),
            dma((NZ - 1,)),
            dma((N_CTX - 1,)),
            dma((N_CTX - 1,)),
        ],
        compiler_params=pltpu.CompilerParams(
            collective_id=1, has_side_effects=True, vmem_limit_bytes=60 << 20
        ),
        name="experts",
    )(rows, state, scale, gate, up, down)


def route_lanes(expert_ids, gate_levels, bin_ids):
    onehot = expert_ids[:, :, None] == jnp.arange(N_EXPERTS, dtype=jnp.int32)

    def spread(v):
        return jnp.sum(jnp.where(onehot, v[:, :, None], 0), axis=1)

    named = jnp.sum(onehot.astype(jnp.int32), axis=1)
    earlier = jnp.arange(TOK)[:, None] > jnp.arange(TOK)[None, :]
    rank = jnp.sum(jnp.where(earlier[:, :, None], named[None, :, :], 0), axis=1)
    lanes = (spread(bin_ids // 64), spread(bin_ids % 64), spread(gate_levels), rank)
    return jnp.concatenate(lanes, axis=1).astype(jnp.bfloat16)


def on_device(
    residual_in,
    norm_gain,
    q_nope,
    q_rope,
    latent,
    k_rope,
    doc_ids,
    uv_weight,
    out_weight,
    expert_ids,
    gate_levels,
    bin_ids,
    gate_weight,
    up_weight,
    down_weight,
):
    block_len, head_count, _ = q_nope.shape
    spare = jnp.zeros((block_len, KEY_TAIL - ROPE), jnp.bfloat16)
    queries = jnp.stack(
        [
            jnp.concatenate(
                (q_nope[:, head], q_rope[:, head * ROPE : (head + 1) * ROPE], spare),
                axis=1,
            )
            for head in range(head_count)
        ]
    )
    doc_column = doc_ids[:, None].astype(jnp.bfloat16)
    keys = jnp.concatenate((latent, k_rope, doc_column, spare[:, 1:]), axis=1)
    attended = attend_sum(queries, keys, uv_weight, out_weight)
    stream_state = residual_in.astype(jnp.float32) + attended
    normed = (
        stream_state
        * lax.rsqrt(jnp.mean(stream_state * stream_state, axis=1, keepdims=True) + norm_eps)
        * norm_gain
    ).astype(jnp.bfloat16)
    rows = jnp.concatenate(
        (normed, route_lanes(expert_ids, gate_levels, bin_ids)), axis=1
    )
    scale = 1.0 / jnp.sum(gate_levels.astype(jnp.float32), axis=1, keepdims=True)
    layer_out, hist = run_experts(
        rows,
        stream_state,
        jnp.broadcast_to(scale, (TOK, 128)),
        gate_weight[0],
        up_weight[0],
        down_weight[0],
    )
    histogram = hist[:, : NBINS // 32].reshape(1, NBINS // N_CTX)
    return (layer_out, histogram)


def solution(mesh):
    return jax.shard_map(
        on_device,
        mesh=mesh,
        in_specs=(
            P(("ctx", "exp"), None),
            P(),
            P("ctx", "exp", None),
            P("ctx", "exp"),
            P("ctx", None),
            P("ctx", None),
            P("ctx"),
            P("exp", None, None),
            P("exp", None),
            P(("ctx", "exp"), None),
            P(("ctx", "exp"), None),
            P(("ctx", "exp"), None),
            P("exp", None, "ctx"),
            P("exp", None, "ctx"),
            P("exp", "ctx", None),
        ),
        out_specs=(P(("ctx", "exp"), None), P("exp", "ctx")),
        check_vma=False,
    )
```

```python
import functools
import math

import jax
import jax.numpy as jnp
from jax import lax
from jax.experimental import pallas as pl
from jax.experimental.pallas import tpu as pltpu
from jax.sharding import PartitionSpec as P

HID = 1024
NBINS = 2048


exponent_scale = 192.0 ** (-0.5) * math.log2(math.e)
norm_eps = 1e-06
masked_score = -1e30

NZ, NX, NY = 8, 4, 2
NQ = NX * NY
NR = NZ * NY
TOK = 8
CAP = 2
N_CTX = 4
N_EXPERTS = 64
ROPE = 64
VDIM = 128
DOC_ROWS = 16
KEY_PIECES = 2
SUBS = 2
MESH = pl.DeviceIdType.MESH


def remote(src, dst, send_sem, recv_sem, target):
    copy = pltpu.make_async_remote_copy(
        src_ref=src,
        dst_ref=dst,
        send_sem=send_sem,
        recv_sem=recv_sem,
        device_id=target,
        device_id_type=MESH,
    )
    copy.start()
    return copy


def greet(targets):
    barrier = pltpu.get_barrier_semaphore()
    for target in targets:
        pl.semaphore_signal(barrier, inc=1, device_id=target, device_id_type=MESH)
    pl.semaphore_wait(barrier, len(targets))


def small(cond):
    return cond.astype(jnp.float32).astype(jnp.bfloat16)


def split3(v):
    first = v.astype(jnp.bfloat16)
    rest = v - first.astype(jnp.float32)
    second = rest.astype(jnp.bfloat16)
    third = (rest - second.astype(jnp.float32)).astype(jnp.bfloat16)
    return first, second, third


def mm(a, b):
    return jnp.dot(a, b, preferred_element_type=jnp.float32)


def mm_t(a, b):
    return lax.dot_general(
        a, b, (((0,), (0,)), ((), ())), preferred_element_type=jnp.float32
    )


def attend_sum_kernel(
    part_a,
    query_ref,
    query_rope_ref,
    latent_ref,
    rope_ref,
    doc_ref,
    uv_hbm,
    weight_hbm,
    out_ref,
    uv_ref,
    weight_ref,
    tail_ref,
    keys,
    tails,
    top,
    denominator,
    accum,
    values_ref,
    a_first,
    a_slots,
    b_first,
    b_slots,
    a_push,
    a_got,
    b_push,
    b_got,
    k_send_sem,
    k_recv_sem,
    t_send_sem,
    t_recv_sem,
    a_send_sem,
    a_recv_sem,
    b_send_sem,
    b_recv_sem,
    ap_send_sem,
    ap_recv_sem,
    bp_send_sem,
    bp_recv_sem,
    load_sem,
):
    loads = [
        pltpu.make_async_copy(uv_hbm, uv_ref, load_sem.at[0]),
        pltpu.make_async_copy(weight_hbm, weight_ref, load_sem.at[1]),
    ]
    for load in loads:
        load.start()
    width = weight_ref.shape[1]
    wide_a, wide_b = part_a // (2 * SUBS), (width - part_a) // (2 * SUBS)
    me = lax.axis_index("exp")
    z, x, y = me // NQ, (me // NY) % NX, me % NY
    q, r = x * NY + y, z * NY + y

    def at(z_at, x_at, y_at):
        return {"exp": (z_at * NX + x_at) * NY + y_at}

    q_peers = [(q + j) % NQ for j in range(NQ)]
    r_peers = [(r + j) % NR for j in range(NR)]
    z_next = [at((z + 1) % NZ, x, y), at((z + NZ - 1) % NZ, x, y)]
    x_next = [at(z, (x + 1) % NX, y), at(z, (x + NX - 1) % NX, y)]
    ctx = lax.axis_index("ctx")
    y_lo, core = ctx // 2, ctx % 2
    mate = {"ctx": y_lo * 2 + 1 - core, "exp": me}
    across = {"ctx": (1 - y_lo) * 2 + core, "exp": me}
    greet(
        [at(z, p // NY, p % NY) for p in q_peers[1:]]
        + [at(p // NY, x, p % NY) for p in r_peers[1:]]
        + [mate, across]
    )

    block_len, lat = latent_ref.shape
    piece = block_len // KEY_PIECES
    for i in range(KEY_PIECES):
        tail_ref[i, :ROPE] = rope_ref[:, i * piece : (i + 1) * piece]
        tail_ref[i, ROPE:] = jnp.broadcast_to(
            doc_ref[:, i * piece : (i + 1) * piece].astype(jnp.float32),
            (DOC_ROWS, piece),
        ).astype(jnp.bfloat16)

    class KeyCopy:
        def __init__(self, back, i, forward, target):
            self.copies = [
                pltpu.make_async_remote_copy(
                    src_ref=src,
                    dst_ref=dst.at[back, i],
                    send_sem=send_sem.at[back, i],
                    recv_sem=recv_sem.at[back, i],
                    device_id=target,
                    device_id_type=MESH,
                )
                for src, dst, send_sem, recv_sem in (
                    (
                        keys.at[1, i]
                        if forward
                        else latent_ref.at[i * piece : (i + 1) * piece],
                        keys,
                        k_send_sem,
                        k_recv_sem,
                    ),
                    (
                        tails.at[1, i] if forward else tail_ref.at[i],
                        tails,
                        t_send_sem,
                        t_recv_sem,
                    ),
                )
            ]

        def start(self):
            for copy in self.copies:
                copy.start()

        def wait_recv(self):
            for copy in self.copies:
                copy.wait_recv()

        def wait_send(self):
            for copy in self.copies:
                copy.wait_send()

    for i in range(KEY_PIECES):

        @pl.when(y_lo == 0)
        def _():
            KeyCopy(1, i, False, across).start()

    for i in range(KEY_PIECES):

        @pl.when(core == 0)
        def _():
            KeyCopy(0, i, False, mate).start()

    def nt(a, b):
        return lax.dot_general(
            a, b, (((1,), (1,)), ((), ())), preferred_element_type=jnp.float32
        )

    heads = uv_ref.shape[0]
    doc_pick = small(lax.broadcasted_iota(jnp.int32, (DOC_ROWS, 128), 0) == 0)
    query_docs = jnp.concatenate(
        [mm_t(tail_ref[i, ROPE:], doc_pick)[:, :1] for i in range(KEY_PIECES)], axis=0
    )

    def fold(block, tail, offset=None):
        first = offset == 0
        allowed = query_docs == tail[ROPE : ROPE + 1].astype(jnp.float32)
        if offset is not None:
            shape = (block_len, block.shape[0])
            query_at = lax.broadcasted_iota(jnp.int32, shape, 0)
            key_at = lax.broadcasted_iota(jnp.int32, shape, 1) + offset
            allowed = allowed & (key_at <= query_at)
        for head in range(heads):
            nope = query_ref[:, head * lat : (head + 1) * lat]
            rope = query_rope_ref[:, head * ROPE : (head + 1) * ROPE]
            raw = nt(nope, block) + mm(rope, tail[:ROPE])
            scores = jnp.where(allowed, raw, masked_score)
            peak = jnp.max(scores, axis=1, keepdims=True)
            if not first:
                old = top[head][:, :1]
                peak = jnp.maximum(old, peak)
                fade = jnp.exp2((old - peak) * exponent_scale)
            probs = jnp.exp2((scores - peak) * exponent_scale)
            mass = jnp.sum(probs, axis=1, keepdims=True)
            mixed = mm(probs.astype(jnp.bfloat16), block)
            if not first:
                mass = mass + denominator[head][:, :1] * fade
                mixed = mixed + accum[head] * fade
            top[head] = jnp.broadcast_to(peak, top.shape[1:])
            denominator[head] = jnp.broadcast_to(mass, denominator.shape[1:])
            accum[head] = mixed

    for i in range(KEY_PIECES):
        fold(latent_ref[i * piece : (i + 1) * piece], tail_ref[i], i * piece)

    @pl.when(core == 1)
    def _():
        for i in range(KEY_PIECES):
            KeyCopy(0, i, False, mate).wait_recv()
            fold(keys[0, i], tails[0, i])

    @pl.when(y_lo == 1)
    def _():
        for i in range(KEY_PIECES):
            KeyCopy(1, i, False, across).wait_recv()

            @pl.when(core == 1)
            def _():
                KeyCopy(0, i, True, mate).start()

            fold(keys[1, i], tails[1, i])

    @pl.when(ctx == 2)
    def _():
        for i in range(KEY_PIECES):
            KeyCopy(0, i, False, mate).wait_recv()
            fold(keys[0, i], tails[0, i])

    for load in loads:
        load.wait()
    for head in range(heads):
        context = (accum[head] / denominator[head][:, :1]).astype(jnp.bfloat16)
        values_ref[:, :, :, head * VDIM : (head + 1) * VDIM] = (
            mm(context, uv_ref[head])
            .astype(jnp.bfloat16)
            .reshape(NZ, NX, NY * TOK, VDIM)
        )

    def a_own(way, sub, chunk):
        rows = values_ref[chunk].reshape(NX * NY * TOK, values_ref.shape[3])
        start = (way * SUBS + sub) * wide_a
        return mm(rows, weight_ref[:, start : start + wide_a])

    def b_own(way, sub, chunk):
        rows = values_ref[:, chunk].reshape(NZ * NY * TOK, values_ref.shape[3])
        start = part_a + (way * SUBS + sub) * wide_b
        return mm(rows, weight_ref[:, start : start + wide_b])

    a_flight, b_flight, pushes = {}, {}, []

    def ring_step(step, here, count, own_of, first, slots, sems, onward, flight):
        for sub in range(SUBS):
            for way in range(2):
                sign = -1 if way == 0 else 1
                own = own_of(way, sub, (here + sign * (1 + step) + 2 * count) % count)
                if step == 0:
                    src = first.at[way, sub]
                    first[way, sub] = own.astype(jnp.bfloat16)
                else:
                    src = slots.at[way, sub, step - 1]
                    flight[way, sub, step - 1].wait_recv()
                    slots[way, sub, step - 1] = (
                        slots[way, sub, step - 1].astype(jnp.float32) + own
                    ).astype(jnp.bfloat16)
                flight[way, sub, step] = remote(
                    src,
                    slots.at[way, sub, step],
                    sems[0].at[way, sub, step],
                    sems[1].at[way, sub, step],
                    onward[way],
                )

    def a_step(step):
        ring_step(
            step, z, NZ, a_own, a_first, a_slots,
            (a_send_sem, a_recv_sem), z_next, a_flight,
        )

    def b_step(step):
        ring_step(
            step, x, NX, b_own, b_first, b_slots,
            (b_send_sem, b_recv_sem), x_next, b_flight,
        )

    def a_push_out():
        for sub in range(SUBS):
            for way in range(2):
                own = a_own(way, sub, z)
                a_flight[way, sub, NZ - 2].wait_recv()
                own = own + a_slots[way, sub, NZ - 2].astype(jnp.float32)
                start = (way * SUBS + sub) * wide_a
                a_push[:, :, start : start + wide_a] = own.reshape(
                    NQ, TOK, wide_a
                ).astype(jnp.bfloat16)
        for j in range(1, NQ):
            p = q_peers[j]
            pushes.append(
                remote(
                    a_push.at[p],
                    a_got.at[j - 1],
                    ap_send_sem.at[j - 1],
                    ap_recv_sem.at[j - 1],
                    at(z, p // NY, p % NY),
                )
            )

    def b_push_out():
        for sub in range(SUBS):
            for way in range(2):
                own = b_own(way, sub, x)
                b_flight[way, sub, NX - 2].wait_recv()
                own = own + b_slots[way, sub, NX - 2].astype(jnp.float32)
                start = (way * SUBS + sub) * wide_b
                b_push[:, :, start : start + wide_b] = own.reshape(
                    NR, TOK, wide_b
                ).astype(jnp.bfloat16)
        for j in range(1, NR):
            p = r_peers[j]
            pushes.append(
                remote(
                    b_push.at[p],
                    b_got.at[j - 1],
                    bp_send_sem.at[j - 1],
                    bp_recv_sem.at[j - 1],
                    at(p // NY, x, p % NY),
                )
            )

    a_step(0)
    b_step(0)
    a_step(1)
    a_step(2)
    b_step(1)
    a_step(3)
    b_step(2)
    a_step(4)
    b_push_out()
    a_step(5)
    a_step(6)
    a_push_out()
    for copy in pushes:
        copy.wait_recv()
    total = b_push[r].astype(jnp.float32)
    for j in range(NR - 1):
        total = total + b_got[j].astype(jnp.float32)
    out_ref[:, part_a:] = total
    total = a_push[q].astype(jnp.float32)
    for j in range(NQ - 1):
        total = total + a_got[j].astype(jnp.float32)
    out_ref[:, :part_a] = total
    for copy in [*a_flight.values(), *b_flight.values(), *pushes]:
        copy.wait_send()
    for i in range(KEY_PIECES):

        @pl.when(y_lo == 0)
        def _():
            KeyCopy(1, i, False, across).wait_send()

        @pl.when((core == 0) | (y_lo == 1))
        def _():
            KeyCopy(0, i, False, mate).wait_send()


def attend_sum(q_nope, q_rope, latent, rope_t, docs, uv_weight, weight, part_a=2048):
    heads, lat = uv_weight.shape[:2]
    rows = latent.shape[0]
    width = weight.shape[1]
    part_b = width - part_a
    wide_a, wide_b = part_a // (2 * SUBS), part_b // (2 * SUBS)
    bf16 = jnp.bfloat16
    dma = pltpu.SemaphoreType.DMA
    return pl.pallas_call(
        functools.partial(attend_sum_kernel, part_a),
        out_shape=jax.ShapeDtypeStruct((TOK, width), jnp.float32),
        in_specs=[pl.BlockSpec(memory_space=pltpu.VMEM)] * 5
        + [pl.BlockSpec(memory_space=pltpu.HBM)] * 2,
        out_specs=pl.BlockSpec(memory_space=pltpu.VMEM),
        scratch_shapes=[
            pltpu.VMEM(uv_weight.shape, bf16),
            pltpu.VMEM(weight.shape, bf16),
            pltpu.VMEM((KEY_PIECES, ROPE + DOC_ROWS, rows // KEY_PIECES), bf16),
            pltpu.VMEM((2, KEY_PIECES, rows // KEY_PIECES, lat), bf16),
            pltpu.VMEM((2, KEY_PIECES, ROPE + DOC_ROWS, rows // KEY_PIECES), bf16),
            pltpu.VMEM((heads, rows, 128), jnp.float32),
            pltpu.VMEM((heads, rows, 128), jnp.float32),
            pltpu.VMEM((heads, rows, lat), jnp.float32),
            pltpu.VMEM((NZ, NX, NY * TOK, heads * VDIM), bf16),
            pltpu.VMEM((2, SUBS, NQ * TOK, wide_a), bf16),
            pltpu.VMEM((2, SUBS, NZ - 1, NQ * TOK, wide_a), bf16),
            pltpu.VMEM((2, SUBS, NR * TOK, wide_b), bf16),
            pltpu.VMEM((2, SUBS, NX - 1, NR * TOK, wide_b), bf16),
            pltpu.VMEM((NQ, TOK, part_a), bf16),
            pltpu.VMEM((NQ - 1, TOK, part_a), bf16),
            pltpu.VMEM((NR, TOK, part_b), bf16),
            pltpu.VMEM((NR - 1, TOK, part_b), bf16),
            dma((2, KEY_PIECES)),
            dma((2, KEY_PIECES)),
            dma((2, KEY_PIECES)),
            dma((2, KEY_PIECES)),
            dma((2, SUBS, NZ - 1)),
            dma((2, SUBS, NZ - 1)),
            dma((2, SUBS, NX - 1)),
            dma((2, SUBS, NX - 1)),
            dma((NQ - 1,)),
            dma((NQ - 1,)),
            dma((NR - 1,)),
            dma((NR - 1,)),
            dma((2,)),
        ],
        compiler_params=pltpu.CompilerParams(
            collective_id=0, has_side_effects=True, vmem_limit_bytes=60 << 20
        ),
        name="attend_sum",
    )(q_nope, q_rope, latent, rope_t, docs, uv_weight, weight)


def experts_kernel(
    rows_ref,
    state_ref,
    scale_ref,
    gate_hbm,
    up_hbm,
    down_hbm,
    out_ref,
    hist_ref,
    gate_ref,
    up_ref,
    down_ref,
    near,
    weigh,
    slots,
    inbox,
    kept,
    to_mate,
    from_mate,
    back,
    returned,
    to_y,
    from_y,
    to_z,
    from_z,
    hist_out,
    hist_in,
    load_sem,
    z_send,
    z_recv,
    y_send,
    y_recv,
    q_send,
    q_recv,
    m_send,
    m_recv,
    o_send,
    o_recv,
    b_send,
    b_recv,
    ys_send,
    ys_recv,
    zs_send,
    zs_recv,
    h_send,
    h_recv,
):
    width = state_ref.shape[1]
    sent = width + 2 * N_EXPERTS
    half_rows, half_slots = NZ * TOK, NQ * NZ * CAP
    piece = NZ * CAP
    ctx, me = lax.axis_index("ctx"), lax.axis_index("exp")
    y_lo, core = ctx // 2, ctx % 2
    z, q = me // NQ, me % NQ

    def z_peer(z_at):
        return {"ctx": ctx, "exp": z_at * NQ + q}

    def q_peer(q_at):
        return {"ctx": ctx, "exp": z * NQ + q_at}

    y_peer = {"ctx": (1 - y_lo) * 2 + core, "exp": me}
    mate = {"ctx": y_lo * 2 + 1 - core, "exp": me}

    def c_peer(j):
        return {"ctx": (ctx + j) % N_CTX, "exp": me}

    loads = [
        pltpu.make_async_copy(src, dst, load_sem.at[i])
        for i, (src, dst) in enumerate(
            ((gate_hbm, gate_ref), (up_hbm, up_ref), (down_hbm, down_ref))
        )
    ]
    for load in loads:
        load.start()
    greet(
        [z_peer((z + j) % NZ) for j in range(1, NZ)]
        + [q_peer((q + j) % NQ) for j in range(1, NQ)]
        + [c_peer(j) for j in range(1, N_CTX)]
    )
    pending = []

    order = (1, 7, 2, 6, 3, 5, 4)
    arrivals = {}
    for j in order:
        arrivals[j] = remote(
            rows_ref, near.at[y_lo, z], z_send.at[j], z_recv.at[j], z_peer((z + j) % NZ)
        )
        pending.append(arrivals[j])
    near[y_lo, z] = rows_ref[...]
    crossings = [remote(rows_ref, near.at[y_lo, z], y_send.at[0], y_recv.at[0], y_peer)]
    for j in order:
        z_from = (z + NZ - j) % NZ
        arrivals[j].wait_recv()
        crossings.append(
            remote(
                near.at[y_lo, z_from],
                near.at[y_lo, z_from],
                y_send.at[j],
                y_recv.at[j],
                y_peer,
            )
        )
    pending += crossings

    lane = lax.broadcasted_iota(jnp.int32, (2 * N_EXPERTS, half_slots), 0)
    wanted = z * NQ + (
        lax.broadcasted_iota(jnp.int32, (2 * N_EXPERTS, half_slots), 1) // piece
    )
    pick_level, pick_rank = small(lane == wanted), small(lane == wanted + N_EXPERTS)
    row = lax.broadcasted_iota(jnp.int32, (half_rows, half_slots), 0)
    col = lax.broadcasted_iota(jnp.int32, (half_rows, half_slots), 1)
    same_source = (row // TOK) == ((col // CAP) % NZ)
    slot_rank = (col % CAP).astype(jnp.float32)

    slot_flight = {}
    for half in range(2):
        if half == 1:
            for copy in crossings:
                copy.wait_recv()
        y_at = y_lo if half == 0 else 1 - y_lo
        held = (
            near[y_at]
            .astype(jnp.float32)
            .reshape(half_rows, sent + 2 * N_EXPERTS)
            .astype(jnp.bfloat16)
        )
        route = held[:, sent:]
        level, rank = mm(route, pick_level), mm(route, pick_rank)
        chosen = (level > 0.5) & (rank == slot_rank) & same_source
        weigh[half] = jnp.where(chosen, level, 0.0).astype(jnp.bfloat16)
        picked = mm_t(small(chosen), held[:, :sent])
        slots[half] = picked.astype(jnp.bfloat16).reshape(NQ, piece, sent)
        for j in order:
            p = (q + j) % NQ
            slot_flight[half, j] = remote(
                slots.at[half, p],
                inbox.at[0, half, q],
                q_send.at[half, j],
                q_recv.at[half, j],
                q_peer(p),
            )
        inbox[0, half, q] = slots[half, q]
    pending += slot_flight.values()

    mate_flight = []
    for half in range(2):
        for j in (0,) + order:
            q_from = (q + NQ - j) % NQ
            if j:
                slot_flight[half, j].wait_recv()
            mate_flight.append(
                remote(
                    inbox.at[0, half, q_from],
                    inbox.at[1, half, q_from],
                    m_send.at[half, j],
                    m_recv.at[half, j],
                    mate,
                )
            )
    pending += mate_flight

    bin_lane = lax.broadcasted_iota(jnp.int32, (2 * half_slots, 2 * N_EXPERTS), 1)
    bins_at = bin_lane.astype(jnp.float32)

    def run_block(which):
        block = inbox[which].reshape(2 * half_slots, sent)
        x = block[:, :width]
        gate_part, up_part = mm(x, gate_ref[...]), mm(x, up_ref[...])
        activation = gate_part / (1.0 + jnp.exp(-gate_part)) * up_part
        energy = jnp.sum(activation * activation, axis=1, keepdims=True) * (1.0 / HID)
        tail = block[:, width:].astype(jnp.float32)
        high = jnp.sum(jnp.where(bin_lane == me, tail, 0.0), axis=1, keepdims=True)
        low = jnp.sum(
            jnp.where(bin_lane == me + N_EXPERTS, tail, 0.0), axis=1, keepdims=True
        )
        at_high = jnp.where(high == bins_at, energy, 0.0)
        at_low = small(low == bins_at)
        first, second, third = split3(at_high)
        hist = mm_t(first, at_low) + mm_t(second, at_low) + mm_t(third, at_low)
        return activation.astype(jnp.bfloat16), hist

    for load in loads:
        load.wait()
    hidden, hist = run_block(0)
    kept[...] = mm(hidden, down_ref[...])
    for copy in mate_flight:
        copy.wait_recv()
    hidden, more = run_block(1)
    to_mate[...] = (
        mm(hidden, down_ref[...]).astype(jnp.bfloat16).reshape(to_mate.shape)
    )
    mate_out = {}
    for half in (1, 0):
        mate_out[half] = remote(
            to_mate.at[half], from_mate.at[half], o_send.at[half], o_recv.at[half], mate
        )
    pending += mate_out.values()

    hist_out[...] = (hist + more)[: N_CTX * 8].reshape(N_CTX, 8, 2 * N_EXPERTS)
    hist_flight = [
        remote(
            hist_out.at[(ctx + j) % N_CTX],
            hist_in.at[j - 1],
            h_send.at[j - 1],
            h_recv.at[j - 1],
            c_peer(j),
        )
        for j in range(1, N_CTX)
    ]
    pending += hist_flight

    back_flight = {}
    for half in (1, 0):
        mate_out[half].wait_recv()
        total = kept[half * half_slots : (half + 1) * half_slots] + from_mate[
            half
        ].reshape(half_slots, width).astype(jnp.float32)
        back[half] = total.astype(jnp.bfloat16).reshape(NQ, piece, width)
        for j in order:
            p = (q + j) % NQ
            back_flight[half, j] = remote(
                back.at[half, p],
                returned.at[half, q],
                b_send.at[half, j],
                b_recv.at[half, j],
                q_peer(p),
            )
        returned[half, q] = back[half, q]
    pending += back_flight.values()

    def mixed(half):
        for j in order:
            back_flight[half, j].wait_recv()
        return mm(weigh[half], returned[half].reshape(half_slots, width))

    to_y[...] = mixed(1).reshape(NZ, TOK, width).astype(jnp.bfloat16)
    y_flight = [
        remote(to_y.at[j], from_y.at[j], ys_send.at[j], ys_recv.at[j], y_peer)
        for j in range(NZ)
    ]
    pending += y_flight
    own = mixed(0).reshape(NZ, TOK, width)
    for copy in y_flight:
        copy.wait_recv()
    to_z[...] = (own + from_y[...].astype(jnp.float32)).astype(jnp.bfloat16)
    z_flight = []
    for j in order:
        z_to = (z + j) % NZ
        z_flight.append(
            remote(
                to_z.at[z_to],
                from_z.at[j - 1],
                zs_send.at[j - 1],
                zs_recv.at[j - 1],
                z_peer(z_to),
            )
        )
    pending += z_flight
    for copy in hist_flight:
        copy.wait_recv()
    hist = hist_out[ctx]
    for j in range(N_CTX - 1):
        hist = hist + hist_in[j]
    hist_ref[...] = hist
    for copy in z_flight:
        copy.wait_recv()
    total = to_z[z].astype(jnp.float32)
    for j in range(NZ - 1):
        total = total + from_z[j].astype(jnp.float32)
    out_ref[...] = (state_ref[...] + total * scale_ref[:, :1]).astype(jnp.bfloat16)
    for copy in pending:
        copy.wait_send()


def run_experts(rows, state, scale, gate, up, down):
    width = state.shape[1]
    sent = width + 2 * N_EXPERTS
    half_slots, piece = NQ * NZ * CAP, NZ * CAP
    bf16, f32 = jnp.bfloat16, jnp.float32
    dma = pltpu.SemaphoreType.DMA
    vmem = pl.BlockSpec(memory_space=pltpu.VMEM)
    hbm = pl.BlockSpec(memory_space=pltpu.HBM)
    return pl.pallas_call(
        experts_kernel,
        out_shape=(
            jax.ShapeDtypeStruct((TOK, width), bf16),
            jax.ShapeDtypeStruct((8, 2 * N_EXPERTS), f32),
        ),
        in_specs=[vmem, vmem, vmem, hbm, hbm, hbm],
        out_specs=(vmem, vmem),
        scratch_shapes=[
            pltpu.VMEM(gate.shape, bf16),
            pltpu.VMEM(up.shape, bf16),
            pltpu.VMEM(down.shape, bf16),
            pltpu.VMEM((2, NZ, TOK, rows.shape[1]), bf16),
            pltpu.VMEM((2, NZ * TOK, half_slots), bf16),
            pltpu.VMEM((2, NQ, piece, sent), bf16),
            pltpu.VMEM((2, 2, NQ, piece, sent), bf16),
            pltpu.VMEM((2 * half_slots, width), f32),
            pltpu.VMEM((2, NQ, piece, width), bf16),
            pltpu.VMEM((2, NQ, piece, width), bf16),
            pltpu.VMEM((2, NQ, piece, width), bf16),
            pltpu.VMEM((2, NQ, piece, width), bf16),
            pltpu.VMEM((NZ, TOK, width), bf16),
            pltpu.VMEM((NZ, TOK, width), bf16),
            pltpu.VMEM((NZ, TOK, width), bf16),
            pltpu.VMEM((NZ - 1, TOK, width), bf16),
            pltpu.VMEM((N_CTX, 8, 2 * N_EXPERTS), f32),
            pltpu.VMEM((N_CTX - 1, 8, 2 * N_EXPERTS), f32),
            dma((3,)),
            dma((NZ,)),
            dma((NZ,)),
            dma((NZ,)),
            dma((NZ,)),
            dma((2, NQ)),
            dma((2, NQ)),
            dma((2, NQ)),
            dma((2, NQ)),
            dma((2,)),
            dma((2,)),
            dma((2, NQ)),
            dma((2, NQ)),
            dma((NZ,)),
            dma((NZ,)),
            dma((NZ - 1,)),
            dma((NZ - 1,)),
            dma((N_CTX - 1,)),
            dma((N_CTX - 1,)),
        ],
        compiler_params=pltpu.CompilerParams(
            collective_id=1, has_side_effects=True, vmem_limit_bytes=60 << 20
        ),
        name="experts",
    )(rows, state, scale, gate, up, down)


def route_lanes(expert_ids, gate_levels, bin_ids):
    onehot = expert_ids[:, :, None] == jnp.arange(N_EXPERTS, dtype=jnp.int32)

    def spread(v):
        return jnp.sum(jnp.where(onehot, v[:, :, None], 0), axis=1)

    named = jnp.sum(onehot.astype(jnp.int32), axis=1)
    earlier = jnp.arange(TOK)[:, None] > jnp.arange(TOK)[None, :]
    rank = jnp.sum(jnp.where(earlier[:, :, None], named[None, :, :], 0), axis=1)
    lanes = (spread(bin_ids // 64), spread(bin_ids % 64), spread(gate_levels), rank)
    return jnp.concatenate(lanes, axis=1).astype(jnp.bfloat16)


def on_device(
    residual_in,
    norm_gain,
    q_nope,
    q_rope,
    latent,
    k_rope,
    doc_ids,
    uv_weight,
    out_weight,
    expert_ids,
    gate_levels,
    bin_ids,
    gate_weight,
    up_weight,
    down_weight,
):
    block_len, head_count, _ = q_nope.shape
    attended = attend_sum(
        q_nope.reshape(block_len, head_count * q_nope.shape[2]),
        q_rope,
        latent,
        k_rope.T,
        doc_ids.reshape(1, block_len),
        uv_weight,
        out_weight,
    )
    stream_state = residual_in.astype(jnp.float32) + attended
    normed = (
        stream_state
        * lax.rsqrt(jnp.mean(stream_state * stream_state, axis=1, keepdims=True) + norm_eps)
        * norm_gain
    ).astype(jnp.bfloat16)
    rows = jnp.concatenate(
        (normed, route_lanes(expert_ids, gate_levels, bin_ids)), axis=1
    )
    scale = 1.0 / jnp.sum(gate_levels.astype(jnp.float32), axis=1, keepdims=True)
    layer_out, hist = run_experts(
        rows,
        stream_state,
        jnp.broadcast_to(scale, (TOK, 128)),
        gate_weight[0],
        up_weight[0],
        down_weight[0],
    )
    histogram = hist[:, : NBINS // 32].reshape(1, NBINS // N_CTX)
    return (layer_out, histogram)


def solution(mesh):
    return jax.shard_map(
        on_device,
        mesh=mesh,
        in_specs=(
            P(("ctx", "exp"), None),
            P(),
            P("ctx", "exp", None),
            P("ctx", "exp"),
            P("ctx", None),
            P("ctx", None),
            P("ctx"),
            P("exp", None, None),
            P("exp", None),
            P(("ctx", "exp"), None),
            P(("ctx", "exp"), None),
            P(("ctx", "exp"), None),
            P("exp", None, "ctx"),
            P("exp", None, "ctx"),
            P("exp", "ctx", None),
        ),
        out_specs=(P(("ctx", "exp"), None), P("exp", "ctx")),
        check_vma=False,
    )
```

```python
import functools
import math

import jax
import jax.numpy as jnp
from jax import lax
from jax.experimental import pallas as pl
from jax.experimental.pallas import tpu as pltpu
from jax.sharding import PartitionSpec as P

HID = 1024
NBINS = 2048


exponent_scale = 192.0 ** (-0.5) * math.log2(math.e)
norm_eps = 1e-06
masked_score = -1e30

NZ, NX, NY = 8, 4, 2
NQ = NX * NY
NR = NZ * NY
TOK = 8
CAP = 2
N_CTX = 4
N_EXPERTS = 64
ROPE = 64
VDIM = 128
DOC_ROWS = 16
KEY_PIECES = 2
SUBS = 2
MESH = pl.DeviceIdType.MESH


def remote(src, dst, send_sem, recv_sem, target):
    copy = pltpu.make_async_remote_copy(
        src_ref=src,
        dst_ref=dst,
        send_sem=send_sem,
        recv_sem=recv_sem,
        device_id=target,
        device_id_type=MESH,
    )
    copy.start()
    return copy


def greet(targets):
    barrier = pltpu.get_barrier_semaphore()
    for target in targets:
        pl.semaphore_signal(barrier, inc=1, device_id=target, device_id_type=MESH)
    pl.semaphore_wait(barrier, len(targets))


def small(cond):
    return cond.astype(jnp.float32).astype(jnp.bfloat16)


def split3(v):
    first = v.astype(jnp.bfloat16)
    rest = v - first.astype(jnp.float32)
    second = rest.astype(jnp.bfloat16)
    third = (rest - second.astype(jnp.float32)).astype(jnp.bfloat16)
    return first, second, third


def mm(a, b):
    return jnp.dot(a, b, preferred_element_type=jnp.float32)


def mm_t(a, b):
    return lax.dot_general(
        a, b, (((0,), (0,)), ((), ())), preferred_element_type=jnp.float32
    )


def attend_sum_kernel(
    part_a,
    query_ref,
    query_rope_ref,
    latent_ref,
    rope_ref,
    doc_ref,
    uv_hbm,
    weight_hbm,
    out_ref,
    uv_ref,
    weight_ref,
    tail_ref,
    keys,
    tails,
    top,
    denominator,
    accum,
    values_ref,
    a_first,
    a_slots,
    b_first,
    b_slots,
    a_push,
    a_got,
    b_push,
    b_got,
    k_send_sem,
    k_recv_sem,
    t_send_sem,
    t_recv_sem,
    a_send_sem,
    a_recv_sem,
    b_send_sem,
    b_recv_sem,
    ap_send_sem,
    ap_recv_sem,
    bp_send_sem,
    bp_recv_sem,
    load_sem,
):
    loads = [
        pltpu.make_async_copy(uv_hbm, uv_ref, load_sem.at[0]),
        pltpu.make_async_copy(weight_hbm, weight_ref, load_sem.at[1]),
    ]
    for load in loads:
        load.start()
    width = weight_ref.shape[1]
    wide_a, wide_b = part_a // (2 * SUBS), (width - part_a) // (2 * SUBS)
    me = lax.axis_index("exp")
    z, x, y = me // NQ, (me // NY) % NX, me % NY
    q, r = x * NY + y, z * NY + y

    def at(z_at, x_at, y_at):
        return {"exp": (z_at * NX + x_at) * NY + y_at}

    q_peers = [(q + j) % NQ for j in range(NQ)]
    r_peers = [(r + j) % NR for j in range(NR)]
    z_next = [at((z + 1) % NZ, x, y), at((z + NZ - 1) % NZ, x, y)]
    x_next = [at(z, (x + 1) % NX, y), at(z, (x + NX - 1) % NX, y)]
    ctx = lax.axis_index("ctx")
    y_lo, core = ctx // 2, ctx % 2
    mate = {"ctx": y_lo * 2 + 1 - core, "exp": me}
    across = {"ctx": (1 - y_lo) * 2 + core, "exp": me}
    greet(
        [at(z, p // NY, p % NY) for p in q_peers[1:]]
        + [at(p // NY, x, p % NY) for p in r_peers[1:]]
        + [mate, across]
    )

    block_len, lat = latent_ref.shape
    piece = block_len // KEY_PIECES
    for i in range(KEY_PIECES):
        tail_ref[i, :ROPE] = rope_ref[:, i * piece : (i + 1) * piece]
        tail_ref[i, ROPE:] = jnp.broadcast_to(
            doc_ref[:, i * piece : (i + 1) * piece].astype(jnp.float32),
            (DOC_ROWS, piece),
        ).astype(jnp.bfloat16)

    class KeyCopy:
        def __init__(self, back, i, forward, target):
            self.copies = [
                pltpu.make_async_remote_copy(
                    src_ref=src,
                    dst_ref=dst.at[back, i],
                    send_sem=send_sem.at[back, i],
                    recv_sem=recv_sem.at[back, i],
                    device_id=target,
                    device_id_type=MESH,
                )
                for src, dst, send_sem, recv_sem in (
                    (
                        keys.at[1, i]
                        if forward
                        else latent_ref.at[i * piece : (i + 1) * piece],
                        keys,
                        k_send_sem,
                        k_recv_sem,
                    ),
                    (
                        tails.at[1, i] if forward else tail_ref.at[i],
                        tails,
                        t_send_sem,
                        t_recv_sem,
                    ),
                )
            ]

        def start(self):
            for copy in self.copies:
                copy.start()

        def wait_recv(self):
            for copy in self.copies:
                copy.wait_recv()

        def wait_send(self):
            for copy in self.copies:
                copy.wait_send()

    for i in range(KEY_PIECES):

        @pl.when(y_lo == 0)
        def _():
            KeyCopy(1, i, False, across).start()

    for i in range(KEY_PIECES):

        @pl.when(core == 0)
        def _():
            KeyCopy(0, i, False, mate).start()

    def nt(a, b):
        return lax.dot_general(
            a, b, (((1,), (1,)), ((), ())), preferred_element_type=jnp.float32
        )

    heads = uv_ref.shape[0]
    doc_pick = small(lax.broadcasted_iota(jnp.int32, (DOC_ROWS, 128), 0) == 0)
    query_docs = jnp.concatenate(
        [mm_t(tail_ref[i, ROPE:], doc_pick)[:, :1] for i in range(KEY_PIECES)], axis=0
    )

    def fold(block, tail, offset=None):
        first = offset == 0
        allowed = query_docs == tail[ROPE : ROPE + 1].astype(jnp.float32)
        if offset is not None:
            shape = (block_len, block.shape[0])
            query_at = lax.broadcasted_iota(jnp.int32, shape, 0)
            key_at = lax.broadcasted_iota(jnp.int32, shape, 1) + offset
            allowed = allowed & (key_at <= query_at)
        for head in range(heads):
            nope = query_ref[:, head * lat : (head + 1) * lat]
            rope = query_rope_ref[:, head * ROPE : (head + 1) * ROPE]
            raw = nt(nope, block) + mm(rope, tail[:ROPE])
            scores = jnp.where(allowed, raw, masked_score)
            peak = jnp.max(scores, axis=1, keepdims=True)
            if not first:
                old = top[head][:, :1]
                peak = jnp.maximum(old, peak)
                fade = jnp.exp2((old - peak) * exponent_scale)
            probs = jnp.exp2((scores - peak) * exponent_scale)
            mass = jnp.sum(probs, axis=1, keepdims=True)
            mixed = mm(probs.astype(jnp.bfloat16), block)
            if not first:
                mass = mass + denominator[head][:, :1] * fade
                mixed = mixed + accum[head] * fade
            top[head] = jnp.broadcast_to(peak, top.shape[1:])
            denominator[head] = jnp.broadcast_to(mass, denominator.shape[1:])
            accum[head] = mixed

    for i in range(KEY_PIECES):
        fold(latent_ref[i * piece : (i + 1) * piece], tail_ref[i], i * piece)

    def fold_from(back, i, target):
        KeyCopy(back, i, False, target).wait_recv()
        if back == 1:

            @pl.when(core == 1)
            def _():
                KeyCopy(0, i, True, mate).start()

        fold(keys[back, i], tails[back, i])

    @pl.when(ctx == 1)
    def _():
        for i in range(KEY_PIECES):
            fold_from(0, i, mate)

    for i in range(KEY_PIECES):

        @pl.when(y_lo == 1)
        def _():
            fold_from(1, i, across)

        if i == 0:

            @pl.when(ctx == 3)
            def _():
                for k in range(KEY_PIECES):
                    fold_from(0, k, mate)

        @pl.when(ctx == 2)
        def _():
            fold_from(0, i, mate)

    for load in loads:
        load.wait()
    for head in range(heads):
        context = (accum[head] / denominator[head][:, :1]).astype(jnp.bfloat16)
        values_ref[:, :, :, head * VDIM : (head + 1) * VDIM] = (
            mm(context, uv_ref[head])
            .astype(jnp.bfloat16)
            .reshape(NZ, NX, NY * TOK, VDIM)
        )

    def a_own(way, sub, chunk):
        rows = values_ref[chunk].reshape(NX * NY * TOK, values_ref.shape[3])
        start = (way * SUBS + sub) * wide_a
        return mm(rows, weight_ref[:, start : start + wide_a])

    def b_own(way, sub, chunk):
        rows = values_ref[:, chunk].reshape(NZ * NY * TOK, values_ref.shape[3])
        start = part_a + (way * SUBS + sub) * wide_b
        return mm(rows, weight_ref[:, start : start + wide_b])

    a_flight, b_flight, pushes = {}, {}, []

    def ring_step(step, here, count, own_of, first, slots, sems, onward, flight):
        for sub in range(SUBS):
            for way in range(2):
                sign = -1 if way == 0 else 1
                own = own_of(way, sub, (here + sign * (1 + step) + 2 * count) % count)
                if step == 0:
                    src = first.at[way, sub]
                    first[way, sub] = own.astype(jnp.bfloat16)
                else:
                    src = slots.at[way, sub, step - 1]
                    flight[way, sub, step - 1].wait_recv()
                    slots[way, sub, step - 1] = (
                        slots[way, sub, step - 1].astype(jnp.float32) + own
                    ).astype(jnp.bfloat16)
                flight[way, sub, step] = remote(
                    src,
                    slots.at[way, sub, step],
                    sems[0].at[way, sub, step],
                    sems[1].at[way, sub, step],
                    onward[way],
                )

    def a_step(step):
        ring_step(
            step, z, NZ, a_own, a_first, a_slots,
            (a_send_sem, a_recv_sem), z_next, a_flight,
        )

    def b_step(step):
        ring_step(
            step, x, NX, b_own, b_first, b_slots,
            (b_send_sem, b_recv_sem), x_next, b_flight,
        )

    def a_push_out():
        for sub in range(SUBS):
            for way in range(2):
                own = a_own(way, sub, z)
                a_flight[way, sub, NZ - 2].wait_recv()
                own = own + a_slots[way, sub, NZ - 2].astype(jnp.float32)
                start = (way * SUBS + sub) * wide_a
                a_push[:, :, start : start + wide_a] = own.reshape(
                    NQ, TOK, wide_a
                ).astype(jnp.bfloat16)
        for j in range(1, NQ):
            p = q_peers[j]
            pushes.append(
                remote(
                    a_push.at[p],
                    a_got.at[j - 1],
                    ap_send_sem.at[j - 1],
                    ap_recv_sem.at[j - 1],
                    at(z, p // NY, p % NY),
                )
            )

    def b_push_out():
        for sub in range(SUBS):
            for way in range(2):
                own = b_own(way, sub, x)
                b_flight[way, sub, NX - 2].wait_recv()
                own = own + b_slots[way, sub, NX - 2].astype(jnp.float32)
                start = (way * SUBS + sub) * wide_b
                b_push[:, :, start : start + wide_b] = own.reshape(
                    NR, TOK, wide_b
                ).astype(jnp.bfloat16)
        for j in range(1, NR):
            p = r_peers[j]
            pushes.append(
                remote(
                    b_push.at[p],
                    b_got.at[j - 1],
                    bp_send_sem.at[j - 1],
                    bp_recv_sem.at[j - 1],
                    at(p // NY, x, p % NY),
                )
            )

    a_step(0)
    b_step(0)
    a_step(1)
    a_step(2)
    b_step(1)
    a_step(3)
    b_step(2)
    a_step(4)
    b_push_out()
    a_step(5)
    a_step(6)
    a_push_out()
    for copy in pushes:
        copy.wait_recv()
    total = b_push[r].astype(jnp.float32)
    for j in range(NR - 1):
        total = total + b_got[j].astype(jnp.float32)
    out_ref[:, part_a:] = total
    total = a_push[q].astype(jnp.float32)
    for j in range(NQ - 1):
        total = total + a_got[j].astype(jnp.float32)
    out_ref[:, :part_a] = total
    for copy in [*a_flight.values(), *b_flight.values(), *pushes]:
        copy.wait_send()
    for i in range(KEY_PIECES):

        @pl.when(y_lo == 0)
        def _():
            KeyCopy(1, i, False, across).wait_send()

        @pl.when((core == 0) | (y_lo == 1))
        def _():
            KeyCopy(0, i, False, mate).wait_send()


def attend_sum(q_nope, q_rope, latent, rope_t, docs, uv_weight, weight, part_a=2048):
    heads, lat = uv_weight.shape[:2]
    rows = latent.shape[0]
    width = weight.shape[1]
    part_b = width - part_a
    wide_a, wide_b = part_a // (2 * SUBS), part_b // (2 * SUBS)
    bf16 = jnp.bfloat16
    dma = pltpu.SemaphoreType.DMA
    return pl.pallas_call(
        functools.partial(attend_sum_kernel, part_a),
        out_shape=jax.ShapeDtypeStruct((TOK, width), jnp.float32),
        in_specs=[pl.BlockSpec(memory_space=pltpu.VMEM)] * 5
        + [pl.BlockSpec(memory_space=pltpu.HBM)] * 2,
        out_specs=pl.BlockSpec(memory_space=pltpu.VMEM),
        scratch_shapes=[
            pltpu.VMEM(uv_weight.shape, bf16),
            pltpu.VMEM(weight.shape, bf16),
            pltpu.VMEM((KEY_PIECES, ROPE + DOC_ROWS, rows // KEY_PIECES), bf16),
            pltpu.VMEM((2, KEY_PIECES, rows // KEY_PIECES, lat), bf16),
            pltpu.VMEM((2, KEY_PIECES, ROPE + DOC_ROWS, rows // KEY_PIECES), bf16),
            pltpu.VMEM((heads, rows, 128), jnp.float32),
            pltpu.VMEM((heads, rows, 128), jnp.float32),
            pltpu.VMEM((heads, rows, lat), jnp.float32),
            pltpu.VMEM((NZ, NX, NY * TOK, heads * VDIM), bf16),
            pltpu.VMEM((2, SUBS, NQ * TOK, wide_a), bf16),
            pltpu.VMEM((2, SUBS, NZ - 1, NQ * TOK, wide_a), bf16),
            pltpu.VMEM((2, SUBS, NR * TOK, wide_b), bf16),
            pltpu.VMEM((2, SUBS, NX - 1, NR * TOK, wide_b), bf16),
            pltpu.VMEM((NQ, TOK, part_a), bf16),
            pltpu.VMEM((NQ - 1, TOK, part_a), bf16),
            pltpu.VMEM((NR, TOK, part_b), bf16),
            pltpu.VMEM((NR - 1, TOK, part_b), bf16),
            dma((2, KEY_PIECES)),
            dma((2, KEY_PIECES)),
            dma((2, KEY_PIECES)),
            dma((2, KEY_PIECES)),
            dma((2, SUBS, NZ - 1)),
            dma((2, SUBS, NZ - 1)),
            dma((2, SUBS, NX - 1)),
            dma((2, SUBS, NX - 1)),
            dma((NQ - 1,)),
            dma((NQ - 1,)),
            dma((NR - 1,)),
            dma((NR - 1,)),
            dma((2,)),
        ],
        compiler_params=pltpu.CompilerParams(
            collective_id=0, has_side_effects=True, vmem_limit_bytes=60 << 20
        ),
        name="attend_sum",
    )(q_nope, q_rope, latent, rope_t, docs, uv_weight, weight)


def experts_kernel(
    rows_ref,
    state_ref,
    scale_ref,
    gate_hbm,
    up_hbm,
    down_hbm,
    out_ref,
    hist_ref,
    gate_ref,
    up_ref,
    down_ref,
    near,
    weigh,
    slots,
    inbox,
    kept,
    to_mate,
    from_mate,
    back,
    returned,
    to_y,
    from_y,
    own,
    to_z,
    from_z,
    hist_out,
    hist_in,
    load_sem,
    z_send,
    z_recv,
    y_send,
    y_recv,
    q_send,
    q_recv,
    m_send,
    m_recv,
    o_send,
    o_recv,
    b_send,
    b_recv,
    ys_send,
    ys_recv,
    zs_send,
    zs_recv,
    h_send,
    h_recv,
):
    width = state_ref.shape[1]
    sent = width + 2 * N_EXPERTS
    half_rows, half_slots = NZ * TOK, NQ * NZ * CAP
    piece = NZ * CAP
    ctx, me = lax.axis_index("ctx"), lax.axis_index("exp")
    y_lo, core = ctx // 2, ctx % 2
    z, q = me // NQ, me % NQ

    def z_peer(z_at):
        return {"ctx": ctx, "exp": z_at * NQ + q}

    def q_peer(q_at):
        return {"ctx": ctx, "exp": z * NQ + q_at}

    y_peer = {"ctx": (1 - y_lo) * 2 + core, "exp": me}
    mate = {"ctx": y_lo * 2 + 1 - core, "exp": me}

    def c_peer(j):
        return {"ctx": (ctx + j) % N_CTX, "exp": me}

    loads = [
        pltpu.make_async_copy(src, dst, load_sem.at[i])
        for i, (src, dst) in enumerate(
            ((gate_hbm, gate_ref), (up_hbm, up_ref), (down_hbm, down_ref))
        )
    ]
    for load in loads:
        load.start()
    greet(
        [z_peer((z + j) % NZ) for j in range(1, NZ)]
        + [q_peer((q + j) % NQ) for j in range(1, NQ)]
        + [c_peer(j) for j in range(1, N_CTX)]
    )
    pending = []

    order = (4, 3, 5, 2, 6, 1, 7)
    near[y_lo, z] = rows_ref[...]
    hops = NZ // 2
    middle = rows_ref.shape[1] // 2
    onward = (z_peer((z + 1) % NZ), z_peer((z + NZ - 1) % NZ))
    ring = {}

    def pass_on(way, step, src, dst):
        ring[way, step] = remote(
            src, dst, z_send.at[way, step], z_recv.at[way, step], onward[way]
        )
        pending.append(ring[way, step])

    crossings = []

    def cross(src, dst):
        n = len(crossings)
        crossings.append(remote(src, dst, y_send.at[n], y_recv.at[n], y_peer))

    for way in range(2):
        pass_on(way, 0, rows_ref, near.at[y_lo, z])
    cross(rows_ref, near.at[y_lo, z])
    for step in range(1, hops):
        for way in range(2):
            z_from = (z + (NZ - step if way == 0 else step)) % NZ
            ring[way, step - 1].wait_recv()
            held = near.at[y_lo, z_from]
            if step < hops - 1:
                pass_on(way, step, held, held)
            else:
                side = pl.ds(way * middle, middle)
                part = near.at[y_lo, z_from, :, side]
                pass_on(way, step, part, part)
            cross(held, held)
    for way in range(2):
        ring[way, hops - 1].wait_recv()
    held = near.at[y_lo, (z + hops) % NZ]
    cross(held, held)
    pending += crossings

    lane = lax.broadcasted_iota(jnp.int32, (2 * N_EXPERTS, half_slots), 0)
    wanted = z * NQ + (
        lax.broadcasted_iota(jnp.int32, (2 * N_EXPERTS, half_slots), 1) // piece
    )
    pick_level, pick_rank = small(lane == wanted), small(lane == wanted + N_EXPERTS)
    row = lax.broadcasted_iota(jnp.int32, (half_rows, half_slots), 0)
    col = lax.broadcasted_iota(jnp.int32, (half_rows, half_slots), 1)
    same_source = (row // TOK) == ((col // CAP) % NZ)
    slot_rank = (col % CAP).astype(jnp.float32)

    q_order = (1, 2, 3, 4, 5, 6, 7)
    slot_flight = {}
    for half in range(2):
        if half == 1:
            for copy in crossings:
                copy.wait_recv()
        y_at = y_lo if half == 0 else 1 - y_lo
        held = (
            near[y_at]
            .astype(jnp.float32)
            .reshape(half_rows, sent + 2 * N_EXPERTS)
            .astype(jnp.bfloat16)
        )
        route = held[:, sent:]
        level, rank = mm(route, pick_level), mm(route, pick_rank)
        chosen = (level > 0.5) & (rank == slot_rank) & same_source
        weigh[half] = jnp.where(chosen, level, 0.0).astype(jnp.bfloat16)
        picked = mm_t(small(chosen), held[:, :sent])
        slots[half] = picked.astype(jnp.bfloat16).reshape(NQ, piece, sent)
        for j in q_order:
            p = (q + j) % NQ
            slot_flight[half, j] = remote(
                slots.at[half, p],
                inbox.at[0, half, q],
                q_send.at[half, j],
                q_recv.at[half, j],
                q_peer(p),
            )
        inbox[0, half, q] = slots[half, q]
    pending += slot_flight.values()

    mate_flight = []
    for half in range(2):
        for j in (0,) + q_order:
            q_from = (q + NQ - j) % NQ
            if j:
                slot_flight[half, j].wait_recv()
            mate_flight.append(
                remote(
                    inbox.at[0, half, q_from],
                    inbox.at[1, half, q_from],
                    m_send.at[half, j],
                    m_recv.at[half, j],
                    mate,
                )
            )
    pending += mate_flight

    bin_lane = lax.broadcasted_iota(jnp.int32, (2 * half_slots, 2 * N_EXPERTS), 1)
    bins_at = bin_lane.astype(jnp.float32)

    def run_block(which):
        block = inbox[which].reshape(2 * half_slots, sent)
        x = block[:, :width]
        gate_part, up_part = mm(x, gate_ref[...]), mm(x, up_ref[...])
        activation = gate_part / (1.0 + jnp.exp(-gate_part)) * up_part
        energy = jnp.sum(activation * activation, axis=1, keepdims=True) * (1.0 / HID)
        tail = block[:, width:].astype(jnp.float32)
        high = jnp.sum(jnp.where(bin_lane == me, tail, 0.0), axis=1, keepdims=True)
        low = jnp.sum(
            jnp.where(bin_lane == me + N_EXPERTS, tail, 0.0), axis=1, keepdims=True
        )
        at_high = jnp.where(high == bins_at, energy, 0.0)
        at_low = small(low == bins_at)
        first, second, third = split3(at_high)
        hist = mm_t(first, at_low) + mm_t(second, at_low) + mm_t(third, at_low)
        return activation.astype(jnp.bfloat16), hist

    for load in loads:
        load.wait()
    hidden, hist = run_block(0)
    kept[...] = mm(hidden, down_ref[...])
    for copy in mate_flight:
        copy.wait_recv()
    hidden, more = run_block(1)
    to_mate[...] = (
        mm(hidden, down_ref[...]).astype(jnp.bfloat16).reshape(to_mate.shape)
    )
    mate_out = {}
    for half in (1, 0):
        mate_out[half] = remote(
            to_mate.at[half], from_mate.at[half], o_send.at[half], o_recv.at[half], mate
        )
    pending += mate_out.values()

    hist_out[...] = (hist + more)[: N_CTX * 8].reshape(N_CTX, 8, 2 * N_EXPERTS)
    hist_flight = [
        remote(
            hist_out.at[(ctx + j) % N_CTX],
            hist_in.at[j - 1],
            h_send.at[j - 1],
            h_recv.at[j - 1],
            c_peer(j),
        )
        for j in range(1, N_CTX)
    ]
    pending += hist_flight

    back_flight = {}
    for half in (1, 0):
        mate_out[half].wait_recv()
        total = kept[half * half_slots : (half + 1) * half_slots] + from_mate[
            half
        ].reshape(half_slots, width).astype(jnp.float32)
        back[half] = total.astype(jnp.bfloat16).reshape(NQ, piece, width)
        for j in q_order:
            p = (q + j) % NQ
            back_flight[half, j] = remote(
                back.at[half, p],
                returned.at[half, q],
                b_send.at[half, j],
                b_recv.at[half, j],
                q_peer(p),
            )
        returned[half, q] = back[half, q]
    pending += back_flight.values()

    def mixed(half):
        for j in q_order:
            back_flight[half, j].wait_recv()
        return mm(weigh[half], returned[half].reshape(half_slots, width))

    to_y[...] = mixed(1).reshape(NZ, TOK, width).astype(jnp.bfloat16)
    y_flight = {}
    for j in order + (0,):
        z_to = (z + j) % NZ
        y_flight[j] = remote(
            to_y.at[z_to], from_y.at[z_to], ys_send.at[j], ys_recv.at[j], y_peer
        )
    pending += y_flight.values()
    own[...] = mixed(0).reshape(NZ, TOK, width)
    z_flight = []
    for j in order + (0,):
        z_to = (z + j) % NZ
        y_flight[j].wait_recv()
        to_z[z_to] = (own[z_to] + from_y[z_to].astype(jnp.float32)).astype(jnp.bfloat16)
        if j:
            z_flight.append(
                remote(
                    to_z.at[z_to],
                    from_z.at[j - 1],
                    zs_send.at[j - 1],
                    zs_recv.at[j - 1],
                    z_peer(z_to),
                )
            )
    pending += z_flight
    for copy in hist_flight:
        copy.wait_recv()
    hist = hist_out[ctx]
    for j in range(N_CTX - 1):
        hist = hist + hist_in[j]
    hist_ref[...] = hist
    for copy in z_flight:
        copy.wait_recv()
    total = to_z[z].astype(jnp.float32)
    for j in range(NZ - 1):
        total = total + from_z[j].astype(jnp.float32)
    out_ref[...] = (state_ref[...] + total * scale_ref[:, :1]).astype(jnp.bfloat16)
    for copy in pending:
        copy.wait_send()


def run_experts(rows, state, scale, gate, up, down):
    width = state.shape[1]
    sent = width + 2 * N_EXPERTS
    half_slots, piece = NQ * NZ * CAP, NZ * CAP
    bf16, f32 = jnp.bfloat16, jnp.float32
    dma = pltpu.SemaphoreType.DMA
    vmem = pl.BlockSpec(memory_space=pltpu.VMEM)
    hbm = pl.BlockSpec(memory_space=pltpu.HBM)
    return pl.pallas_call(
        experts_kernel,
        out_shape=(
            jax.ShapeDtypeStruct((TOK, width), bf16),
            jax.ShapeDtypeStruct((8, 2 * N_EXPERTS), f32),
        ),
        in_specs=[vmem, vmem, vmem, hbm, hbm, hbm],
        out_specs=(vmem, vmem),
        scratch_shapes=[
            pltpu.VMEM(gate.shape, bf16),
            pltpu.VMEM(up.shape, bf16),
            pltpu.VMEM(down.shape, bf16),
            pltpu.VMEM((2, NZ, TOK, rows.shape[1]), bf16),
            pltpu.VMEM((2, NZ * TOK, half_slots), bf16),
            pltpu.VMEM((2, NQ, piece, sent), bf16),
            pltpu.VMEM((2, 2, NQ, piece, sent), bf16),
            pltpu.VMEM((2 * half_slots, width), f32),
            pltpu.VMEM((2, NQ, piece, width), bf16),
            pltpu.VMEM((2, NQ, piece, width), bf16),
            pltpu.VMEM((2, NQ, piece, width), bf16),
            pltpu.VMEM((2, NQ, piece, width), bf16),
            pltpu.VMEM((NZ, TOK, width), bf16),
            pltpu.VMEM((NZ, TOK, width), bf16),
            pltpu.VMEM((NZ, TOK, width), f32),
            pltpu.VMEM((NZ, TOK, width), bf16),
            pltpu.VMEM((NZ - 1, TOK, width), bf16),
            pltpu.VMEM((N_CTX, 8, 2 * N_EXPERTS), f32),
            pltpu.VMEM((N_CTX - 1, 8, 2 * N_EXPERTS), f32),
            dma((3,)),
            dma((2, NZ // 2)),
            dma((2, NZ // 2)),
            dma((NZ,)),
            dma((NZ,)),
            dma((2, NQ)),
            dma((2, NQ)),
            dma((2, NQ)),
            dma((2, NQ)),
            dma((2,)),
            dma((2,)),
            dma((2, NQ)),
            dma((2, NQ)),
            dma((NZ,)),
            dma((NZ,)),
            dma((NZ - 1,)),
            dma((NZ - 1,)),
            dma((N_CTX - 1,)),
            dma((N_CTX - 1,)),
        ],
        compiler_params=pltpu.CompilerParams(
            collective_id=1, has_side_effects=True, vmem_limit_bytes=60 << 20
        ),
        name="experts",
    )(rows, state, scale, gate, up, down)


def route_lanes(expert_ids, gate_levels, bin_ids):
    onehot = expert_ids[:, :, None] == jnp.arange(N_EXPERTS, dtype=jnp.int32)

    def spread(v):
        return jnp.sum(jnp.where(onehot, v[:, :, None], 0), axis=1)

    named = jnp.sum(onehot.astype(jnp.int32), axis=1)
    earlier = jnp.arange(TOK)[:, None] > jnp.arange(TOK)[None, :]
    rank = jnp.sum(jnp.where(earlier[:, :, None], named[None, :, :], 0), axis=1)
    lanes = (spread(bin_ids // 64), spread(bin_ids % 64), spread(gate_levels), rank)
    return jnp.concatenate(lanes, axis=1).astype(jnp.bfloat16)


def on_device(
    residual_in,
    norm_gain,
    q_nope,
    q_rope,
    latent,
    k_rope,
    doc_ids,
    uv_weight,
    out_weight,
    expert_ids,
    gate_levels,
    bin_ids,
    gate_weight,
    up_weight,
    down_weight,
):
    block_len, head_count, _ = q_nope.shape
    attended = attend_sum(
        q_nope.reshape(block_len, head_count * q_nope.shape[2]),
        q_rope,
        latent,
        k_rope.T,
        doc_ids.reshape(1, block_len),
        uv_weight,
        out_weight,
    )
    stream_state = residual_in.astype(jnp.float32) + attended
    normed = (
        stream_state
        * lax.rsqrt(jnp.mean(stream_state * stream_state, axis=1, keepdims=True) + norm_eps)
        * norm_gain
    ).astype(jnp.bfloat16)
    rows = jnp.concatenate(
        (normed, route_lanes(expert_ids, gate_levels, bin_ids)), axis=1
    )
    scale = 1.0 / jnp.sum(gate_levels.astype(jnp.float32), axis=1, keepdims=True)
    layer_out, hist = run_experts(
        rows,
        stream_state,
        jnp.broadcast_to(scale, (TOK, 128)),
        gate_weight[0],
        up_weight[0],
        down_weight[0],
    )
    histogram = hist[:, : NBINS // 32].reshape(1, NBINS // N_CTX)
    return (layer_out, histogram)


def solution(mesh):
    return jax.shard_map(
        on_device,
        mesh=mesh,
        in_specs=(
            P(("ctx", "exp"), None),
            P(),
            P("ctx", "exp", None),
            P("ctx", "exp"),
            P("ctx", None),
            P("ctx", None),
            P("ctx"),
            P("exp", None, None),
            P("exp", None),
            P(("ctx", "exp"), None),
            P(("ctx", "exp"), None),
            P(("ctx", "exp"), None),
            P("exp", None, "ctx"),
            P("exp", None, "ctx"),
            P("exp", "ctx", None),
        ),
        out_specs=(P(("ctx", "exp"), None), P("exp", "ctx")),
        check_vma=False,
    )
```

```python
import functools
import math

import jax
import jax.numpy as jnp
from jax import lax
from jax.experimental import pallas as pl
from jax.experimental.pallas import tpu as pltpu
from jax.sharding import PartitionSpec as P

HID = 1024
NBINS = 2048


exponent_scale = 192.0 ** (-0.5) * math.log2(math.e)
norm_eps = 1e-06
masked_score = -1e30

NZ, NX, NY = 8, 4, 2
NQ = NX * NY
NR = NZ * NY
TOK = 8
CAP = 2
N_CTX = 4
N_EXPERTS = 64
ROPE = 64
VDIM = 128
DOC_ROWS = 16
KEY_PIECES = 2
SUBS = 2
MESH = pl.DeviceIdType.MESH


def remote(src, dst, send_sem, recv_sem, target):
    copy = pltpu.make_async_remote_copy(
        src_ref=src,
        dst_ref=dst,
        send_sem=send_sem,
        recv_sem=recv_sem,
        device_id=target,
        device_id_type=MESH,
    )
    copy.start()
    return copy


def greet(targets):
    barrier = pltpu.get_barrier_semaphore()
    for target in targets:
        pl.semaphore_signal(barrier, inc=1, device_id=target, device_id_type=MESH)
    pl.semaphore_wait(barrier, len(targets))


def small(cond):
    return cond.astype(jnp.float32).astype(jnp.bfloat16)


def split3(v):
    first = v.astype(jnp.bfloat16)
    rest = v - first.astype(jnp.float32)
    second = rest.astype(jnp.bfloat16)
    third = (rest - second.astype(jnp.float32)).astype(jnp.bfloat16)
    return first, second, third


def mm(a, b):
    return jnp.dot(a, b, preferred_element_type=jnp.float32)


def mm_t(a, b):
    return lax.dot_general(
        a, b, (((0,), (0,)), ((), ())), preferred_element_type=jnp.float32
    )


def attend_sum_kernel(
    part_a,
    query_ref,
    query_rope_ref,
    latent_ref,
    rope_ref,
    doc_ref,
    uv_hbm,
    weight_hbm,
    out_ref,
    uv_ref,
    weight_ref,
    tail_ref,
    keys,
    tails,
    top,
    denominator,
    accum,
    values_ref,
    a_first,
    a_slots,
    b_first,
    b_slots,
    a_push,
    a_got,
    b_mid,
    b_other,
    b_push,
    b_got,
    k_send_sem,
    k_recv_sem,
    t_send_sem,
    t_recv_sem,
    a_send_sem,
    a_recv_sem,
    b_send_sem,
    b_recv_sem,
    ap_send_sem,
    ap_recv_sem,
    bp_send_sem,
    bp_recv_sem,
    bc_send_sem,
    bc_recv_sem,
    load_sem,
):
    loads = [
        pltpu.make_async_copy(uv_hbm, uv_ref, load_sem.at[0]),
        pltpu.make_async_copy(weight_hbm, weight_ref, load_sem.at[1]),
    ]
    for load in loads:
        load.start()
    width = weight_ref.shape[1]
    wide_a, wide_b = part_a // (2 * SUBS), (width - part_a) // (2 * SUBS)
    me = lax.axis_index("exp")
    z, x, y = me // NQ, (me // NY) % NX, me % NY
    q = x * NY + y

    def at(z_at, x_at, y_at):
        return {"exp": (z_at * NX + x_at) * NY + y_at}

    q_peers = [(q + j) % NQ for j in range(NQ)]
    z_peers = [(z + j) % NZ for j in range(NZ)]
    y_other = at(z, x, 1 - y)
    z_next = [at((z + 1) % NZ, x, y), at((z + NZ - 1) % NZ, x, y)]
    x_next = [at(z, (x + 1) % NX, y), at(z, (x + NX - 1) % NX, y)]
    ctx = lax.axis_index("ctx")
    y_lo, core = ctx // 2, ctx % 2
    mate = {"ctx": y_lo * 2 + 1 - core, "exp": me}
    across = {"ctx": (1 - y_lo) * 2 + core, "exp": me}
    greet(
        [at(z, p // NY, p % NY) for p in q_peers[1:]]
        + [at(p, x, y) for p in z_peers[1:]]
        + [mate, across]
    )

    block_len, lat = latent_ref.shape
    piece = block_len // KEY_PIECES
    for i in range(KEY_PIECES):
        tail_ref[i, :ROPE] = rope_ref[:, i * piece : (i + 1) * piece]
        tail_ref[i, ROPE:] = jnp.broadcast_to(
            doc_ref[:, i * piece : (i + 1) * piece].astype(jnp.float32),
            (DOC_ROWS, piece),
        ).astype(jnp.bfloat16)

    class KeyCopy:
        def __init__(self, back, i, forward, target):
            self.copies = [
                pltpu.make_async_remote_copy(
                    src_ref=src,
                    dst_ref=dst.at[i, back],
                    send_sem=send_sem.at[back, i],
                    recv_sem=recv_sem.at[back, i],
                    device_id=target,
                    device_id_type=MESH,
                )
                for src, dst, send_sem, recv_sem in (
                    (
                        keys.at[i, 1]
                        if forward
                        else latent_ref.at[i * piece : (i + 1) * piece],
                        keys,
                        k_send_sem,
                        k_recv_sem,
                    ),
                    (
                        tails.at[i, 1] if forward else tail_ref.at[i],
                        tails,
                        t_send_sem,
                        t_recv_sem,
                    ),
                )
            ]

        def start(self):
            for copy in self.copies:
                copy.start()

        def wait_recv(self):
            for copy in self.copies:
                copy.wait_recv()

        def wait_send(self):
            for copy in self.copies:
                copy.wait_send()

    for i in range(KEY_PIECES):

        @pl.when(y_lo == 0)
        def _():
            KeyCopy(1, i, False, across).start()

    for i in range(KEY_PIECES):

        @pl.when(core == 0)
        def _():
            KeyCopy(0, i, False, mate).start()

    def nt(a, b):
        return lax.dot_general(
            a, b, (((1,), (1,)), ((), ())), preferred_element_type=jnp.float32
        )

    heads = uv_ref.shape[0]
    doc_pick = small(lax.broadcasted_iota(jnp.int32, (DOC_ROWS, 128), 0) == 0)
    query_docs = jnp.concatenate(
        [mm_t(tail_ref[i, ROPE:], doc_pick)[:, :1] for i in range(KEY_PIECES)], axis=0
    )

    def fold(block, tail, offset=None):
        first = offset == 0
        allowed = query_docs == tail[ROPE : ROPE + 1].astype(jnp.float32)
        if offset is not None:
            shape = (block_len, block.shape[0])
            query_at = lax.broadcasted_iota(jnp.int32, shape, 0)
            key_at = lax.broadcasted_iota(jnp.int32, shape, 1) + offset
            allowed = allowed & (key_at <= query_at)
        for head in range(heads):
            nope = query_ref[:, head * lat : (head + 1) * lat]
            rope = query_rope_ref[:, head * ROPE : (head + 1) * ROPE]
            raw = nt(nope, block) + mm(rope, tail[:ROPE])
            scores = jnp.where(allowed, raw, masked_score)
            peak = jnp.max(scores, axis=1, keepdims=True)
            if not first:
                old = top[head][:, :1]
                peak = jnp.maximum(old, peak)
                fade = jnp.exp2((old - peak) * exponent_scale)
            probs = jnp.exp2((scores - peak) * exponent_scale)
            mass = jnp.sum(probs, axis=1, keepdims=True)
            mixed = mm(probs.astype(jnp.bfloat16), block)
            if not first:
                mass = mass + denominator[head][:, :1] * fade
                mixed = mixed + accum[head] * fade
            top[head] = jnp.broadcast_to(peak, top.shape[1:])
            denominator[head] = jnp.broadcast_to(mass, denominator.shape[1:])
            accum[head] = mixed

    own_tail = jnp.concatenate([tail_ref[i] for i in range(KEY_PIECES)], axis=1)
    fold(latent_ref[...], own_tail, 0)

    def fold_pair(blocks):
        block = jnp.concatenate([keys[i, back] for i, back in blocks], axis=0)
        tail = jnp.concatenate([tails[i, back] for i, back in blocks], axis=1)
        fold(block, tail)

    def near_arrived(i):
        KeyCopy(0, i, False, mate).wait_recv()

    def far_arrived(i):
        KeyCopy(1, i, False, across).wait_recv()

    @pl.when(ctx == 1)
    def _():
        near_arrived(0)
        near_arrived(1)
        fold_pair(((0, 0), (1, 0)))

    @pl.when(ctx == 2)
    def _():
        for i in range(KEY_PIECES):
            far_arrived(i)
            near_arrived(i)
            fold_pair(((i, 0), (i, 1)))

    @pl.when(ctx == 3)
    def _():
        far_arrived(0)
        KeyCopy(0, 0, True, mate).start()
        near_arrived(0)
        near_arrived(1)
        fold_pair(((0, 0), (1, 0), (0, 1)))
        far_arrived(1)
        KeyCopy(0, 1, True, mate).start()
        fold(keys[1, 1], tails[1, 1])

    for load in loads:
        load.wait()
    for head in range(heads):
        context = (accum[head] / denominator[head][:, :1]).astype(jnp.bfloat16)
        values_ref[:, :, :, head * VDIM : (head + 1) * VDIM] = (
            mm(context, uv_ref[head])
            .astype(jnp.bfloat16)
            .reshape(NZ, NX, NY * TOK, VDIM)
        )

    def a_own(way, sub, chunk):
        rows = values_ref[chunk].reshape(NX * NY * TOK, values_ref.shape[3])
        start = (way * SUBS + sub) * wide_a
        return mm(rows, weight_ref[:, start : start + wide_a])

    def b_own(way, sub, chunk):
        rows = values_ref[:, chunk].reshape(NZ * NY * TOK, values_ref.shape[3])
        start = part_a + (way * SUBS + sub) * wide_b
        return mm(rows, weight_ref[:, start : start + wide_b])

    a_flight, b_flight, pushes = {}, {}, []

    def ring_step(step, here, count, own_of, first, slots, sems, onward, flight):
        for sub in range(SUBS):
            for way in range(2):
                sign = -1 if way == 0 else 1
                own = own_of(way, sub, (here + sign * (1 + step) + 2 * count) % count)
                if step == 0:
                    src = first.at[way, sub]
                    first[way, sub] = own.astype(jnp.bfloat16)
                else:
                    src = slots.at[way, sub, step - 1]
                    flight[way, sub, step - 1].wait_recv()
                    slots[way, sub, step - 1] = (
                        slots[way, sub, step - 1].astype(jnp.float32) + own
                    ).astype(jnp.bfloat16)
                flight[way, sub, step] = remote(
                    src,
                    slots.at[way, sub, step],
                    sems[0].at[way, sub, step],
                    sems[1].at[way, sub, step],
                    onward[way],
                )

    def a_step(step):
        ring_step(
            step, z, NZ, a_own, a_first, a_slots,
            (a_send_sem, a_recv_sem), z_next, a_flight,
        )

    def b_step(step):
        ring_step(
            step, x, NX, b_own, b_first, b_slots,
            (b_send_sem, b_recv_sem), x_next, b_flight,
        )

    def a_push_out():
        for sub in range(SUBS):
            for way in range(2):
                own = a_own(way, sub, z)
                a_flight[way, sub, NZ - 2].wait_recv()
                own = own + a_slots[way, sub, NZ - 2].astype(jnp.float32)
                start = (way * SUBS + sub) * wide_a
                a_push[:, :, start : start + wide_a] = own.reshape(
                    NQ, TOK, wide_a
                ).astype(jnp.bfloat16)
        for j in range(1, NQ):
            p = q_peers[j]
            pushes.append(
                remote(
                    a_push.at[p],
                    a_got.at[j - 1],
                    ap_send_sem.at[j - 1],
                    ap_recv_sem.at[j - 1],
                    at(z, p // NY, p % NY),
                )
            )

    b_cross = []

    def b_cross_out():
        for sub in range(SUBS):
            for way in range(2):
                k = way * SUBS + sub
                own = b_own(way, sub, x)
                b_flight[way, sub, NX - 2].wait_recv()
                own = own + b_slots[way, sub, NX - 2].astype(jnp.float32)
                own = own.reshape(NZ, NY, TOK, wide_b)
                for y_at in range(NY):
                    b_mid[k, y_at] = own[:, y_at].astype(jnp.bfloat16)
                b_cross.append(
                    (
                        k,
                        remote(
                            b_mid.at[k, 1 - y],
                            b_other.at[k],
                            bc_send_sem.at[k],
                            bc_recv_sem.at[k],
                            y_other,
                        ),
                    )
                )

    def b_push_out():
        for k, copy in b_cross:
            copy.wait_recv()
            own = b_mid[k, y].astype(jnp.float32) + b_other[k].astype(jnp.float32)
            b_push[:, :, k * wide_b : (k + 1) * wide_b] = own.astype(jnp.bfloat16)
        for j in (4, 3, 5, 2, 6, 1, 7):
            p = z_peers[j]
            pushes.append(
                remote(
                    b_push.at[p],
                    b_got.at[j - 1],
                    bp_send_sem.at[j - 1],
                    bp_recv_sem.at[j - 1],
                    at(p, x, y),
                )
            )

    a_step(0)
    b_step(0)
    a_step(1)
    a_step(2)
    b_step(1)
    a_step(3)
    b_step(2)
    a_step(4)
    b_cross_out()
    a_step(5)
    b_push_out()
    a_step(6)
    a_push_out()
    for copy in pushes:
        copy.wait_recv()
    total = b_push[z].astype(jnp.float32)
    for j in range(NZ - 1):
        total = total + b_got[j].astype(jnp.float32)
    out_ref[:, part_a:] = total
    total = a_push[q].astype(jnp.float32)
    for j in range(NQ - 1):
        total = total + a_got[j].astype(jnp.float32)
    out_ref[:, :part_a] = total
    crossed = [copy for _, copy in b_cross]
    for copy in [*a_flight.values(), *b_flight.values(), *crossed, *pushes]:
        copy.wait_send()
    for i in range(KEY_PIECES):

        @pl.when(y_lo == 0)
        def _():
            KeyCopy(1, i, False, across).wait_send()

        @pl.when((core == 0) | (y_lo == 1))
        def _():
            KeyCopy(0, i, False, mate).wait_send()


def attend_sum(q_nope, q_rope, latent, rope_t, docs, uv_weight, weight, part_a=2048):
    heads, lat = uv_weight.shape[:2]
    rows = latent.shape[0]
    width = weight.shape[1]
    part_b = width - part_a
    wide_a, wide_b = part_a // (2 * SUBS), part_b // (2 * SUBS)
    bf16 = jnp.bfloat16
    dma = pltpu.SemaphoreType.DMA
    return pl.pallas_call(
        functools.partial(attend_sum_kernel, part_a),
        out_shape=jax.ShapeDtypeStruct((TOK, width), jnp.float32),
        in_specs=[pl.BlockSpec(memory_space=pltpu.VMEM)] * 5
        + [pl.BlockSpec(memory_space=pltpu.HBM)] * 2,
        out_specs=pl.BlockSpec(memory_space=pltpu.VMEM),
        scratch_shapes=[
            pltpu.VMEM(uv_weight.shape, bf16),
            pltpu.VMEM(weight.shape, bf16),
            pltpu.VMEM((KEY_PIECES, ROPE + DOC_ROWS, rows // KEY_PIECES), bf16),
            pltpu.VMEM((KEY_PIECES, 2, rows // KEY_PIECES, lat), bf16),
            pltpu.VMEM((KEY_PIECES, 2, ROPE + DOC_ROWS, rows // KEY_PIECES), bf16),
            pltpu.VMEM((heads, rows, 128), jnp.float32),
            pltpu.VMEM((heads, rows, 128), jnp.float32),
            pltpu.VMEM((heads, rows, lat), jnp.float32),
            pltpu.VMEM((NZ, NX, NY * TOK, heads * VDIM), bf16),
            pltpu.VMEM((2, SUBS, NQ * TOK, wide_a), bf16),
            pltpu.VMEM((2, SUBS, NZ - 1, NQ * TOK, wide_a), bf16),
            pltpu.VMEM((2, SUBS, NR * TOK, wide_b), bf16),
            pltpu.VMEM((2, SUBS, NX - 1, NR * TOK, wide_b), bf16),
            pltpu.VMEM((NQ, TOK, part_a), bf16),
            pltpu.VMEM((NQ - 1, TOK, part_a), bf16),
            pltpu.VMEM((2 * SUBS, NY, NZ, TOK, wide_b), bf16),
            pltpu.VMEM((2 * SUBS, NZ, TOK, wide_b), bf16),
            pltpu.VMEM((NZ, TOK, part_b), bf16),
            pltpu.VMEM((NZ - 1, TOK, part_b), bf16),
            dma((2, KEY_PIECES)),
            dma((2, KEY_PIECES)),
            dma((2, KEY_PIECES)),
            dma((2, KEY_PIECES)),
            dma((2, SUBS, NZ - 1)),
            dma((2, SUBS, NZ - 1)),
            dma((2, SUBS, NX - 1)),
            dma((2, SUBS, NX - 1)),
            dma((NQ - 1,)),
            dma((NQ - 1,)),
            dma((NZ - 1,)),
            dma((NZ - 1,)),
            dma((2 * SUBS,)),
            dma((2 * SUBS,)),
            dma((2,)),
        ],
        compiler_params=pltpu.CompilerParams(
            collective_id=0, has_side_effects=True, vmem_limit_bytes=60 << 20
        ),
        name="attend_sum",
    )(q_nope, q_rope, latent, rope_t, docs, uv_weight, weight)


def experts_kernel(
    rows_ref,
    gate_hbm,
    up_hbm,
    down_hbm,
    out_ref,
    hist_ref,
    gate_ref,
    up_ref,
    down_ref,
    near,
    weigh,
    slots,
    inbox,
    kept,
    to_mate,
    from_mate,
    back,
    returned,
    to_y,
    from_y,
    own,
    to_z,
    from_z,
    hist_out,
    hist_in,
    load_sem,
    z_send,
    z_recv,
    y_send,
    y_recv,
    q_send,
    q_recv,
    m_send,
    m_recv,
    o_send,
    o_recv,
    b_send,
    b_recv,
    ys_send,
    ys_recv,
    zs_send,
    zs_recv,
    h_send,
    h_recv,
):
    width = down_hbm.shape[1]
    sent = width + 2 * N_EXPERTS
    half_rows, half_slots = NZ * TOK, NQ * NZ * CAP
    piece = NZ * CAP
    ctx, me = lax.axis_index("ctx"), lax.axis_index("exp")
    y_lo, core = ctx // 2, ctx % 2
    z, q = me // NQ, me % NQ

    def z_peer(z_at):
        return {"ctx": ctx, "exp": z_at * NQ + q}

    def q_peer(q_at):
        return {"ctx": ctx, "exp": z * NQ + q_at}

    y_peer = {"ctx": (1 - y_lo) * 2 + core, "exp": me}
    mate = {"ctx": y_lo * 2 + 1 - core, "exp": me}

    def c_peer(j):
        return {"ctx": (ctx + j) % N_CTX, "exp": me}

    loads = [
        pltpu.make_async_copy(src, dst, load_sem.at[i])
        for i, (src, dst) in enumerate(
            ((gate_hbm, gate_ref), (up_hbm, up_ref), (down_hbm, down_ref))
        )
    ]
    for load in loads:
        load.start()
    greet(
        [z_peer((z + j) % NZ) for j in range(1, NZ)]
        + [q_peer((q + j) % NQ) for j in range(1, NQ)]
        + [c_peer(j) for j in range(1, N_CTX)]
    )
    pending = []

    order = (4, 3, 5, 2, 6, 1, 7)
    near[y_lo, z] = rows_ref[...]
    hops = NZ // 2
    middle = rows_ref.shape[1] // 2
    onward = (z_peer((z + 1) % NZ), z_peer((z + NZ - 1) % NZ))
    ring = {}

    def pass_on(way, step, src, dst):
        ring[way, step] = remote(
            src, dst, z_send.at[way, step], z_recv.at[way, step], onward[way]
        )
        pending.append(ring[way, step])

    crossings = []

    def cross(src, dst):
        n = len(crossings)
        crossings.append(remote(src, dst, y_send.at[n], y_recv.at[n], y_peer))

    for way in range(2):
        pass_on(way, 0, rows_ref, near.at[y_lo, z])
    cross(rows_ref, near.at[y_lo, z])
    for step in range(1, hops):
        for way in range(2):
            z_from = (z + (NZ - step if way == 0 else step)) % NZ
            ring[way, step - 1].wait_recv()
            held = near.at[y_lo, z_from]
            if step < hops - 1:
                pass_on(way, step, held, held)
            else:
                side = pl.ds(way * middle, middle)
                part = near.at[y_lo, z_from, :, side]
                pass_on(way, step, part, part)
            cross(held, held)
    for way in range(2):
        ring[way, hops - 1].wait_recv()
    held = near.at[y_lo, (z + hops) % NZ]
    cross(held, held)
    pending += crossings

    lane = lax.broadcasted_iota(jnp.int32, (2 * N_EXPERTS, half_slots), 0)
    wanted = z * NQ + (
        lax.broadcasted_iota(jnp.int32, (2 * N_EXPERTS, half_slots), 1) // piece
    )
    pick_level, pick_rank = small(lane == wanted), small(lane == wanted + N_EXPERTS)
    row = lax.broadcasted_iota(jnp.int32, (half_rows, half_slots), 0)
    col = lax.broadcasted_iota(jnp.int32, (half_rows, half_slots), 1)
    same_source = (row // TOK) == ((col // CAP) % NZ)
    slot_rank = (col % CAP).astype(jnp.float32)

    q_order = (1, 2, 3, 4, 5, 6, 7)
    slot_flight = {}
    for half in range(2):
        if half == 1:
            for copy in crossings:
                copy.wait_recv()
        y_at = y_lo if half == 0 else 1 - y_lo
        held = (
            near[y_at]
            .astype(jnp.float32)
            .reshape(half_rows, sent + 2 * N_EXPERTS)
            .astype(jnp.bfloat16)
        )
        route = held[:, sent:]
        level, rank = mm(route, pick_level), mm(route, pick_rank)
        chosen = (level > 0.5) & (rank == slot_rank) & same_source
        weigh[half] = jnp.where(chosen, level, 0.0).astype(jnp.bfloat16)
        picked = mm_t(small(chosen), held[:, :sent])
        slots[half] = picked.astype(jnp.bfloat16).reshape(NQ, piece, sent)
        for j in q_order:
            p = (q + j) % NQ
            slot_flight[half, j] = remote(
                slots.at[half, p],
                inbox.at[0, half, q],
                q_send.at[half, j],
                q_recv.at[half, j],
                q_peer(p),
            )
        inbox[0, half, q] = slots[half, q]
    pending += slot_flight.values()

    mate_flight = []
    for half in range(2):
        for j in (0,) + q_order:
            q_from = (q + NQ - j) % NQ
            if j:
                slot_flight[half, j].wait_recv()
            mate_flight.append(
                remote(
                    inbox.at[0, half, q_from],
                    inbox.at[1, half, q_from],
                    m_send.at[half, j],
                    m_recv.at[half, j],
                    mate,
                )
            )
    pending += mate_flight

    bin_lane = lax.broadcasted_iota(jnp.int32, (2 * half_slots, 2 * N_EXPERTS), 1)
    bins_at = bin_lane.astype(jnp.float32)

    def run_block(which):
        block = inbox[which].reshape(2 * half_slots, sent)
        x = block[:, :width]
        gate_part, up_part = mm(x, gate_ref[...]), mm(x, up_ref[...])
        activation = gate_part / (1.0 + jnp.exp(-gate_part)) * up_part
        energy = jnp.sum(activation * activation, axis=1, keepdims=True) * (1.0 / HID)
        tail = block[:, width:].astype(jnp.float32)
        high = jnp.sum(jnp.where(bin_lane == me, tail, 0.0), axis=1, keepdims=True)
        low = jnp.sum(
            jnp.where(bin_lane == me + N_EXPERTS, tail, 0.0), axis=1, keepdims=True
        )
        at_high = jnp.where(high == bins_at, energy, 0.0)
        at_low = small(low == bins_at)
        first, second, third = split3(at_high)
        hist = mm_t(first, at_low) + mm_t(second, at_low) + mm_t(third, at_low)
        return activation.astype(jnp.bfloat16), hist

    for load in loads:
        load.wait()
    hidden, hist = run_block(0)
    kept[...] = mm(hidden, down_ref[...])
    for copy in mate_flight:
        copy.wait_recv()
    hidden, more = run_block(1)
    to_mate[...] = (
        mm(hidden, down_ref[...]).astype(jnp.bfloat16).reshape(to_mate.shape)
    )
    mate_out = {}
    for half in (1, 0):
        mate_out[half] = remote(
            to_mate.at[half], from_mate.at[half], o_send.at[half], o_recv.at[half], mate
        )
    pending += mate_out.values()

    hist_out[...] = (hist + more)[: N_CTX * 8].reshape(N_CTX, 8, 2 * N_EXPERTS)
    hist_flight = [
        remote(
            hist_out.at[(ctx + j) % N_CTX],
            hist_in.at[j - 1],
            h_send.at[j - 1],
            h_recv.at[j - 1],
            c_peer(j),
        )
        for j in range(1, N_CTX)
    ]
    pending += hist_flight

    back_flight = {}
    for half in (1, 0):
        mate_out[half].wait_recv()
        total = kept[half * half_slots : (half + 1) * half_slots] + from_mate[
            half
        ].reshape(half_slots, width).astype(jnp.float32)
        back[half] = total.astype(jnp.bfloat16).reshape(NQ, piece, width)
        for j in q_order:
            p = (q + j) % NQ
            back_flight[half, j] = remote(
                back.at[half, p],
                returned.at[half, q],
                b_send.at[half, j],
                b_recv.at[half, j],
                q_peer(p),
            )
        returned[half, q] = back[half, q]
    pending += back_flight.values()

    def mixed(half):
        for j in q_order:
            back_flight[half, j].wait_recv()
        return mm(weigh[half], returned[half].reshape(half_slots, width))

    to_y[...] = mixed(1).reshape(NZ, TOK, width).astype(jnp.bfloat16)
    y_flight = {}
    for j in order + (0,):
        z_to = (z + j) % NZ
        y_flight[j] = remote(
            to_y.at[z_to], from_y.at[z_to], ys_send.at[j], ys_recv.at[j], y_peer
        )
    pending += y_flight.values()
    own[...] = mixed(0).reshape(NZ, TOK, width)
    z_flight = []
    for j in order + (0,):
        z_to = (z + j) % NZ
        y_flight[j].wait_recv()
        to_z[z_to] = (own[z_to] + from_y[z_to].astype(jnp.float32)).astype(jnp.bfloat16)
        if j:
            z_flight.append(
                remote(
                    to_z.at[z_to],
                    from_z.at[j - 1],
                    zs_send.at[j - 1],
                    zs_recv.at[j - 1],
                    z_peer(z_to),
                )
            )
    pending += z_flight
    for copy in hist_flight:
        copy.wait_recv()
    hist = hist_out[ctx]
    for j in range(N_CTX - 1):
        hist = hist + hist_in[j]
    hist_ref[...] = hist
    for copy in z_flight:
        copy.wait_recv()
    total = to_z[z].astype(jnp.float32)
    for j in range(NZ - 1):
        total = total + from_z[j].astype(jnp.float32)
    out_ref[...] = total
    for copy in pending:
        copy.wait_send()


def run_experts(rows, gate, up, down):
    width = down.shape[1]
    sent = width + 2 * N_EXPERTS
    half_slots, piece = NQ * NZ * CAP, NZ * CAP
    bf16, f32 = jnp.bfloat16, jnp.float32
    dma = pltpu.SemaphoreType.DMA
    vmem = pl.BlockSpec(memory_space=pltpu.VMEM)
    hbm = pl.BlockSpec(memory_space=pltpu.HBM)
    return pl.pallas_call(
        experts_kernel,
        out_shape=(
            jax.ShapeDtypeStruct((TOK, width), f32),
            jax.ShapeDtypeStruct((8, 2 * N_EXPERTS), f32),
        ),
        in_specs=[vmem, hbm, hbm, hbm],
        out_specs=(vmem, vmem),
        scratch_shapes=[
            pltpu.VMEM(gate.shape, bf16),
            pltpu.VMEM(up.shape, bf16),
            pltpu.VMEM(down.shape, bf16),
            pltpu.VMEM((2, NZ, TOK, rows.shape[1]), bf16),
            pltpu.VMEM((2, NZ * TOK, half_slots), bf16),
            pltpu.VMEM((2, NQ, piece, sent), bf16),
            pltpu.VMEM((2, 2, NQ, piece, sent), bf16),
            pltpu.VMEM((2 * half_slots, width), f32),
            pltpu.VMEM((2, NQ, piece, width), bf16),
            pltpu.VMEM((2, NQ, piece, width), bf16),
            pltpu.VMEM((2, NQ, piece, width), bf16),
            pltpu.VMEM((2, NQ, piece, width), bf16),
            pltpu.VMEM((NZ, TOK, width), bf16),
            pltpu.VMEM((NZ, TOK, width), bf16),
            pltpu.VMEM((NZ, TOK, width), f32),
            pltpu.VMEM((NZ, TOK, width), bf16),
            pltpu.VMEM((NZ - 1, TOK, width), bf16),
            pltpu.VMEM((N_CTX, 8, 2 * N_EXPERTS), f32),
            pltpu.VMEM((N_CTX - 1, 8, 2 * N_EXPERTS), f32),
            dma((3,)),
            dma((2, NZ // 2)),
            dma((2, NZ // 2)),
            dma((NZ,)),
            dma((NZ,)),
            dma((2, NQ)),
            dma((2, NQ)),
            dma((2, NQ)),
            dma((2, NQ)),
            dma((2,)),
            dma((2,)),
            dma((2, NQ)),
            dma((2, NQ)),
            dma((NZ,)),
            dma((NZ,)),
            dma((NZ - 1,)),
            dma((NZ - 1,)),
            dma((N_CTX - 1,)),
            dma((N_CTX - 1,)),
        ],
        compiler_params=pltpu.CompilerParams(
            collective_id=1, has_side_effects=True, vmem_limit_bytes=60 << 20
        ),
        name="experts",
    )(rows, gate, up, down)


def route_lanes(expert_ids, gate_levels, bin_ids):
    onehot = expert_ids[:, :, None] == jnp.arange(N_EXPERTS, dtype=jnp.int32)

    def spread(v):
        return jnp.sum(jnp.where(onehot, v[:, :, None], 0), axis=1)

    named = jnp.sum(onehot.astype(jnp.int32), axis=1)
    earlier = jnp.arange(TOK)[:, None] > jnp.arange(TOK)[None, :]
    rank = jnp.sum(jnp.where(earlier[:, :, None], named[None, :, :], 0), axis=1)
    lanes = (spread(bin_ids // 64), spread(bin_ids % 64), spread(gate_levels), rank)
    return jnp.concatenate(lanes, axis=1).astype(jnp.bfloat16)


def on_device(
    residual_in,
    norm_gain,
    q_nope,
    q_rope,
    latent,
    k_rope,
    doc_ids,
    uv_weight,
    out_weight,
    expert_ids,
    gate_levels,
    bin_ids,
    gate_weight,
    up_weight,
    down_weight,
):
    block_len, head_count, _ = q_nope.shape
    attended = attend_sum(
        q_nope.reshape(block_len, head_count * q_nope.shape[2]),
        q_rope,
        latent,
        k_rope.T,
        doc_ids.reshape(1, block_len),
        uv_weight,
        out_weight,
    )
    stream_state = residual_in.astype(jnp.float32) + attended
    normed = (
        stream_state
        * lax.rsqrt(jnp.mean(stream_state * stream_state, axis=1, keepdims=True) + norm_eps)
        * norm_gain
    ).astype(jnp.bfloat16)
    rows = jnp.concatenate(
        (normed, route_lanes(expert_ids, gate_levels, bin_ids)), axis=1
    )
    mixture, hist = run_experts(rows, gate_weight[0], up_weight[0], down_weight[0])
    scale = 1.0 / jnp.sum(gate_levels.astype(jnp.float32), axis=1, keepdims=True)
    layer_out = (stream_state + mixture * scale).astype(jnp.bfloat16)
    histogram = hist[:, : NBINS // 32].reshape(1, NBINS // N_CTX)
    return (layer_out, histogram)


def solution(mesh):
    return jax.shard_map(
        on_device,
        mesh=mesh,
        in_specs=(
            P(("ctx", "exp"), None),
            P(),
            P("ctx", "exp", None),
            P("ctx", "exp"),
            P("ctx", None),
            P("ctx", None),
            P("ctx"),
            P("exp", None, None),
            P("exp", None),
            P(("ctx", "exp"), None),
            P(("ctx", "exp"), None),
            P(("ctx", "exp"), None),
            P("exp", None, "ctx"),
            P("exp", None, "ctx"),
            P("exp", "ctx", None),
        ),
        out_specs=(P(("ctx", "exp"), None), P("exp", "ctx")),
        check_vma=False,
    )
```

```python
import functools
import math

import jax
import jax.numpy as jnp
from jax import lax
from jax.experimental import pallas as pl
from jax.experimental.pallas import tpu as pltpu
from jax.sharding import PartitionSpec as P

HID = 1024
NBINS = 2048


exponent_scale = 192.0 ** (-0.5) * math.log2(math.e)
norm_eps = 1e-06
masked_score = -1e30

NZ, NX, NY = 8, 4, 2
NQ = NX * NY
NR = NZ * NY
TOK = 8
CAP = 2
N_CTX = 4
N_EXPERTS = 64
ROPE = 64
VDIM = 128
DOC_ROWS = 16
KEY_PIECES = 2
SUBS = 2
MESH = pl.DeviceIdType.MESH


def remote(src, dst, send_sem, recv_sem, target):
    copy = pltpu.make_async_remote_copy(
        src_ref=src,
        dst_ref=dst,
        send_sem=send_sem,
        recv_sem=recv_sem,
        device_id=target,
        device_id_type=MESH,
    )
    copy.start()
    return copy


def greet(targets):
    barrier = pltpu.get_barrier_semaphore()
    for target in targets:
        pl.semaphore_signal(barrier, inc=1, device_id=target, device_id_type=MESH)
    pl.semaphore_wait(barrier, len(targets))


def small(cond):
    return cond.astype(jnp.float32).astype(jnp.bfloat16)


def split3(v):
    first = v.astype(jnp.bfloat16)
    rest = v - first.astype(jnp.float32)
    second = rest.astype(jnp.bfloat16)
    third = (rest - second.astype(jnp.float32)).astype(jnp.bfloat16)
    return first, second, third


def mm(a, b):
    return jnp.dot(a, b, preferred_element_type=jnp.float32)


def mm_t(a, b):
    return lax.dot_general(
        a, b, (((0,), (0,)), ((), ())), preferred_element_type=jnp.float32
    )


def attend_sum_kernel(
    part_a,
    query_ref,
    query_rope_ref,
    latent_ref,
    rope_ref,
    doc_ref,
    uv_hbm,
    weight_hbm,
    out_ref,
    uv_ref,
    weight_ref,
    nope_ref,
    tail_ref,
    keys,
    tails,
    top,
    denominator,
    accum,
    values_ref,
    a_first,
    a_slots,
    b_first,
    b_slots,
    a_push,
    a_got,
    b_mid,
    b_other,
    b_push,
    b_got,
    k_send_sem,
    k_recv_sem,
    t_send_sem,
    t_recv_sem,
    a_send_sem,
    a_recv_sem,
    b_send_sem,
    b_recv_sem,
    ap_send_sem,
    ap_recv_sem,
    bp_send_sem,
    bp_recv_sem,
    bc_send_sem,
    bc_recv_sem,
    load_sem,
):
    loads = [
        pltpu.make_async_copy(uv_hbm, uv_ref, load_sem.at[0]),
        pltpu.make_async_copy(weight_hbm, weight_ref, load_sem.at[1]),
    ]
    for load in loads:
        load.start()
    width = weight_ref.shape[1]
    wide_a, wide_b = part_a // (2 * SUBS), (width - part_a) // (2 * SUBS)
    me = lax.axis_index("exp")
    z, x, y = me // NQ, (me // NY) % NX, me % NY
    q = x * NY + y

    def at(z_at, x_at, y_at):
        return {"exp": (z_at * NX + x_at) * NY + y_at}

    q_peers = [(q + j) % NQ for j in range(NQ)]
    z_peers = [(z + j) % NZ for j in range(NZ)]
    y_other = at(z, x, 1 - y)
    z_next = [at((z + 1) % NZ, x, y), at((z + NZ - 1) % NZ, x, y)]
    x_next = [at(z, (x + 1) % NX, y), at(z, (x + NX - 1) % NX, y)]
    ctx = lax.axis_index("ctx")
    y_lo, core = ctx // 2, ctx % 2
    mate = {"ctx": y_lo * 2 + 1 - core, "exp": me}
    across = {"ctx": (1 - y_lo) * 2 + core, "exp": me}
    greet(
        [at(z, p // NY, p % NY) for p in q_peers[1:]]
        + [at(p, x, y) for p in z_peers[1:]]
        + [mate, across]
    )

    block_len, lat = latent_ref.shape
    piece = block_len // KEY_PIECES
    for i in range(KEY_PIECES):
        tail_ref[i, :ROPE] = rope_ref[:, i * piece : (i + 1) * piece]
        tail_ref[i, ROPE:] = jnp.broadcast_to(
            doc_ref[:, i * piece : (i + 1) * piece].astype(jnp.float32),
            (DOC_ROWS, piece),
        ).astype(jnp.bfloat16)

    class KeyCopy:
        def __init__(self, back, i, forward, target):
            self.copies = [
                pltpu.make_async_remote_copy(
                    src_ref=src,
                    dst_ref=dst.at[i, back],
                    send_sem=send_sem.at[back, i],
                    recv_sem=recv_sem.at[back, i],
                    device_id=target,
                    device_id_type=MESH,
                )
                for src, dst, send_sem, recv_sem in (
                    (
                        keys.at[i, 1]
                        if forward
                        else latent_ref.at[i * piece : (i + 1) * piece],
                        keys,
                        k_send_sem,
                        k_recv_sem,
                    ),
                    (
                        tails.at[i, 1] if forward else tail_ref.at[i],
                        tails,
                        t_send_sem,
                        t_recv_sem,
                    ),
                )
            ]

        def start(self):
            for copy in self.copies:
                copy.start()

        def wait_recv(self):
            for copy in self.copies:
                copy.wait_recv()

        def wait_send(self):
            for copy in self.copies:
                copy.wait_send()

    for i in range(KEY_PIECES):

        @pl.when(y_lo == 0)
        def _():
            KeyCopy(1, i, False, across).start()

    for i in range(KEY_PIECES):

        @pl.when(core == 0)
        def _():
            KeyCopy(0, i, False, mate).start()

    def nt(a, b):
        return lax.dot_general(
            a, b, (((1,), (1,)), ((), ())), preferred_element_type=jnp.float32
        )

    heads = uv_ref.shape[0]
    part = block_len // 8

    def unpack(i, carry):
        here = pl.ds(pl.multiple_of(i * part, part), part)
        for head in range(heads):
            nope_ref[head, here] = query_ref[here, head]
        return carry

    lax.fori_loop(0, 8, unpack, 0)
    doc_pick = small(lax.broadcasted_iota(jnp.int32, (DOC_ROWS, 128), 0) == 0)
    query_docs = jnp.concatenate(
        [mm_t(tail_ref[i, ROPE:], doc_pick)[:, :1] for i in range(KEY_PIECES)], axis=0
    )

    def fold(block, tail, offset=None):
        first = offset == 0
        allowed = query_docs == tail[ROPE : ROPE + 1].astype(jnp.float32)
        if offset is not None:
            shape = (block_len, block.shape[0])
            query_at = lax.broadcasted_iota(jnp.int32, shape, 0)
            key_at = lax.broadcasted_iota(jnp.int32, shape, 1) + offset
            allowed = allowed & (key_at <= query_at)
        for head in range(heads):
            nope = nope_ref[head]
            rope = query_rope_ref[:, head * ROPE : (head + 1) * ROPE]
            raw = nt(nope, block) + mm(rope, tail[:ROPE])
            scores = jnp.where(allowed, raw, masked_score)
            peak = jnp.max(scores, axis=1, keepdims=True)
            if not first:
                old = top[head][:, :1]
                peak = jnp.maximum(old, peak)
                fade = jnp.exp2((old - peak) * exponent_scale)
            probs = jnp.exp2((scores - peak) * exponent_scale)
            mass = jnp.sum(probs, axis=1, keepdims=True)
            mixed = mm(probs.astype(jnp.bfloat16), block)
            if not first:
                mass = mass + denominator[head][:, :1] * fade
                mixed = mixed + accum[head] * fade
            top[head] = jnp.broadcast_to(peak, top.shape[1:])
            denominator[head] = jnp.broadcast_to(mass, denominator.shape[1:])
            accum[head] = mixed

    own_tail = jnp.concatenate([tail_ref[i] for i in range(KEY_PIECES)], axis=1)
    fold(latent_ref[...], own_tail, 0)

    def fold_pair(blocks):
        block = jnp.concatenate([keys[i, back] for i, back in blocks], axis=0)
        tail = jnp.concatenate([tails[i, back] for i, back in blocks], axis=1)
        fold(block, tail)

    def near_arrived(i):
        KeyCopy(0, i, False, mate).wait_recv()

    def far_arrived(i):
        KeyCopy(1, i, False, across).wait_recv()

    @pl.when(ctx == 1)
    def _():
        near_arrived(0)
        near_arrived(1)
        fold_pair(((0, 0), (1, 0)))

    @pl.when(ctx == 2)
    def _():
        for i in range(KEY_PIECES):
            far_arrived(i)
            near_arrived(i)
            fold_pair(((i, 0), (i, 1)))

    @pl.when(ctx == 3)
    def _():
        far_arrived(0)
        KeyCopy(0, 0, True, mate).start()
        near_arrived(0)
        near_arrived(1)
        fold_pair(((0, 0), (1, 0), (0, 1)))
        far_arrived(1)
        KeyCopy(0, 1, True, mate).start()
        fold(keys[1, 1], tails[1, 1])

    for load in loads:
        load.wait()
    for head in range(heads):
        context = (accum[head] / denominator[head][:, :1]).astype(jnp.bfloat16)
        values_ref[:, :, :, head * VDIM : (head + 1) * VDIM] = (
            mm(context, uv_ref[head])
            .astype(jnp.bfloat16)
            .reshape(NZ, NX, NY * TOK, VDIM)
        )

    def a_own(way, sub, chunk):
        rows = values_ref[chunk].reshape(NX * NY * TOK, values_ref.shape[3])
        start = (way * SUBS + sub) * wide_a
        return mm(rows, weight_ref[:, start : start + wide_a])

    def b_own(way, sub, chunk):
        rows = values_ref[:, chunk].reshape(NZ * NY * TOK, values_ref.shape[3])
        start = part_a + (way * SUBS + sub) * wide_b
        return mm(rows, weight_ref[:, start : start + wide_b])

    a_flight, b_flight, pushes = {}, {}, []

    def ring_step(step, here, count, own_of, first, slots, sems, onward, flight):
        for sub in range(SUBS):
            for way in range(2):
                sign = -1 if way == 0 else 1
                own = own_of(way, sub, (here + sign * (1 + step) + 2 * count) % count)
                if step == 0:
                    src = first.at[way, sub]
                    first[way, sub] = own.astype(jnp.bfloat16)
                else:
                    src = slots.at[way, sub, step - 1]
                    flight[way, sub, step - 1].wait_recv()
                    slots[way, sub, step - 1] = (
                        slots[way, sub, step - 1].astype(jnp.float32) + own
                    ).astype(jnp.bfloat16)
                flight[way, sub, step] = remote(
                    src,
                    slots.at[way, sub, step],
                    sems[0].at[way, sub, step],
                    sems[1].at[way, sub, step],
                    onward[way],
                )

    def a_step(step):
        ring_step(
            step, z, NZ, a_own, a_first, a_slots,
            (a_send_sem, a_recv_sem), z_next, a_flight,
        )

    def b_step(step):
        ring_step(
            step, x, NX, b_own, b_first, b_slots,
            (b_send_sem, b_recv_sem), x_next, b_flight,
        )

    def a_push_out():
        for sub in range(SUBS):
            for way in range(2):
                own = a_own(way, sub, z)
                a_flight[way, sub, NZ - 2].wait_recv()
                own = own + a_slots[way, sub, NZ - 2].astype(jnp.float32)
                start = (way * SUBS + sub) * wide_a
                a_push[:, :, start : start + wide_a] = own.reshape(
                    NQ, TOK, wide_a
                ).astype(jnp.bfloat16)
        for j in range(1, NQ):
            p = q_peers[j]
            pushes.append(
                remote(
                    a_push.at[p],
                    a_got.at[j - 1],
                    ap_send_sem.at[j - 1],
                    ap_recv_sem.at[j - 1],
                    at(z, p // NY, p % NY),
                )
            )

    b_cross = []

    def b_cross_out():
        for sub in range(SUBS):
            for way in range(2):
                k = way * SUBS + sub
                own = b_own(way, sub, x)
                b_flight[way, sub, NX - 2].wait_recv()
                own = own + b_slots[way, sub, NX - 2].astype(jnp.float32)
                own = own.reshape(NZ, NY, TOK, wide_b)
                for y_at in range(NY):
                    b_mid[k, y_at] = own[:, y_at].astype(jnp.bfloat16)
                b_cross.append(
                    (
                        k,
                        remote(
                            b_mid.at[k, 1 - y],
                            b_other.at[k],
                            bc_send_sem.at[k],
                            bc_recv_sem.at[k],
                            y_other,
                        ),
                    )
                )

    def b_push_out():
        for k, copy in b_cross:
            copy.wait_recv()
            own = b_mid[k, y].astype(jnp.float32) + b_other[k].astype(jnp.float32)
            b_push[:, :, k * wide_b : (k + 1) * wide_b] = own.astype(jnp.bfloat16)
        for j in (4, 3, 5, 2, 6, 1, 7):
            p = z_peers[j]
            pushes.append(
                remote(
                    b_push.at[p],
                    b_got.at[j - 1],
                    bp_send_sem.at[j - 1],
                    bp_recv_sem.at[j - 1],
                    at(p, x, y),
                )
            )

    a_step(0)
    b_step(0)
    a_step(1)
    a_step(2)
    b_step(1)
    a_step(3)
    b_step(2)
    a_step(4)
    b_cross_out()
    a_step(5)
    b_push_out()
    a_step(6)
    a_push_out()
    for copy in pushes:
        copy.wait_recv()
    total = b_push[z].astype(jnp.float32)
    for j in range(NZ - 1):
        total = total + b_got[j].astype(jnp.float32)
    out_ref[:, part_a:] = total
    total = a_push[q].astype(jnp.float32)
    for j in range(NQ - 1):
        total = total + a_got[j].astype(jnp.float32)
    out_ref[:, :part_a] = total
    crossed = [copy for _, copy in b_cross]
    for copy in [*a_flight.values(), *b_flight.values(), *crossed, *pushes]:
        copy.wait_send()
    for i in range(KEY_PIECES):

        @pl.when(y_lo == 0)
        def _():
            KeyCopy(1, i, False, across).wait_send()

        @pl.when((core == 0) | (y_lo == 1))
        def _():
            KeyCopy(0, i, False, mate).wait_send()


def attend_sum(q_nope, q_rope, latent, rope_t, docs, uv_weight, weight, part_a=2048):
    heads, lat = uv_weight.shape[:2]
    rows = latent.shape[0]
    width = weight.shape[1]
    part_b = width - part_a
    wide_a, wide_b = part_a // (2 * SUBS), part_b // (2 * SUBS)
    bf16 = jnp.bfloat16
    dma = pltpu.SemaphoreType.DMA
    return pl.pallas_call(
        functools.partial(attend_sum_kernel, part_a),
        out_shape=jax.ShapeDtypeStruct((TOK, width), jnp.float32),
        in_specs=[pl.BlockSpec(memory_space=pltpu.VMEM)] * 5
        + [pl.BlockSpec(memory_space=pltpu.HBM)] * 2,
        out_specs=pl.BlockSpec(memory_space=pltpu.VMEM),
        scratch_shapes=[
            pltpu.VMEM(uv_weight.shape, bf16),
            pltpu.VMEM(weight.shape, bf16),
            pltpu.VMEM((heads, rows, lat), bf16),
            pltpu.VMEM((KEY_PIECES, ROPE + DOC_ROWS, rows // KEY_PIECES), bf16),
            pltpu.VMEM((KEY_PIECES, 2, rows // KEY_PIECES, lat), bf16),
            pltpu.VMEM((KEY_PIECES, 2, ROPE + DOC_ROWS, rows // KEY_PIECES), bf16),
            pltpu.VMEM((heads, rows, 128), jnp.float32),
            pltpu.VMEM((heads, rows, 128), jnp.float32),
            pltpu.VMEM((heads, rows, lat), jnp.float32),
            pltpu.VMEM((NZ, NX, NY * TOK, heads * VDIM), bf16),
            pltpu.VMEM((2, SUBS, NQ * TOK, wide_a), bf16),
            pltpu.VMEM((2, SUBS, NZ - 1, NQ * TOK, wide_a), bf16),
            pltpu.VMEM((2, SUBS, NR * TOK, wide_b), bf16),
            pltpu.VMEM((2, SUBS, NX - 1, NR * TOK, wide_b), bf16),
            pltpu.VMEM((NQ, TOK, part_a), bf16),
            pltpu.VMEM((NQ - 1, TOK, part_a), bf16),
            pltpu.VMEM((2 * SUBS, NY, NZ, TOK, wide_b), bf16),
            pltpu.VMEM((2 * SUBS, NZ, TOK, wide_b), bf16),
            pltpu.VMEM((NZ, TOK, part_b), bf16),
            pltpu.VMEM((NZ - 1, TOK, part_b), bf16),
            dma((2, KEY_PIECES)),
            dma((2, KEY_PIECES)),
            dma((2, KEY_PIECES)),
            dma((2, KEY_PIECES)),
            dma((2, SUBS, NZ - 1)),
            dma((2, SUBS, NZ - 1)),
            dma((2, SUBS, NX - 1)),
            dma((2, SUBS, NX - 1)),
            dma((NQ - 1,)),
            dma((NQ - 1,)),
            dma((NZ - 1,)),
            dma((NZ - 1,)),
            dma((2 * SUBS,)),
            dma((2 * SUBS,)),
            dma((2,)),
        ],
        compiler_params=pltpu.CompilerParams(
            collective_id=0, has_side_effects=True, vmem_limit_bytes=60 << 20
        ),
        name="attend_sum",
    )(q_nope, q_rope, latent, rope_t, docs, uv_weight, weight)


def experts_kernel(
    rows_ref,
    gate_hbm,
    up_hbm,
    down_hbm,
    out_ref,
    hist_ref,
    gate_ref,
    up_ref,
    down_ref,
    near,
    weigh,
    slots,
    inbox,
    kept,
    to_mate,
    from_mate,
    back,
    returned,
    to_y,
    from_y,
    own,
    to_z,
    from_z,
    hist_out,
    hist_in,
    load_sem,
    z_send,
    z_recv,
    y_send,
    y_recv,
    q_send,
    q_recv,
    m_send,
    m_recv,
    o_send,
    o_recv,
    b_send,
    b_recv,
    ys_send,
    ys_recv,
    zs_send,
    zs_recv,
    h_send,
    h_recv,
):
    width = down_hbm.shape[1]
    sent = width + 2 * N_EXPERTS
    half_rows, half_slots = NZ * TOK, NQ * NZ * CAP
    piece = NZ * CAP
    ctx, me = lax.axis_index("ctx"), lax.axis_index("exp")
    y_lo, core = ctx // 2, ctx % 2
    z, q = me // NQ, me % NQ

    def z_peer(z_at):
        return {"ctx": ctx, "exp": z_at * NQ + q}

    def q_peer(q_at):
        return {"ctx": ctx, "exp": z * NQ + q_at}

    y_peer = {"ctx": (1 - y_lo) * 2 + core, "exp": me}
    mate = {"ctx": y_lo * 2 + 1 - core, "exp": me}

    def c_peer(j):
        return {"ctx": (ctx + j) % N_CTX, "exp": me}

    loads = [
        pltpu.make_async_copy(src, dst, load_sem.at[i])
        for i, (src, dst) in enumerate(
            ((gate_hbm, gate_ref), (up_hbm, up_ref), (down_hbm, down_ref))
        )
    ]
    for load in loads:
        load.start()
    greet(
        [z_peer((z + j) % NZ) for j in range(1, NZ)]
        + [q_peer((q + j) % NQ) for j in range(1, NQ)]
        + [c_peer(j) for j in range(1, N_CTX)]
    )
    pending = []

    order = (4, 3, 5, 2, 6, 1, 7)
    near[y_lo, z] = rows_ref[...]
    hops = NZ // 2
    middle = rows_ref.shape[1] // 2
    onward = (z_peer((z + 1) % NZ), z_peer((z + NZ - 1) % NZ))
    ring = {}

    def pass_on(way, step, src, dst):
        ring[way, step] = remote(
            src, dst, z_send.at[way, step], z_recv.at[way, step], onward[way]
        )
        pending.append(ring[way, step])

    crossings = []

    def cross(src, dst):
        n = len(crossings)
        crossings.append(remote(src, dst, y_send.at[n], y_recv.at[n], y_peer))

    for way in range(2):
        pass_on(way, 0, rows_ref, near.at[y_lo, z])
    cross(rows_ref, near.at[y_lo, z])
    for step in range(1, hops):
        for way in range(2):
            z_from = (z + (NZ - step if way == 0 else step)) % NZ
            ring[way, step - 1].wait_recv()
            held = near.at[y_lo, z_from]
            if step < hops - 1:
                pass_on(way, step, held, held)
            else:
                side = pl.ds(way * middle, middle)
                part = near.at[y_lo, z_from, :, side]
                pass_on(way, step, part, part)
            cross(held, held)
    for way in range(2):
        ring[way, hops - 1].wait_recv()
    held = near.at[y_lo, (z + hops) % NZ]
    cross(held, held)
    pending += crossings

    lane = lax.broadcasted_iota(jnp.int32, (2 * N_EXPERTS, half_slots), 0)
    wanted = z * NQ + (
        lax.broadcasted_iota(jnp.int32, (2 * N_EXPERTS, half_slots), 1) // piece
    )
    pick_level, pick_rank = small(lane == wanted), small(lane == wanted + N_EXPERTS)
    row = lax.broadcasted_iota(jnp.int32, (half_rows, half_slots), 0)
    col = lax.broadcasted_iota(jnp.int32, (half_rows, half_slots), 1)
    same_source = (row // TOK) == ((col // CAP) % NZ)
    slot_rank = (col % CAP).astype(jnp.float32)

    q_order = (1, 2, 3, 4, 5, 6, 7)
    slot_flight = {}
    for half in range(2):
        if half == 1:
            for copy in crossings:
                copy.wait_recv()
        y_at = y_lo if half == 0 else 1 - y_lo
        held = (
            near[y_at]
            .astype(jnp.float32)
            .reshape(half_rows, sent + 2 * N_EXPERTS)
            .astype(jnp.bfloat16)
        )
        route = held[:, sent:]
        level, rank = mm(route, pick_level), mm(route, pick_rank)
        chosen = (level > 0.5) & (rank == slot_rank) & same_source
        weigh[half] = jnp.where(chosen, level, 0.0).astype(jnp.bfloat16)
        picked = mm_t(small(chosen), held[:, :sent])
        slots[half] = picked.astype(jnp.bfloat16).reshape(NQ, piece, sent)
        for j in q_order:
            p = (q + j) % NQ
            slot_flight[half, j] = remote(
                slots.at[half, p],
                inbox.at[half, 0, q],
                q_send.at[half, j],
                q_recv.at[half, j],
                q_peer(p),
            )
        inbox[half, 0, q] = slots[half, q]
    pending += slot_flight.values()

    bin_lane = lax.broadcasted_iota(jnp.int32, (2 * half_slots, 2 * N_EXPERTS), 1)
    bins_at = bin_lane.astype(jnp.float32)

    def run_block(half):
        block = inbox[half].reshape(2 * half_slots, sent)
        x = block[:, :width]
        gate_part, up_part = mm(x, gate_ref[...]), mm(x, up_ref[...])
        activation = gate_part / (1.0 + jnp.exp(-gate_part)) * up_part
        energy = jnp.sum(activation * activation, axis=1, keepdims=True) * (1.0 / HID)
        tail = block[:, width:].astype(jnp.float32)
        high = jnp.sum(jnp.where(bin_lane == me, tail, 0.0), axis=1, keepdims=True)
        low = jnp.sum(
            jnp.where(bin_lane == me + N_EXPERTS, tail, 0.0), axis=1, keepdims=True
        )
        at_high = jnp.where(high == bins_at, energy, 0.0)
        at_low = small(low == bins_at)
        first, second, third = split3(at_high)
        hist = mm_t(first, at_low) + mm_t(second, at_low) + mm_t(third, at_low)
        return activation.astype(jnp.bfloat16), hist

    back_flight = {}

    def run_half(half):
        flight = []
        for j in (0,) + q_order:
            q_from = (q + NQ - j) % NQ
            if j:
                slot_flight[half, j].wait_recv()
            flight.append(
                remote(
                    inbox.at[half, 0, q_from],
                    inbox.at[half, 1, q_from],
                    m_send.at[half, j],
                    m_recv.at[half, j],
                    mate,
                )
            )
        for copy in flight:
            copy.wait_recv()
        if half == 0:
            for load in loads:
                load.wait()
        hidden, hist = run_block(half)
        to_mate[half] = (
            mm(hidden[half_slots:], down_ref[...])
            .astype(jnp.bfloat16)
            .reshape(NQ, piece, width)
        )
        swap = remote(
            to_mate.at[half], from_mate.at[half], o_send.at[half], o_recv.at[half], mate
        )
        kept[...] = mm(hidden[:half_slots], down_ref[...])
        swap.wait_recv()
        total = kept[...] + from_mate[half].reshape(half_slots, width).astype(
            jnp.float32
        )
        back[half] = total.astype(jnp.bfloat16).reshape(NQ, piece, width)
        for j in q_order:
            p = (q + j) % NQ
            back_flight[half, j] = remote(
                back.at[half, p],
                returned.at[half, q],
                b_send.at[half, j],
                b_recv.at[half, j],
                q_peer(p),
            )
        returned[half, q] = back[half, q]
        pending.extend(flight + [swap])
        return hist

    hist = run_half(0)
    more = run_half(1)

    hist_out[...] = (hist + more)[: N_CTX * 8].reshape(N_CTX, 8, 2 * N_EXPERTS)
    hist_flight = [
        remote(
            hist_out.at[(ctx + j) % N_CTX],
            hist_in.at[j - 1],
            h_send.at[j - 1],
            h_recv.at[j - 1],
            c_peer(j),
        )
        for j in range(1, N_CTX)
    ]
    pending += hist_flight

    pending += back_flight.values()

    def mixed(half):
        for j in q_order:
            back_flight[half, j].wait_recv()
        return mm(weigh[half], returned[half].reshape(half_slots, width))

    own[...] = mixed(0).reshape(NZ, TOK, width)
    to_y[...] = mixed(1).reshape(NZ, TOK, width).astype(jnp.bfloat16)
    y_flight = {}
    for j in order + (0,):
        z_to = (z + j) % NZ
        y_flight[j] = remote(
            to_y.at[z_to], from_y.at[z_to], ys_send.at[j], ys_recv.at[j], y_peer
        )
    pending += y_flight.values()
    z_flight = []
    for j in order + (0,):
        z_to = (z + j) % NZ
        y_flight[j].wait_recv()
        to_z[z_to] = (own[z_to] + from_y[z_to].astype(jnp.float32)).astype(jnp.bfloat16)
        if j:
            z_flight.append(
                remote(
                    to_z.at[z_to],
                    from_z.at[j - 1],
                    zs_send.at[j - 1],
                    zs_recv.at[j - 1],
                    z_peer(z_to),
                )
            )
    pending += z_flight
    for copy in hist_flight:
        copy.wait_recv()
    hist = hist_out[ctx]
    for j in range(N_CTX - 1):
        hist = hist + hist_in[j]
    hist_ref[...] = hist
    for copy in z_flight:
        copy.wait_recv()
    total = to_z[z].astype(jnp.float32)
    for j in range(NZ - 1):
        total = total + from_z[j].astype(jnp.float32)
    out_ref[...] = total
    for copy in pending:
        copy.wait_send()


def run_experts(rows, gate, up, down):
    width = down.shape[1]
    sent = width + 2 * N_EXPERTS
    half_slots, piece = NQ * NZ * CAP, NZ * CAP
    bf16, f32 = jnp.bfloat16, jnp.float32
    dma = pltpu.SemaphoreType.DMA
    vmem = pl.BlockSpec(memory_space=pltpu.VMEM)
    hbm = pl.BlockSpec(memory_space=pltpu.HBM)
    return pl.pallas_call(
        experts_kernel,
        out_shape=(
            jax.ShapeDtypeStruct((TOK, width), f32),
            jax.ShapeDtypeStruct((8, 2 * N_EXPERTS), f32),
        ),
        in_specs=[vmem, hbm, hbm, hbm],
        out_specs=(vmem, vmem),
        scratch_shapes=[
            pltpu.VMEM(gate.shape, bf16),
            pltpu.VMEM(up.shape, bf16),
            pltpu.VMEM(down.shape, bf16),
            pltpu.VMEM((2, NZ, TOK, rows.shape[1]), bf16),
            pltpu.VMEM((2, NZ * TOK, half_slots), bf16),
            pltpu.VMEM((2, NQ, piece, sent), bf16),
            pltpu.VMEM((2, 2, NQ, piece, sent), bf16),
            pltpu.VMEM((half_slots, width), f32),
            pltpu.VMEM((2, NQ, piece, width), bf16),
            pltpu.VMEM((2, NQ, piece, width), bf16),
            pltpu.VMEM((2, NQ, piece, width), bf16),
            pltpu.VMEM((2, NQ, piece, width), bf16),
            pltpu.VMEM((NZ, TOK, width), bf16),
            pltpu.VMEM((NZ, TOK, width), bf16),
            pltpu.VMEM((NZ, TOK, width), f32),
            pltpu.VMEM((NZ, TOK, width), bf16),
            pltpu.VMEM((NZ - 1, TOK, width), bf16),
            pltpu.VMEM((N_CTX, 8, 2 * N_EXPERTS), f32),
            pltpu.VMEM((N_CTX - 1, 8, 2 * N_EXPERTS), f32),
            dma((3,)),
            dma((2, NZ // 2)),
            dma((2, NZ // 2)),
            dma((NZ,)),
            dma((NZ,)),
            dma((2, NQ)),
            dma((2, NQ)),
            dma((2, NQ)),
            dma((2, NQ)),
            dma((2,)),
            dma((2,)),
            dma((2, NQ)),
            dma((2, NQ)),
            dma((NZ,)),
            dma((NZ,)),
            dma((NZ - 1,)),
            dma((NZ - 1,)),
            dma((N_CTX - 1,)),
            dma((N_CTX - 1,)),
        ],
        compiler_params=pltpu.CompilerParams(
            collective_id=1, has_side_effects=True, vmem_limit_bytes=60 << 20
        ),
        name="experts",
    )(rows, gate, up, down)


def route_lanes(expert_ids, gate_levels, bin_ids):
    onehot = expert_ids[:, :, None] == jnp.arange(N_EXPERTS, dtype=jnp.int32)

    def spread(v):
        return jnp.sum(jnp.where(onehot, v[:, :, None], 0), axis=1)

    named = jnp.sum(onehot.astype(jnp.int32), axis=1)
    earlier = jnp.arange(TOK)[:, None] > jnp.arange(TOK)[None, :]
    rank = jnp.sum(jnp.where(earlier[:, :, None], named[None, :, :], 0), axis=1)
    lanes = (spread(bin_ids // 64), spread(bin_ids % 64), spread(gate_levels), rank)
    return jnp.concatenate(lanes, axis=1).astype(jnp.bfloat16)


def on_device(
    residual_in,
    norm_gain,
    q_nope,
    q_rope,
    latent,
    k_rope,
    doc_ids,
    uv_weight,
    out_weight,
    expert_ids,
    gate_levels,
    bin_ids,
    gate_weight,
    up_weight,
    down_weight,
):
    block_len = q_nope.shape[0]
    attended = attend_sum(
        q_nope,
        q_rope,
        latent,
        k_rope.T,
        doc_ids.reshape(1, block_len),
        uv_weight,
        out_weight,
    )
    stream_state = residual_in.astype(jnp.float32) + attended
    normed = (
        stream_state
        * lax.rsqrt(jnp.mean(stream_state * stream_state, axis=1, keepdims=True) + norm_eps)
        * norm_gain
    ).astype(jnp.bfloat16)
    rows = jnp.concatenate(
        (normed, route_lanes(expert_ids, gate_levels, bin_ids)), axis=1
    )
    mixture, hist = run_experts(rows, gate_weight[0], up_weight[0], down_weight[0])
    scale = 1.0 / jnp.sum(gate_levels.astype(jnp.float32), axis=1, keepdims=True)
    layer_out = (stream_state + mixture * scale).astype(jnp.bfloat16)
    histogram = hist[:, : NBINS // 32].reshape(1, NBINS // N_CTX)
    return (layer_out, histogram)


def solution(mesh):
    return jax.shard_map(
        on_device,
        mesh=mesh,
        in_specs=(
            P(("ctx", "exp"), None),
            P(),
            P("ctx", "exp", None),
            P("ctx", "exp"),
            P("ctx", None),
            P("ctx", None),
            P("ctx"),
            P("exp", None, None),
            P("exp", None),
            P(("ctx", "exp"), None),
            P(("ctx", "exp"), None),
            P(("ctx", "exp"), None),
            P("exp", None, "ctx"),
            P("exp", None, "ctx"),
            P("exp", "ctx", None),
        ),
        out_specs=(P(("ctx", "exp"), None), P("exp", "ctx")),
        check_vma=False,
    )
```

```python
import functools
import math

import jax
import jax.numpy as jnp
from jax import lax
from jax.experimental import pallas as pl
from jax.experimental.pallas import tpu as pltpu
from jax.sharding import PartitionSpec as P

HID = 1024
NBINS = 2048


exponent_scale = 192.0 ** (-0.5) * math.log2(math.e)
norm_eps = 1e-06
masked_score = -1e30

NZ, NX, NY = 8, 4, 2
NQ = NX * NY
NR = NZ * NY
TOK = 8
CAP = 2
N_CTX = 4
N_EXPERTS = 64
ROPE = 64
VDIM = 128
DOC_ROWS = 16
KEY_PIECES = 2
SUBS = 2
MESH = pl.DeviceIdType.MESH


def remote(src, dst, send_sem, recv_sem, target):
    copy = pltpu.make_async_remote_copy(
        src_ref=src,
        dst_ref=dst,
        send_sem=send_sem,
        recv_sem=recv_sem,
        device_id=target,
        device_id_type=MESH,
    )
    copy.start()
    return copy


def greet(targets):
    barrier = pltpu.get_barrier_semaphore()
    for target in targets:
        pl.semaphore_signal(barrier, inc=1, device_id=target, device_id_type=MESH)
    pl.semaphore_wait(barrier, len(targets))


def small(cond):
    return cond.astype(jnp.float32).astype(jnp.bfloat16)


def split3(v):
    first = v.astype(jnp.bfloat16)
    rest = v - first.astype(jnp.float32)
    second = rest.astype(jnp.bfloat16)
    third = (rest - second.astype(jnp.float32)).astype(jnp.bfloat16)
    return first, second, third


def mm(a, b):
    return jnp.dot(a, b, preferred_element_type=jnp.float32)


def mm_t(a, b):
    return lax.dot_general(
        a, b, (((0,), (0,)), ((), ())), preferred_element_type=jnp.float32
    )


def attend_sum_kernel(
    part_a,
    query_ref,
    query_rope_ref,
    latent_ref,
    rope_ref,
    doc_ref,
    uv_hbm,
    weight_hbm,
    out_ref,
    uv_ref,
    weight_ref,
    nope_ref,
    tail_ref,
    keys,
    tails,
    top,
    denominator,
    accum,
    values_ref,
    a_first,
    a_slots,
    b_first,
    b_slots,
    a_push,
    a_got,
    b_mid,
    b_other,
    b_push,
    b_got,
    k_send_sem,
    k_recv_sem,
    t_send_sem,
    t_recv_sem,
    a_send_sem,
    a_recv_sem,
    b_send_sem,
    b_recv_sem,
    ap_send_sem,
    ap_recv_sem,
    bp_send_sem,
    bp_recv_sem,
    bc_send_sem,
    bc_recv_sem,
    load_sem,
):
    loads = [
        pltpu.make_async_copy(uv_hbm, uv_ref, load_sem.at[0]),
        pltpu.make_async_copy(weight_hbm, weight_ref, load_sem.at[1]),
    ]
    for load in loads:
        load.start()
    width = weight_ref.shape[1]
    wide_a, wide_b = part_a // (2 * SUBS), (width - part_a) // (2 * SUBS)
    me = lax.axis_index("exp")
    z, x, y = me // NQ, (me // NY) % NX, me % NY
    q = x * NY + y

    def at(z_at, x_at, y_at):
        return {"exp": (z_at * NX + x_at) * NY + y_at}

    q_peers = [(q + j) % NQ for j in range(NQ)]
    z_peers = [(z + j) % NZ for j in range(NZ)]
    y_other = at(z, x, 1 - y)
    z_next = [at((z + 1) % NZ, x, y), at((z + NZ - 1) % NZ, x, y)]
    x_next = [at(z, (x + 1) % NX, y), at(z, (x + NX - 1) % NX, y)]
    ctx = lax.axis_index("ctx")
    y_lo, core = ctx // 2, ctx % 2
    mate = {"ctx": y_lo * 2 + 1 - core, "exp": me}
    across = {"ctx": (1 - y_lo) * 2 + core, "exp": me}
    greet(
        [at(z, p // NY, p % NY) for p in q_peers[1:]]
        + [at(p, x, y) for p in z_peers[1:]]
        + [mate, across, {"ctx": 3 - ctx, "exp": me}]
    )

    block_len, lat = latent_ref.shape
    piece = block_len // KEY_PIECES
    for i in range(KEY_PIECES):
        tail_ref[i, :ROPE] = rope_ref[:, i * piece : (i + 1) * piece]
        tail_ref[i, ROPE:] = jnp.broadcast_to(
            doc_ref[:, i * piece : (i + 1) * piece].astype(jnp.float32),
            (DOC_ROWS, piece),
        ).astype(jnp.bfloat16)

    class KeyCopy:
        def __init__(self, back, i, forward, target):
            self.copies = [
                pltpu.make_async_remote_copy(
                    src_ref=src,
                    dst_ref=dst.at[i, back],
                    send_sem=send_sem.at[back, i],
                    recv_sem=recv_sem.at[back, i],
                    device_id=target,
                    device_id_type=MESH,
                )
                for src, dst, send_sem, recv_sem in (
                    (
                        keys.at[i, 1]
                        if forward
                        else latent_ref.at[i * piece : (i + 1) * piece],
                        keys,
                        k_send_sem,
                        k_recv_sem,
                    ),
                    (
                        tails.at[i, 1] if forward else tail_ref.at[i],
                        tails,
                        t_send_sem,
                        t_recv_sem,
                    ),
                )
            ]

        def start(self):
            for copy in self.copies:
                copy.start()

        def wait_recv(self):
            for copy in self.copies:
                copy.wait_recv()

        def wait_send(self):
            for copy in self.copies:
                copy.wait_send()

    for i in range(KEY_PIECES):

        @pl.when(y_lo == 0)
        def _():
            KeyCopy(1, i, False, across).start()

    for i in range(KEY_PIECES):

        @pl.when(core == 0)
        def _():
            KeyCopy(0, i, False, mate).start()

    def nt(a, b):
        return lax.dot_general(
            a, b, (((1,), (1,)), ((), ())), preferred_element_type=jnp.float32
        )

    heads = uv_ref.shape[0]
    part = block_len // 8

    def unpack(i, carry):
        here = pl.ds(pl.multiple_of(i * part, part), part)
        for head in range(heads):
            nope_ref[head, here] = query_ref[here, head]
        return carry

    lax.fori_loop(0, 8, unpack, 0)
    doc_pick = small(lax.broadcasted_iota(jnp.int32, (DOC_ROWS, 128), 0) == 0)
    query_docs = jnp.concatenate(
        [mm_t(tail_ref[i, ROPE:], doc_pick)[:, :1] for i in range(KEY_PIECES)], axis=0
    )

    def fold(block, tail, offset=None):
        first = offset == 0
        allowed = query_docs == tail[ROPE : ROPE + 1].astype(jnp.float32)
        if offset is not None:
            shape = (block_len, block.shape[0])
            query_at = lax.broadcasted_iota(jnp.int32, shape, 0)
            key_at = lax.broadcasted_iota(jnp.int32, shape, 1) + offset
            allowed = allowed & (key_at <= query_at)
        for head in range(heads):
            nope = nope_ref[head]
            rope = query_rope_ref[:, head * ROPE : (head + 1) * ROPE]
            raw = nt(nope, block) + mm(rope, tail[:ROPE])
            scores = jnp.where(allowed, raw, masked_score)
            peak = jnp.max(scores, axis=1, keepdims=True)
            if not first:
                old = top[head][:, :1]
                peak = jnp.maximum(old, peak)
                fade = jnp.exp2((old - peak) * exponent_scale)
            probs = jnp.exp2((scores - peak) * exponent_scale)
            mass = jnp.sum(probs, axis=1, keepdims=True)
            mixed = mm(probs.astype(jnp.bfloat16), block)
            if not first:
                mass = mass + denominator[head][:, :1] * fade
                mixed = mixed + accum[head] * fade
            top[head] = jnp.broadcast_to(peak, top.shape[1:])
            denominator[head] = jnp.broadcast_to(mass, denominator.shape[1:])
            accum[head] = mixed

    own_tail = jnp.concatenate([tail_ref[i] for i in range(KEY_PIECES)], axis=1)
    fold(latent_ref[...], own_tail, 0)

    def fold_pair(blocks):
        block = jnp.concatenate([keys[i, back] for i, back in blocks], axis=0)
        tail = jnp.concatenate([tails[i, back] for i, back in blocks], axis=1)
        fold(block, tail)

    def near_arrived(i):
        KeyCopy(0, i, False, mate).wait_recv()

    def far_arrived(i):
        KeyCopy(1, i, False, across).wait_recv()

    @pl.when(ctx == 1)
    def _():
        near_arrived(0)
        near_arrived(1)
        fold_pair(((0, 0), (1, 0)))

    @pl.when(ctx == 2)
    def _():
        for i in range(KEY_PIECES):
            far_arrived(i)
            near_arrived(i)
            fold_pair(((i, 0), (i, 1)))

    @pl.when(ctx == 3)
    def _():
        far_arrived(0)
        KeyCopy(0, 0, True, mate).start()
        near_arrived(0)
        near_arrived(1)
        fold_pair(((0, 0), (1, 0), (0, 1)))
        far_arrived(1)
        KeyCopy(0, 1, True, mate).start()
        fold(keys[1, 1], tails[1, 1])

    for load in loads:
        load.wait()
    for head in range(heads):
        context = (accum[head] / denominator[head][:, :1]).astype(jnp.bfloat16)
        values_ref[:, :, :, head * VDIM : (head + 1) * VDIM] = (
            mm(context, uv_ref[head])
            .astype(jnp.bfloat16)
            .reshape(NZ, NX, NY * TOK, VDIM)
        )

    def a_own(way, sub, chunk):
        rows = values_ref[chunk].reshape(NX * NY * TOK, values_ref.shape[3])
        start = (way * SUBS + sub) * wide_a
        return mm(rows, weight_ref[:, start : start + wide_a])

    def b_own(way, sub, chunk):
        rows = values_ref[:, chunk].reshape(NZ * NY * TOK, values_ref.shape[3])
        start = part_a + (way * SUBS + sub) * wide_b
        return mm(rows, weight_ref[:, start : start + wide_b])

    a_flight, b_flight, pushes = {}, {}, []

    def ring_step(step, here, count, own_of, first, slots, sems, onward, flight):
        for sub in range(SUBS):
            for way in range(2):
                sign = -1 if way == 0 else 1
                own = own_of(way, sub, (here + sign * (1 + step) + 2 * count) % count)
                if step == 0:
                    src = first.at[way, sub]
                    first[way, sub] = own.astype(jnp.bfloat16)
                else:
                    src = slots.at[way, sub, step - 1]
                    flight[way, sub, step - 1].wait_recv()
                    slots[way, sub, step - 1] = (
                        slots[way, sub, step - 1].astype(jnp.float32) + own
                    ).astype(jnp.bfloat16)
                flight[way, sub, step] = remote(
                    src,
                    slots.at[way, sub, step],
                    sems[0].at[way, sub, step],
                    sems[1].at[way, sub, step],
                    onward[way],
                )

    def a_step(step):
        ring_step(
            step, z, NZ, a_own, a_first, a_slots,
            (a_send_sem, a_recv_sem), z_next, a_flight,
        )

    def b_step(step):
        ring_step(
            step, x, NX, b_own, b_first, b_slots,
            (b_send_sem, b_recv_sem), x_next, b_flight,
        )

    def a_push_out():
        for sub in range(SUBS):
            for way in range(2):
                own = a_own(way, sub, z)
                a_flight[way, sub, NZ - 2].wait_recv()
                own = own + a_slots[way, sub, NZ - 2].astype(jnp.float32)
                start = (way * SUBS + sub) * wide_a
                a_push[:, :, start : start + wide_a] = own.reshape(
                    NQ, TOK, wide_a
                ).astype(jnp.bfloat16)
        for j in range(1, NQ):
            p = q_peers[j]
            pushes.append(
                remote(
                    a_push.at[p],
                    a_got.at[j - 1],
                    ap_send_sem.at[j - 1],
                    ap_recv_sem.at[j - 1],
                    at(z, p // NY, p % NY),
                )
            )

    b_cross = []

    def b_cross_out():
        for sub in range(SUBS):
            for way in range(2):
                k = way * SUBS + sub
                own = b_own(way, sub, x)
                b_flight[way, sub, NX - 2].wait_recv()
                own = own + b_slots[way, sub, NX - 2].astype(jnp.float32)
                own = own.reshape(NZ, NY, TOK, wide_b)
                for y_at in range(NY):
                    b_mid[k, y_at] = own[:, y_at].astype(jnp.bfloat16)
                b_cross.append(
                    (
                        k,
                        remote(
                            b_mid.at[k, 1 - y],
                            b_other.at[k],
                            bc_send_sem.at[k],
                            bc_recv_sem.at[k],
                            y_other,
                        ),
                    )
                )

    def b_push_out():
        for k, copy in b_cross:
            copy.wait_recv()
            own = b_mid[k, y].astype(jnp.float32) + b_other[k].astype(jnp.float32)
            b_push[:, :, k * wide_b : (k + 1) * wide_b] = own.astype(jnp.bfloat16)
        for j in (4, 3, 5, 2, 6, 1, 7):
            p = z_peers[j]
            pushes.append(
                remote(
                    b_push.at[p],
                    b_got.at[j - 1],
                    bp_send_sem.at[j - 1],
                    bp_recv_sem.at[j - 1],
                    at(p, x, y),
                )
            )

    a_step(0)
    b_step(0)
    a_step(1)
    a_step(2)
    b_step(1)
    a_step(3)
    b_step(2)
    a_step(4)
    b_cross_out()
    a_step(5)
    b_push_out()
    a_step(6)
    a_push_out()
    for copy in pushes:
        copy.wait_recv()
    total = b_push[z].astype(jnp.float32)
    for j in range(NZ - 1):
        total = total + b_got[j].astype(jnp.float32)
    out_ref[:, part_a:] = total
    total = a_push[q].astype(jnp.float32)
    for j in range(NQ - 1):
        total = total + a_got[j].astype(jnp.float32)
    out_ref[:, :part_a] = total
    crossed = [copy for _, copy in b_cross]
    for copy in [*a_flight.values(), *b_flight.values(), *crossed, *pushes]:
        copy.wait_send()
    for i in range(KEY_PIECES):

        @pl.when(y_lo == 0)
        def _():
            KeyCopy(1, i, False, across).wait_send()

        @pl.when((core == 0) | (y_lo == 1))
        def _():
            KeyCopy(0, i, False, mate).wait_send()


def attend_scratch(latent, uv_weight, weight, part_a):
    heads, lat = uv_weight.shape[:2]
    rows = latent.shape[0]
    width = weight.shape[1]
    part_b = width - part_a
    wide_a, wide_b = part_a // (2 * SUBS), part_b // (2 * SUBS)
    bf16 = jnp.bfloat16
    dma = pltpu.SemaphoreType.DMA
    return [
            pltpu.VMEM(uv_weight.shape, bf16),
            pltpu.VMEM(weight.shape, bf16),
            pltpu.VMEM((heads, rows, lat), bf16),
            pltpu.VMEM((KEY_PIECES, ROPE + DOC_ROWS, rows // KEY_PIECES), bf16),
            pltpu.VMEM((KEY_PIECES, 2, rows // KEY_PIECES, lat), bf16),
            pltpu.VMEM((KEY_PIECES, 2, ROPE + DOC_ROWS, rows // KEY_PIECES), bf16),
            pltpu.VMEM((heads, rows, 128), jnp.float32),
            pltpu.VMEM((heads, rows, 128), jnp.float32),
            pltpu.VMEM((heads, rows, lat), jnp.float32),
            pltpu.VMEM((NZ, NX, NY * TOK, heads * VDIM), bf16),
            pltpu.VMEM((2, SUBS, NQ * TOK, wide_a), bf16),
            pltpu.VMEM((2, SUBS, NZ - 1, NQ * TOK, wide_a), bf16),
            pltpu.VMEM((2, SUBS, NR * TOK, wide_b), bf16),
            pltpu.VMEM((2, SUBS, NX - 1, NR * TOK, wide_b), bf16),
            pltpu.VMEM((NQ, TOK, part_a), bf16),
            pltpu.VMEM((NQ - 1, TOK, part_a), bf16),
            pltpu.VMEM((2 * SUBS, NY, NZ, TOK, wide_b), bf16),
            pltpu.VMEM((2 * SUBS, NZ, TOK, wide_b), bf16),
            pltpu.VMEM((NZ, TOK, part_b), bf16),
            pltpu.VMEM((NZ - 1, TOK, part_b), bf16),
            dma((2, KEY_PIECES)),
            dma((2, KEY_PIECES)),
            dma((2, KEY_PIECES)),
            dma((2, KEY_PIECES)),
            dma((2, SUBS, NZ - 1)),
            dma((2, SUBS, NZ - 1)),
            dma((2, SUBS, NX - 1)),
            dma((2, SUBS, NX - 1)),
            dma((NQ - 1,)),
            dma((NQ - 1,)),
            dma((NZ - 1,)),
            dma((NZ - 1,)),
            dma((2 * SUBS,)),
            dma((2 * SUBS,)),
            dma((2,)),
    ]


def expert_loads(gate_hbm, up_hbm, down_hbm, gate_ref, up_ref, down_ref, load_sem):
    return [
        pltpu.make_async_copy(gate_hbm, gate_ref, load_sem.at[0]),
        pltpu.make_async_copy(up_hbm, up_ref, load_sem.at[1]),
        pltpu.make_async_copy(down_hbm, down_ref, load_sem.at[2]),
    ]


def experts_kernel(
    rows_ref,
    gate_hbm,
    up_hbm,
    down_hbm,
    out_ref,
    hist_ref,
    gate_ref,
    up_ref,
    down_ref,
    near,
    weigh,
    slots,
    inbox,
    kept,
    to_mate,
    from_mate,
    back,
    returned,
    to_y,
    from_y,
    own,
    to_z,
    from_z,
    hist_out,
    hist_in,
    load_sem,
    z_send,
    z_recv,
    y_send,
    y_recv,
    q_send,
    q_recv,
    m_send,
    m_recv,
    o_send,
    o_recv,
    b_send,
    b_recv,
    ys_send,
    ys_recv,
    zs_send,
    zs_recv,
    h_send,
    h_recv,
):
    width = down_hbm.shape[1]
    sent = width + 2 * N_EXPERTS
    half_rows, half_slots = NZ * TOK, NQ * NZ * CAP
    piece = NZ * CAP
    ctx, me = lax.axis_index("ctx"), lax.axis_index("exp")
    y_lo, core = ctx // 2, ctx % 2
    z, q = me // NQ, me % NQ

    def z_peer(z_at):
        return {"ctx": ctx, "exp": z_at * NQ + q}

    def q_peer(q_at):
        return {"ctx": ctx, "exp": z * NQ + q_at}

    y_peer = {"ctx": (1 - y_lo) * 2 + core, "exp": me}
    mate = {"ctx": y_lo * 2 + 1 - core, "exp": me}

    def c_peer(j):
        return {"ctx": (ctx + j) % N_CTX, "exp": me}

    loads = expert_loads(
        gate_hbm, up_hbm, down_hbm, gate_ref, up_ref, down_ref, load_sem
    )
    pending = []

    order = (4, 3, 5, 2, 6, 1, 7)
    near[y_lo, z] = rows_ref[...]
    hops = NZ // 2
    middle = rows_ref.shape[1] // 2
    onward = (z_peer((z + 1) % NZ), z_peer((z + NZ - 1) % NZ))
    ring = {}

    def pass_on(way, step, src, dst):
        ring[way, step] = remote(
            src, dst, z_send.at[way, step], z_recv.at[way, step], onward[way]
        )
        pending.append(ring[way, step])

    crossings = []

    def cross(src, dst):
        n = len(crossings)
        crossings.append(remote(src, dst, y_send.at[n], y_recv.at[n], y_peer))

    for way in range(2):
        pass_on(way, 0, rows_ref, near.at[y_lo, z])
    cross(rows_ref, near.at[y_lo, z])
    for step in range(1, hops):
        for way in range(2):
            z_from = (z + (NZ - step if way == 0 else step)) % NZ
            ring[way, step - 1].wait_recv()
            held = near.at[y_lo, z_from]
            if step < hops - 1:
                pass_on(way, step, held, held)
            else:
                side = pl.ds(way * middle, middle)
                part = near.at[y_lo, z_from, :, side]
                pass_on(way, step, part, part)
            cross(held, held)
    for way in range(2):
        ring[way, hops - 1].wait_recv()
    held = near.at[y_lo, (z + hops) % NZ]
    cross(held, held)
    pending += crossings

    lane = lax.broadcasted_iota(jnp.int32, (2 * N_EXPERTS, half_slots), 0)
    wanted = z * NQ + (
        lax.broadcasted_iota(jnp.int32, (2 * N_EXPERTS, half_slots), 1) // piece
    )
    pick_level, pick_rank = small(lane == wanted), small(lane == wanted + N_EXPERTS)
    row = lax.broadcasted_iota(jnp.int32, (half_rows, half_slots), 0)
    col = lax.broadcasted_iota(jnp.int32, (half_rows, half_slots), 1)
    same_source = (row // TOK) == ((col // CAP) % NZ)
    slot_rank = (col % CAP).astype(jnp.float32)

    q_order = (1, 2, 3, 4, 5, 6, 7)
    slot_flight = {}
    for half in range(2):
        if half == 1:
            for copy in crossings:
                copy.wait_recv()
        y_at = y_lo if half == 0 else 1 - y_lo
        held = (
            near[y_at]
            .astype(jnp.float32)
            .reshape(half_rows, sent + 2 * N_EXPERTS)
            .astype(jnp.bfloat16)
        )
        route = held[:, sent:]
        level, rank = mm(route, pick_level), mm(route, pick_rank)
        chosen = (level > 0.5) & (rank == slot_rank) & same_source
        weigh[half] = jnp.where(chosen, level, 0.0).astype(jnp.bfloat16)
        picked = mm_t(small(chosen), held[:, :sent])
        slots[half] = picked.astype(jnp.bfloat16).reshape(NQ, piece, sent)
        for j in q_order:
            p = (q + j) % NQ
            slot_flight[half, j] = remote(
                slots.at[half, p],
                inbox.at[half, 0, q],
                q_send.at[half, j],
                q_recv.at[half, j],
                q_peer(p),
            )
        inbox[half, 0, q] = slots[half, q]
    pending += slot_flight.values()

    bin_lane = lax.broadcasted_iota(jnp.int32, (2 * half_slots, 2 * N_EXPERTS), 1)
    bins_at = bin_lane.astype(jnp.float32)

    def run_block(half):
        block = inbox[half].reshape(2 * half_slots, sent)
        x = block[:, :width]
        gate_part, up_part = mm(x, gate_ref[...]), mm(x, up_ref[...])
        activation = gate_part / (1.0 + jnp.exp(-gate_part)) * up_part
        energy = jnp.sum(activation * activation, axis=1, keepdims=True) * (1.0 / HID)
        tail = block[:, width:].astype(jnp.float32)
        high = jnp.sum(jnp.where(bin_lane == me, tail, 0.0), axis=1, keepdims=True)
        low = jnp.sum(
            jnp.where(bin_lane == me + N_EXPERTS, tail, 0.0), axis=1, keepdims=True
        )
        at_high = jnp.where(high == bins_at, energy, 0.0)
        at_low = small(low == bins_at)
        first, second, third = split3(at_high)
        hist = mm_t(first, at_low) + mm_t(second, at_low) + mm_t(third, at_low)
        return activation.astype(jnp.bfloat16), hist

    back_flight = {}

    def run_half(half):
        flight = []
        for j in (0,) + q_order:
            q_from = (q + NQ - j) % NQ
            if j:
                slot_flight[half, j].wait_recv()
            flight.append(
                remote(
                    inbox.at[half, 0, q_from],
                    inbox.at[half, 1, q_from],
                    m_send.at[half, j],
                    m_recv.at[half, j],
                    mate,
                )
            )
        for copy in flight:
            copy.wait_recv()
        if half == 0:
            for load in loads:
                load.wait()
        hidden, hist = run_block(half)
        to_mate[half] = (
            mm(hidden[half_slots:], down_ref[...])
            .astype(jnp.bfloat16)
            .reshape(NQ, piece, width)
        )
        swap = remote(
            to_mate.at[half], from_mate.at[half], o_send.at[half], o_recv.at[half], mate
        )
        kept[...] = mm(hidden[:half_slots], down_ref[...])
        swap.wait_recv()
        total = kept[...] + from_mate[half].reshape(half_slots, width).astype(
            jnp.float32
        )
        back[half] = total.astype(jnp.bfloat16).reshape(NQ, piece, width)
        for j in q_order:
            p = (q + j) % NQ
            back_flight[half, j] = remote(
                back.at[half, p],
                returned.at[half, q],
                b_send.at[half, j],
                b_recv.at[half, j],
                q_peer(p),
            )
        returned[half, q] = back[half, q]
        pending.extend(flight + [swap])
        return hist

    hist = run_half(0)
    more = run_half(1)

    hist_out[...] = (hist + more)[: N_CTX * 8].reshape(N_CTX, 8, 2 * N_EXPERTS)
    hist_flight = [
        remote(
            hist_out.at[(ctx + j) % N_CTX],
            hist_in.at[j - 1],
            h_send.at[j - 1],
            h_recv.at[j - 1],
            c_peer(j),
        )
        for j in range(1, N_CTX)
    ]
    pending += hist_flight

    pending += back_flight.values()

    def mixed(half):
        for j in q_order:
            back_flight[half, j].wait_recv()
        return mm(weigh[half], returned[half].reshape(half_slots, width))

    own[...] = mixed(0).reshape(NZ, TOK, width)
    to_y[...] = mixed(1).reshape(NZ, TOK, width).astype(jnp.bfloat16)
    y_flight = {}
    for j in order + (0,):
        z_to = (z + j) % NZ
        y_flight[j] = remote(
            to_y.at[z_to], from_y.at[z_to], ys_send.at[j], ys_recv.at[j], y_peer
        )
    pending += y_flight.values()
    z_flight = []
    for j in order + (0,):
        z_to = (z + j) % NZ
        y_flight[j].wait_recv()
        to_z[z_to] = (own[z_to] + from_y[z_to].astype(jnp.float32)).astype(jnp.bfloat16)
        if j:
            z_flight.append(
                remote(
                    to_z.at[z_to],
                    from_z.at[j - 1],
                    zs_send.at[j - 1],
                    zs_recv.at[j - 1],
                    z_peer(z_to),
                )
            )
    pending += z_flight
    for copy in hist_flight:
        copy.wait_recv()
    hist = hist_out[ctx]
    for j in range(N_CTX - 1):
        hist = hist + hist_in[j]
    hist_ref[...] = hist
    for copy in z_flight:
        copy.wait_recv()
    total = to_z[z].astype(jnp.float32)
    for j in range(NZ - 1):
        total = total + from_z[j].astype(jnp.float32)
    out_ref[...] = total
    for copy in pending:
        copy.wait_send()


def expert_scratch(gate, up, down):
    width = down.shape[1]
    sent = width + 2 * N_EXPERTS
    half_slots, piece = NQ * NZ * CAP, NZ * CAP
    bf16, f32 = jnp.bfloat16, jnp.float32
    dma = pltpu.SemaphoreType.DMA
    return [
            pltpu.VMEM(gate.shape, bf16),
            pltpu.VMEM(up.shape, bf16),
            pltpu.VMEM(down.shape, bf16),
            pltpu.VMEM((2, NZ, TOK, sent + 2 * N_EXPERTS), bf16),
            pltpu.VMEM((2, NZ * TOK, half_slots), bf16),
            pltpu.VMEM((2, NQ, piece, sent), bf16),
            pltpu.VMEM((2, 2, NQ, piece, sent), bf16),
            pltpu.VMEM((half_slots, width), f32),
            pltpu.VMEM((2, NQ, piece, width), bf16),
            pltpu.VMEM((2, NQ, piece, width), bf16),
            pltpu.VMEM((2, NQ, piece, width), bf16),
            pltpu.VMEM((2, NQ, piece, width), bf16),
            pltpu.VMEM((NZ, TOK, width), bf16),
            pltpu.VMEM((NZ, TOK, width), bf16),
            pltpu.VMEM((NZ, TOK, width), f32),
            pltpu.VMEM((NZ, TOK, width), bf16),
            pltpu.VMEM((NZ - 1, TOK, width), bf16),
            pltpu.VMEM((N_CTX, 8, 2 * N_EXPERTS), f32),
            pltpu.VMEM((N_CTX - 1, 8, 2 * N_EXPERTS), f32),
            dma((3,)),
            dma((2, NZ // 2)),
            dma((2, NZ // 2)),
            dma((NZ,)),
            dma((NZ,)),
            dma((2, NQ)),
            dma((2, NQ)),
            dma((2, NQ)),
            dma((2, NQ)),
            dma((2,)),
            dma((2,)),
            dma((2, NQ)),
            dma((2, NQ)),
            dma((NZ,)),
            dma((NZ,)),
            dma((NZ - 1,)),
            dma((NZ - 1,)),
            dma((N_CTX - 1,)),
            dma((N_CTX - 1,)),
    ]


def fill_lanes(ids_ref, levels_ref, bins_ref, rows_ref, width):
    expert = lax.broadcasted_iota(jnp.int32, (TOK, N_EXPERTS), 1)
    none = jnp.zeros((TOK, N_EXPERTS), jnp.int32)
    high, low, level, named = none, none, none, none
    for k in range(ids_ref.shape[1]):
        here = ids_ref[:, k : k + 1] == expert
        bins = bins_ref[:, k : k + 1]
        high = high + jnp.where(here, bins >> 6, 0)
        low = low + jnp.where(here, bins & 63, 0)
        level = level + jnp.where(here, levels_ref[:, k : k + 1], 0)
        named = named + jnp.where(here, 1, 0)
    row = lax.broadcasted_iota(jnp.int32, (TOK, N_EXPERTS), 0)
    rank = none
    for t in range(TOK - 1):
        rank = rank + jnp.where(row > t, named[t : t + 1], 0)
    for i, lanes in enumerate((high, low, level, rank)):
        rows_ref[:, width + i * N_EXPERTS : width + (i + 1) * N_EXPERTS] = lanes.astype(
            jnp.float32
        ).astype(jnp.bfloat16)


def layer_kernel(part_a, attend_count, *refs):
    attend_in, (residual, gain, ids, levels, bins), weights = (
        refs[:7],
        refs[7:12],
        refs[12:15],
    )
    state_out, mixture_out, hist_out = refs[15:18]
    attended, rows = refs[18:20]
    attend_refs = refs[20 : 20 + attend_count]
    expert_refs = refs[20 + attend_count :]
    for load in expert_loads(*weights, *expert_refs[:3], expert_refs[19]):
        load.start()
    width = residual.shape[1]
    fill_lanes(ids, levels, bins, rows, width)
    attend_sum_kernel(part_a, *attend_in, attended, *attend_refs)
    state = residual[...].astype(jnp.float32) + attended[...]
    state_out[...] = state
    mean = jnp.mean(state * state, axis=1, keepdims=True)
    rows[:, :width] = (state * lax.rsqrt(mean + norm_eps) * gain[...]).astype(
        jnp.bfloat16
    )
    experts_kernel(rows, *weights, mixture_out, hist_out, *expert_refs)


def run_layer(attend_in, uv_weight, weight, row_in, gate, up, down, part_a=2048):
    width = weight.shape[1]
    vmem = pl.BlockSpec(memory_space=pltpu.VMEM)
    hbm = pl.BlockSpec(memory_space=pltpu.HBM)
    attend_refs = attend_scratch(attend_in[2], uv_weight, weight, part_a)
    return pl.pallas_call(
        functools.partial(layer_kernel, part_a, len(attend_refs)),
        out_shape=(
            jax.ShapeDtypeStruct((TOK, width), jnp.float32),
            jax.ShapeDtypeStruct((TOK, width), jnp.float32),
            jax.ShapeDtypeStruct((8, 2 * N_EXPERTS), jnp.float32),
        ),
        in_specs=[vmem] * 5 + [hbm] * 2 + [vmem] * 5 + [hbm] * 3,
        out_specs=(vmem, vmem, vmem),
        scratch_shapes=[
            pltpu.VMEM((TOK, width), jnp.float32),
            pltpu.VMEM((TOK, width + 4 * N_EXPERTS), jnp.bfloat16),
            *attend_refs,
            *expert_scratch(gate, up, down),
        ],
        compiler_params=pltpu.CompilerParams(
            collective_id=0, has_side_effects=True, vmem_limit_bytes=60 << 20
        ),
        name="layer",
    )(*attend_in, uv_weight, weight, *row_in, gate, up, down)


def on_device(
    residual_in,
    norm_gain,
    q_nope,
    q_rope,
    latent,
    k_rope,
    doc_ids,
    uv_weight,
    out_weight,
    expert_ids,
    gate_levels,
    bin_ids,
    gate_weight,
    up_weight,
    down_weight,
):
    block_len = q_nope.shape[0]
    stream_state, mixture, hist = run_layer(
        (q_nope, q_rope, latent, k_rope.T, doc_ids.reshape(1, block_len)),
        uv_weight,
        out_weight,
        (residual_in, norm_gain[None], expert_ids, gate_levels, bin_ids),
        gate_weight[0],
        up_weight[0],
        down_weight[0],
    )
    scale = 1.0 / jnp.sum(gate_levels.astype(jnp.float32), axis=1, keepdims=True)
    layer_out = (stream_state + mixture * scale).astype(jnp.bfloat16)
    histogram = hist[:, : NBINS // 32].reshape(1, NBINS // N_CTX)
    return (layer_out, histogram)


def solution(mesh):
    return jax.shard_map(
        on_device,
        mesh=mesh,
        in_specs=(
            P(("ctx", "exp"), None),
            P(),
            P("ctx", "exp", None),
            P("ctx", "exp"),
            P("ctx", None),
            P("ctx", None),
            P("ctx"),
            P("exp", None, None),
            P("exp", None),
            P(("ctx", "exp"), None),
            P(("ctx", "exp"), None),
            P(("ctx", "exp"), None),
            P("exp", None, "ctx"),
            P("exp", None, "ctx"),
            P("exp", "ctx", None),
        ),
        out_specs=(P(("ctx", "exp"), None), P("exp", "ctx")),
        check_vma=False,
    )
```

```python
import functools
import math

import jax
import jax.numpy as jnp
from jax import lax
from jax.experimental import pallas as pl
from jax.experimental.pallas import tpu as pltpu
from jax.sharding import PartitionSpec as P

HID = 1024
NBINS = 2048


exponent_scale = 192.0 ** (-0.5) * math.log2(math.e)
norm_eps = 1e-06
masked_score = -1e30

NZ, NX, NY = 8, 4, 2
NQ = NX * NY
NR = NZ * NY
TOK = 8
CAP = 2
N_CTX = 4
N_EXPERTS = 64
ROPE = 64
VDIM = 128
DOC_ROWS = 16
KEY_PIECES = 2
SUBS = 2
MESH = pl.DeviceIdType.MESH


def remote(src, dst, send_sem, recv_sem, target):
    copy = pltpu.make_async_remote_copy(
        src_ref=src,
        dst_ref=dst,
        send_sem=send_sem,
        recv_sem=recv_sem,
        device_id=target,
        device_id_type=MESH,
    )
    copy.start()
    return copy


def greet(targets):
    barrier = pltpu.get_barrier_semaphore()
    for target in targets:
        pl.semaphore_signal(barrier, inc=1, device_id=target, device_id_type=MESH)
    pl.semaphore_wait(barrier, len(targets))


def small(cond):
    return cond.astype(jnp.float32).astype(jnp.bfloat16)


def split3(v):
    first = v.astype(jnp.bfloat16)
    rest = v - first.astype(jnp.float32)
    second = rest.astype(jnp.bfloat16)
    third = (rest - second.astype(jnp.float32)).astype(jnp.bfloat16)
    return first, second, third


def mm(a, b):
    return jnp.dot(a, b, preferred_element_type=jnp.float32)


def mm_t(a, b):
    return lax.dot_general(
        a, b, (((0,), (0,)), ((), ())), preferred_element_type=jnp.float32
    )


def attend_sum_kernel(
    part_a,
    query_ref,
    query_rope_ref,
    latent_ref,
    rope_ref,
    doc_ref,
    uv_hbm,
    weight_hbm,
    out_ref,
    uv_ref,
    weight_ref,
    nope_ref,
    tail_ref,
    keys,
    tails,
    top,
    denominator,
    accum,
    values_ref,
    a_first,
    a_slots,
    b_first,
    b_slots,
    a_push,
    a_got,
    b_mid,
    b_other,
    b_push,
    b_got,
    k_send_sem,
    k_recv_sem,
    t_send_sem,
    t_recv_sem,
    a_send_sem,
    a_recv_sem,
    b_send_sem,
    b_recv_sem,
    ap_send_sem,
    ap_recv_sem,
    bp_send_sem,
    bp_recv_sem,
    bc_send_sem,
    bc_recv_sem,
    load_sem,
):
    loads = [
        pltpu.make_async_copy(uv_hbm, uv_ref, load_sem.at[0]),
        pltpu.make_async_copy(weight_hbm, weight_ref, load_sem.at[1]),
    ]
    for load in loads:
        load.start()
    width = weight_ref.shape[1]
    wide_a, wide_b = part_a // (2 * SUBS), (width - part_a) // (2 * SUBS)
    me = lax.axis_index("exp")
    z, x, y = me // NQ, (me // NY) % NX, me % NY
    q = x * NY + y

    def at(z_at, x_at, y_at):
        return {"exp": (z_at * NX + x_at) * NY + y_at}

    q_peers = [(q + j) % NQ for j in range(NQ)]
    z_peers = [(z + j) % NZ for j in range(NZ)]
    y_other = at(z, x, 1 - y)
    z_next = [at((z + 1) % NZ, x, y), at((z + NZ - 1) % NZ, x, y)]
    x_next = [at(z, (x + 1) % NX, y), at(z, (x + NX - 1) % NX, y)]
    ctx = lax.axis_index("ctx")
    y_lo, core = ctx // 2, ctx % 2
    mate = {"ctx": y_lo * 2 + 1 - core, "exp": me}
    across = {"ctx": (1 - y_lo) * 2 + core, "exp": me}
    greet(
        [at(z, p // NY, p % NY) for p in q_peers[1:]]
        + [at(p, x, y) for p in z_peers[1:]]
        + [mate, across, {"ctx": 3 - ctx, "exp": me}]
    )

    block_len, lat = latent_ref.shape
    piece = block_len // KEY_PIECES
    for i in range(KEY_PIECES):
        tail_ref[i, :ROPE] = rope_ref[:, i * piece : (i + 1) * piece]
        tail_ref[i, ROPE:] = jnp.broadcast_to(
            doc_ref[:, i * piece : (i + 1) * piece].astype(jnp.float32),
            (DOC_ROWS, piece),
        ).astype(jnp.bfloat16)

    class KeyCopy:
        def __init__(self, back, i, forward, target):
            self.copies = [
                pltpu.make_async_remote_copy(
                    src_ref=src,
                    dst_ref=dst.at[i, back],
                    send_sem=send_sem.at[back, i],
                    recv_sem=recv_sem.at[back, i],
                    device_id=target,
                    device_id_type=MESH,
                )
                for src, dst, send_sem, recv_sem in (
                    (
                        keys.at[i, 1]
                        if forward
                        else latent_ref.at[i * piece : (i + 1) * piece],
                        keys,
                        k_send_sem,
                        k_recv_sem,
                    ),
                    (
                        tails.at[i, 1] if forward else tail_ref.at[i],
                        tails,
                        t_send_sem,
                        t_recv_sem,
                    ),
                )
            ]

        def start(self):
            for copy in self.copies:
                copy.start()

        def wait_recv(self):
            for copy in self.copies:
                copy.wait_recv()

        def wait_send(self):
            for copy in self.copies:
                copy.wait_send()

    for i in range(KEY_PIECES):

        @pl.when(y_lo == 0)
        def _():
            KeyCopy(1, i, False, across).start()

    for i in range(KEY_PIECES):

        @pl.when(core == 0)
        def _():
            KeyCopy(0, i, False, mate).start()

    def nt(a, b):
        return lax.dot_general(
            a, b, (((1,), (1,)), ((), ())), preferred_element_type=jnp.float32
        )

    heads = uv_ref.shape[0]
    part = block_len // 8

    def unpack(i, carry):
        here = pl.ds(pl.multiple_of(i * part, part), part)
        for head in range(heads):
            nope_ref[head, here] = query_ref[here, head]
        return carry

    lax.fori_loop(0, 8, unpack, 0)
    doc_pick = small(lax.broadcasted_iota(jnp.int32, (DOC_ROWS, 128), 0) == 0)
    query_docs = jnp.concatenate(
        [mm_t(tail_ref[i, ROPE:], doc_pick)[:, :1] for i in range(KEY_PIECES)], axis=0
    )

    def fold(block, tail, offset=None):
        first = offset == 0
        allowed = query_docs == tail[ROPE : ROPE + 1].astype(jnp.float32)
        if offset is not None:
            shape = (block_len, block.shape[0])
            query_at = lax.broadcasted_iota(jnp.int32, shape, 0)
            key_at = lax.broadcasted_iota(jnp.int32, shape, 1) + offset
            allowed = allowed & (key_at <= query_at)
        for head in range(heads):
            nope = nope_ref[head]
            rope = query_rope_ref[:, head * ROPE : (head + 1) * ROPE]
            raw = nt(nope, block) + mm(rope, tail[:ROPE])
            scores = jnp.where(allowed, raw, masked_score)
            peak = jnp.max(scores, axis=1, keepdims=True)
            if not first:
                old = top[head][:, :1]
                peak = jnp.maximum(old, peak)
                fade = jnp.exp2((old - peak) * exponent_scale)
            probs = jnp.exp2((scores - peak) * exponent_scale)
            mass = jnp.sum(probs, axis=1, keepdims=True)
            mixed = mm(probs.astype(jnp.bfloat16), block)
            if not first:
                mass = mass + denominator[head][:, :1] * fade
                mixed = mixed + accum[head] * fade
            top[head] = jnp.broadcast_to(peak, top.shape[1:])
            denominator[head] = jnp.broadcast_to(mass, denominator.shape[1:])
            accum[head] = mixed

    own_tail = jnp.concatenate([tail_ref[i] for i in range(KEY_PIECES)], axis=1)
    fold(latent_ref[...], own_tail, 0)

    def fold_pair(blocks):
        block = jnp.concatenate([keys[i, back] for i, back in blocks], axis=0)
        tail = jnp.concatenate([tails[i, back] for i, back in blocks], axis=1)
        fold(block, tail)

    def near_arrived(i):
        KeyCopy(0, i, False, mate).wait_recv()

    def far_arrived(i):
        KeyCopy(1, i, False, across).wait_recv()

    @pl.when(ctx == 1)
    def _():
        near_arrived(0)
        near_arrived(1)
        fold_pair(((0, 0), (1, 0)))

    @pl.when(ctx == 2)
    def _():
        for i in range(KEY_PIECES):
            far_arrived(i)
            near_arrived(i)
            fold_pair(((i, 0), (i, 1)))

    @pl.when(ctx == 3)
    def _():
        far_arrived(0)
        KeyCopy(0, 0, True, mate).start()
        near_arrived(0)
        near_arrived(1)
        fold_pair(((0, 0), (1, 0), (0, 1)))
        far_arrived(1)
        KeyCopy(0, 1, True, mate).start()
        fold(keys[1, 1], tails[1, 1])

    for load in loads:
        load.wait()
    for head in range(heads):
        context = (accum[head] / denominator[head][:, :1]).astype(jnp.bfloat16)
        values_ref[:, :, :, head * VDIM : (head + 1) * VDIM] = (
            mm(context, uv_ref[head])
            .astype(jnp.bfloat16)
            .reshape(NZ, NX, NY * TOK, VDIM)
        )

    def a_own(way, sub, chunk):
        rows = values_ref[chunk].reshape(NX * NY * TOK, values_ref.shape[3])
        start = (way * SUBS + sub) * wide_a
        return mm(rows, weight_ref[:, start : start + wide_a])

    def b_own(way, sub, chunk):
        rows = values_ref[:, chunk].reshape(NZ * NY * TOK, values_ref.shape[3])
        start = part_a + (way * SUBS + sub) * wide_b
        return mm(rows, weight_ref[:, start : start + wide_b])

    a_flight, b_flight, pushes = {}, {}, []

    def ring_step(step, here, count, own_of, first, slots, sems, onward, flight):
        for sub in range(SUBS):
            for way in range(2):
                sign = -1 if way == 0 else 1
                own = own_of(way, sub, (here + sign * (1 + step) + 2 * count) % count)
                if step == 0:
                    src = first.at[way, sub]
                    first[way, sub] = own.astype(jnp.bfloat16)
                else:
                    src = slots.at[way, sub, step - 1]
                    flight[way, sub, step - 1].wait_recv()
                    slots[way, sub, step - 1] = (
                        slots[way, sub, step - 1].astype(jnp.float32) + own
                    ).astype(jnp.bfloat16)
                flight[way, sub, step] = remote(
                    src,
                    slots.at[way, sub, step],
                    sems[0].at[way, sub, step],
                    sems[1].at[way, sub, step],
                    onward[way],
                )

    def a_step(step):
        ring_step(
            step, z, NZ, a_own, a_first, a_slots,
            (a_send_sem, a_recv_sem), z_next, a_flight,
        )

    def b_step(step):
        ring_step(
            step, x, NX, b_own, b_first, b_slots,
            (b_send_sem, b_recv_sem), x_next, b_flight,
        )

    def a_push_out():
        for sub in range(SUBS):
            for way in range(2):
                own = a_own(way, sub, z)
                a_flight[way, sub, NZ - 2].wait_recv()
                own = own + a_slots[way, sub, NZ - 2].astype(jnp.float32)
                start = (way * SUBS + sub) * wide_a
                a_push[:, :, start : start + wide_a] = own.reshape(
                    NQ, TOK, wide_a
                ).astype(jnp.bfloat16)
        for j in range(1, NQ):
            p = q_peers[j]
            pushes.append(
                remote(
                    a_push.at[p],
                    a_got.at[j - 1],
                    ap_send_sem.at[j - 1],
                    ap_recv_sem.at[j - 1],
                    at(z, p // NY, p % NY),
                )
            )

    b_cross = []

    def b_cross_out():
        for sub in range(SUBS):
            for way in range(2):
                k = way * SUBS + sub
                own = b_own(way, sub, x)
                b_flight[way, sub, NX - 2].wait_recv()
                own = own + b_slots[way, sub, NX - 2].astype(jnp.float32)
                own = own.reshape(NZ, NY, TOK, wide_b)
                for y_at in range(NY):
                    b_mid[k, y_at] = own[:, y_at].astype(jnp.bfloat16)
                b_cross.append(
                    (
                        k,
                        remote(
                            b_mid.at[k, 1 - y],
                            b_other.at[k],
                            bc_send_sem.at[k],
                            bc_recv_sem.at[k],
                            y_other,
                        ),
                    )
                )

    def b_push_out():
        for k, copy in b_cross:
            copy.wait_recv()
            own = b_mid[k, y].astype(jnp.float32) + b_other[k].astype(jnp.float32)
            b_push[:, :, k * wide_b : (k + 1) * wide_b] = own.astype(jnp.bfloat16)
        for j in (4, 3, 5, 2, 6, 1, 7):
            p = z_peers[j]
            pushes.append(
                remote(
                    b_push.at[p],
                    b_got.at[j - 1],
                    bp_send_sem.at[j - 1],
                    bp_recv_sem.at[j - 1],
                    at(p, x, y),
                )
            )

    a_step(0)
    b_step(0)
    a_step(1)
    a_step(2)
    b_step(1)
    a_step(3)
    b_step(2)
    a_step(4)
    b_cross_out()
    a_step(5)
    b_push_out()
    a_step(6)
    a_push_out()
    for copy in pushes:
        copy.wait_recv()
    total = b_push[z].astype(jnp.float32)
    for j in range(NZ - 1):
        total = total + b_got[j].astype(jnp.float32)
    out_ref[:, part_a:] = total
    total = a_push[q].astype(jnp.float32)
    for j in range(NQ - 1):
        total = total + a_got[j].astype(jnp.float32)
    out_ref[:, :part_a] = total
    crossed = [copy for _, copy in b_cross]
    for copy in [*a_flight.values(), *b_flight.values(), *crossed, *pushes]:
        copy.wait_send()
    for i in range(KEY_PIECES):

        @pl.when(y_lo == 0)
        def _():
            KeyCopy(1, i, False, across).wait_send()

        @pl.when((core == 0) | (y_lo == 1))
        def _():
            KeyCopy(0, i, False, mate).wait_send()


def attend_scratch(latent, uv_weight, weight, part_a):
    heads, lat = uv_weight.shape[:2]
    rows = latent.shape[0]
    width = weight.shape[1]
    part_b = width - part_a
    wide_a, wide_b = part_a // (2 * SUBS), part_b // (2 * SUBS)
    bf16 = jnp.bfloat16
    dma = pltpu.SemaphoreType.DMA
    return [
            pltpu.VMEM(uv_weight.shape, bf16),
            pltpu.VMEM(weight.shape, bf16),
            pltpu.VMEM((heads, rows, lat), bf16),
            pltpu.VMEM((KEY_PIECES, ROPE + DOC_ROWS, rows // KEY_PIECES), bf16),
            pltpu.VMEM((KEY_PIECES, 2, rows // KEY_PIECES, lat), bf16),
            pltpu.VMEM((KEY_PIECES, 2, ROPE + DOC_ROWS, rows // KEY_PIECES), bf16),
            pltpu.VMEM((heads, rows, 128), jnp.float32),
            pltpu.VMEM((heads, rows, 128), jnp.float32),
            pltpu.VMEM((heads, rows, lat), jnp.float32),
            pltpu.VMEM((NZ, NX, NY * TOK, heads * VDIM), bf16),
            pltpu.VMEM((2, SUBS, NQ * TOK, wide_a), bf16),
            pltpu.VMEM((2, SUBS, NZ - 1, NQ * TOK, wide_a), bf16),
            pltpu.VMEM((2, SUBS, NR * TOK, wide_b), bf16),
            pltpu.VMEM((2, SUBS, NX - 1, NR * TOK, wide_b), bf16),
            pltpu.VMEM((NQ, TOK, part_a), bf16),
            pltpu.VMEM((NQ - 1, TOK, part_a), bf16),
            pltpu.VMEM((2 * SUBS, NY, NZ, TOK, wide_b), bf16),
            pltpu.VMEM((2 * SUBS, NZ, TOK, wide_b), bf16),
            pltpu.VMEM((NZ, TOK, part_b), bf16),
            pltpu.VMEM((NZ - 1, TOK, part_b), bf16),
            dma((2, KEY_PIECES)),
            dma((2, KEY_PIECES)),
            dma((2, KEY_PIECES)),
            dma((2, KEY_PIECES)),
            dma((2, SUBS, NZ - 1)),
            dma((2, SUBS, NZ - 1)),
            dma((2, SUBS, NX - 1)),
            dma((2, SUBS, NX - 1)),
            dma((NQ - 1,)),
            dma((NQ - 1,)),
            dma((NZ - 1,)),
            dma((NZ - 1,)),
            dma((2 * SUBS,)),
            dma((2 * SUBS,)),
            dma((2,)),
    ]


def expert_loads(gate_hbm, up_hbm, down_hbm, gate_ref, up_ref, down_ref, load_sem):
    return [
        pltpu.make_async_copy(gate_hbm, gate_ref, load_sem.at[0]),
        pltpu.make_async_copy(up_hbm, up_ref, load_sem.at[1]),
        pltpu.make_async_copy(down_hbm, down_ref, load_sem.at[2]),
    ]


def experts_kernel(
    rows_ref,
    gate_hbm,
    up_hbm,
    down_hbm,
    out_ref,
    hist_ref,
    gate_ref,
    up_ref,
    down_ref,
    near,
    weigh,
    slots,
    inbox,
    kept,
    to_mate,
    from_mate,
    back,
    returned,
    to_y,
    from_y,
    own,
    to_z,
    from_z,
    hist_out,
    hist_in,
    load_sem,
    z_send,
    z_recv,
    y_send,
    y_recv,
    q_send,
    q_recv,
    m_send,
    m_recv,
    o_send,
    o_recv,
    b_send,
    b_recv,
    ys_send,
    ys_recv,
    zs_send,
    zs_recv,
    h_send,
    h_recv,
):
    width = down_hbm.shape[1]
    sent = width + 2 * N_EXPERTS
    half_rows, half_slots = NZ * TOK, NQ * NZ * CAP
    piece = NZ * CAP
    ctx, me = lax.axis_index("ctx"), lax.axis_index("exp")
    y_lo, core = ctx // 2, ctx % 2
    z, q = me // NQ, me % NQ

    def z_peer(z_at):
        return {"ctx": ctx, "exp": z_at * NQ + q}

    def q_peer(q_at):
        return {"ctx": ctx, "exp": z * NQ + q_at}

    y_peer = {"ctx": (1 - y_lo) * 2 + core, "exp": me}
    mate = {"ctx": y_lo * 2 + 1 - core, "exp": me}

    def c_peer(j):
        return {"ctx": (ctx + j) % N_CTX, "exp": me}

    loads = expert_loads(
        gate_hbm, up_hbm, down_hbm, gate_ref, up_ref, down_ref, load_sem
    )
    pending = []

    order = (4, 3, 5, 2, 6, 1, 7)
    near[y_lo, z] = rows_ref[...]
    hops = NZ // 2
    middle = rows_ref.shape[1] // 2
    onward = (z_peer((z + 1) % NZ), z_peer((z + NZ - 1) % NZ))
    ring = {}

    def pass_on(way, step, src, dst):
        ring[way, step] = remote(
            src, dst, z_send.at[way, step], z_recv.at[way, step], onward[way]
        )
        pending.append(ring[way, step])

    crossings = []

    def cross(src, dst):
        n = len(crossings)
        crossings.append(remote(src, dst, y_send.at[n], y_recv.at[n], y_peer))

    for way in range(2):
        pass_on(way, 0, rows_ref, near.at[y_lo, z])
    cross(rows_ref, near.at[y_lo, z])
    for step in range(1, hops):
        for way in range(2):
            z_from = (z + (NZ - step if way == 0 else step)) % NZ
            ring[way, step - 1].wait_recv()
            held = near.at[y_lo, z_from]
            if step < hops - 1:
                pass_on(way, step, held, held)
            else:
                side = pl.ds(way * middle, middle)
                part = near.at[y_lo, z_from, :, side]
                pass_on(way, step, part, part)
            cross(held, held)
    for way in range(2):
        ring[way, hops - 1].wait_recv()
    held = near.at[y_lo, (z + hops) % NZ]
    cross(held, held)
    pending += crossings

    lane = lax.broadcasted_iota(jnp.int32, (2 * N_EXPERTS, half_slots), 0)
    wanted = z * NQ + (
        lax.broadcasted_iota(jnp.int32, (2 * N_EXPERTS, half_slots), 1) // piece
    )
    pick_level, pick_rank = small(lane == wanted), small(lane == wanted + N_EXPERTS)
    row = lax.broadcasted_iota(jnp.int32, (half_rows, half_slots), 0)
    col = lax.broadcasted_iota(jnp.int32, (half_rows, half_slots), 1)
    same_source = (row // TOK) == ((col // CAP) % NZ)
    slot_rank = (col % CAP).astype(jnp.float32)

    q_order = (1, 2, 3, 4, 5, 6, 7)
    slot_flight = {}
    for half in range(2):
        if half == 1:
            for copy in crossings:
                copy.wait_recv()
        y_at = y_lo if half == 0 else 1 - y_lo
        held = (
            near[y_at]
            .astype(jnp.float32)
            .reshape(half_rows, sent + 2 * N_EXPERTS)
            .astype(jnp.bfloat16)
        )
        route = held[:, sent:]
        level, rank = mm(route, pick_level), mm(route, pick_rank)
        chosen = (level > 0.5) & (rank == slot_rank) & same_source
        weigh[half] = jnp.where(chosen, level, 0.0).astype(jnp.bfloat16)
        picked = mm_t(small(chosen), held[:, :sent])
        slots[half] = picked.astype(jnp.bfloat16).reshape(NQ, piece, sent)
        for j in q_order:
            p = (q + j) % NQ
            slot_flight[half, j] = remote(
                slots.at[half, p],
                inbox.at[half, 0, q],
                q_send.at[half, j],
                q_recv.at[half, j],
                q_peer(p),
            )
        inbox[half, 0, q] = slots[half, q]
    pending += slot_flight.values()

    bin_lane = lax.broadcasted_iota(jnp.int32, (2 * half_slots, 2 * N_EXPERTS), 1)
    bins_at = bin_lane.astype(jnp.float32)

    def run_block(half):
        block = inbox[half].reshape(2 * half_slots, sent)
        x = block[:, :width]
        gate_part, up_part = mm(x, gate_ref[...]), mm(x, up_ref[...])
        activation = gate_part / (1.0 + jnp.exp(-gate_part)) * up_part
        energy = jnp.sum(activation * activation, axis=1, keepdims=True) * (1.0 / HID)
        tail = block[:, width:].astype(jnp.float32)
        high = jnp.sum(jnp.where(bin_lane == me, tail, 0.0), axis=1, keepdims=True)
        low = jnp.sum(
            jnp.where(bin_lane == me + N_EXPERTS, tail, 0.0), axis=1, keepdims=True
        )
        at_high = jnp.where(high == bins_at, energy, 0.0)
        at_low = small(low == bins_at)
        first, second, third = split3(at_high)
        hist = mm_t(first, at_low) + mm_t(second, at_low) + mm_t(third, at_low)
        return activation.astype(jnp.bfloat16), hist

    back_flight = {}

    def run_half(half):
        flight = []
        for j in (0,) + q_order:
            q_from = (q + NQ - j) % NQ
            if j:
                slot_flight[half, j].wait_recv()
            flight.append(
                remote(
                    inbox.at[half, 0, q_from],
                    inbox.at[half, 1, q_from],
                    m_send.at[half, j],
                    m_recv.at[half, j],
                    mate,
                )
            )
        for copy in flight:
            copy.wait_recv()
        if half == 0:
            for load in loads:
                load.wait()
        hidden, hist = run_block(half)
        to_mate[half] = (
            mm(hidden[half_slots:], down_ref[...])
            .astype(jnp.bfloat16)
            .reshape(NQ, piece, width)
        )
        swap = remote(
            to_mate.at[half], from_mate.at[half], o_send.at[half], o_recv.at[half], mate
        )
        kept[...] = mm(hidden[:half_slots], down_ref[...])
        swap.wait_recv()
        total = kept[...] + from_mate[half].reshape(half_slots, width).astype(
            jnp.float32
        )
        back[half] = total.astype(jnp.bfloat16).reshape(NQ, piece, width)
        for j in q_order:
            p = (q + j) % NQ
            back_flight[half, j] = remote(
                back.at[half, p],
                returned.at[half, q],
                b_send.at[half, j],
                b_recv.at[half, j],
                q_peer(p),
            )
        returned[half, q] = back[half, q]
        pending.extend(flight + [swap])
        return hist

    hist = run_half(0)
    more = run_half(1)

    hist_out[...] = (hist + more)[: N_CTX * 8].reshape(N_CTX, 8, 2 * N_EXPERTS)
    hist_flight = [
        remote(
            hist_out.at[(ctx + j) % N_CTX],
            hist_in.at[j - 1],
            h_send.at[j - 1],
            h_recv.at[j - 1],
            c_peer(j),
        )
        for j in range(1, N_CTX)
    ]
    pending += hist_flight

    pending += back_flight.values()

    def mixed(half):
        for j in q_order:
            back_flight[half, j].wait_recv()
        return mm(weigh[half], returned[half].reshape(half_slots, width))

    own[...] = mixed(0).reshape(NZ, TOK, width)
    to_y[...] = mixed(1).reshape(NZ, TOK, width).astype(jnp.bfloat16)
    y_flight = {}
    for j in order + (0,):
        z_to = (z + j) % NZ
        y_flight[j] = remote(
            to_y.at[z_to], from_y.at[z_to], ys_send.at[j], ys_recv.at[j], y_peer
        )
    pending += y_flight.values()
    z_flight = []
    for j in order + (0,):
        z_to = (z + j) % NZ
        y_flight[j].wait_recv()
        to_z[z_to] = (own[z_to] + from_y[z_to].astype(jnp.float32)).astype(jnp.bfloat16)
        if j:
            z_flight.append(
                remote(
                    to_z.at[z_to],
                    from_z.at[j - 1],
                    zs_send.at[j - 1],
                    zs_recv.at[j - 1],
                    z_peer(z_to),
                )
            )
    pending += z_flight
    for copy in hist_flight:
        copy.wait_recv()
    hist = hist_out[ctx]
    for j in range(N_CTX - 1):
        hist = hist + hist_in[j]
    hist_ref[...] = hist
    for copy in z_flight:
        copy.wait_recv()
    total = to_z[z].astype(jnp.float32)
    for j in range(NZ - 1):
        total = total + from_z[j].astype(jnp.float32)
    out_ref[...] = total
    for copy in pending:
        copy.wait_send()


def expert_scratch(gate, up, down):
    width = down.shape[1]
    sent = width + 2 * N_EXPERTS
    half_slots, piece = NQ * NZ * CAP, NZ * CAP
    bf16, f32 = jnp.bfloat16, jnp.float32
    dma = pltpu.SemaphoreType.DMA
    return [
            pltpu.VMEM(gate.shape, bf16),
            pltpu.VMEM(up.shape, bf16),
            pltpu.VMEM(down.shape, bf16),
            pltpu.VMEM((2, NZ, TOK, sent + 2 * N_EXPERTS), bf16),
            pltpu.VMEM((2, NZ * TOK, half_slots), bf16),
            pltpu.VMEM((2, NQ, piece, sent), bf16),
            pltpu.VMEM((2, 2, NQ, piece, sent), bf16),
            pltpu.VMEM((half_slots, width), f32),
            pltpu.VMEM((2, NQ, piece, width), bf16),
            pltpu.VMEM((2, NQ, piece, width), bf16),
            pltpu.VMEM((2, NQ, piece, width), bf16),
            pltpu.VMEM((2, NQ, piece, width), bf16),
            pltpu.VMEM((NZ, TOK, width), bf16),
            pltpu.VMEM((NZ, TOK, width), bf16),
            pltpu.VMEM((NZ, TOK, width), f32),
            pltpu.VMEM((NZ, TOK, width), bf16),
            pltpu.VMEM((NZ - 1, TOK, width), bf16),
            pltpu.VMEM((N_CTX, 8, 2 * N_EXPERTS), f32),
            pltpu.VMEM((N_CTX - 1, 8, 2 * N_EXPERTS), f32),
            dma((3,)),
            dma((2, NZ // 2)),
            dma((2, NZ // 2)),
            dma((NZ,)),
            dma((NZ,)),
            dma((2, NQ)),
            dma((2, NQ)),
            dma((2, NQ)),
            dma((2, NQ)),
            dma((2,)),
            dma((2,)),
            dma((2, NQ)),
            dma((2, NQ)),
            dma((NZ,)),
            dma((NZ,)),
            dma((NZ - 1,)),
            dma((NZ - 1,)),
            dma((N_CTX - 1,)),
            dma((N_CTX - 1,)),
    ]


def fill_lanes(ids_ref, levels_ref, bins_ref, rows_ref, width):
    expert = lax.broadcasted_iota(jnp.int32, (TOK, N_EXPERTS), 1)
    none = jnp.zeros((TOK, N_EXPERTS), jnp.int32)
    high, low, level, named = none, none, none, none
    for k in range(ids_ref.shape[1]):
        here = ids_ref[:, k : k + 1] == expert
        bins = bins_ref[:, k : k + 1]
        high = high + jnp.where(here, bins >> 6, 0)
        low = low + jnp.where(here, bins & 63, 0)
        level = level + jnp.where(here, levels_ref[:, k : k + 1], 0)
        named = named + jnp.where(here, 1, 0)
    row = lax.broadcasted_iota(jnp.int32, (TOK, N_EXPERTS), 0)
    rank = none
    for t in range(TOK - 1):
        rank = rank + jnp.where(row > t, named[t : t + 1], 0)
    for i, lanes in enumerate((high, low, level, rank)):
        rows_ref[:, width + i * N_EXPERTS : width + (i + 1) * N_EXPERTS] = lanes.astype(
            jnp.float32
        ).astype(jnp.bfloat16)


def layer_kernel(part_a, attend_count, *refs):
    attend_in, (residual, gain, ids, levels, bins), weights = (
        refs[:7],
        refs[7:12],
        refs[12:15],
    )
    layer_out, hist_out = refs[15:17]
    attended, mixture, rows = refs[17:20]
    attend_refs = refs[20 : 20 + attend_count]
    expert_refs = refs[20 + attend_count :]
    for load in expert_loads(*weights, *expert_refs[:3], expert_refs[19]):
        load.start()
    width = residual.shape[1]
    fill_lanes(ids, levels, bins, rows, width)
    attend_sum_kernel(part_a, *attend_in, attended, *attend_refs)
    state = residual[...].astype(jnp.float32) + attended[...]
    attended[...] = state
    mean = jnp.mean(state * state, axis=1, keepdims=True)
    rows[:, :width] = (state * lax.rsqrt(mean + norm_eps) * gain[...][None]).astype(
        jnp.bfloat16
    )
    experts_kernel(rows, *weights, mixture, hist_out, *expert_refs)
    total = jnp.sum(levels[...].astype(jnp.float32), axis=1, keepdims=True)
    layer_out[...] = attended[...] + mixture[...] / total


def run_layer(attend_in, uv_weight, weight, row_in, gate, up, down, part_a=2048):
    width = weight.shape[1]
    vmem = pl.BlockSpec(memory_space=pltpu.VMEM)
    hbm = pl.BlockSpec(memory_space=pltpu.HBM)
    attend_refs = attend_scratch(attend_in[2], uv_weight, weight, part_a)
    return pl.pallas_call(
        functools.partial(layer_kernel, part_a, len(attend_refs)),
        out_shape=(
            jax.ShapeDtypeStruct((TOK, width), jnp.float32),
            jax.ShapeDtypeStruct((8, 2 * N_EXPERTS), jnp.float32),
        ),
        in_specs=[vmem] * 5 + [hbm] * 2 + [vmem] * 5 + [hbm] * 3,
        out_specs=(vmem, vmem),
        scratch_shapes=[
            pltpu.VMEM((TOK, width), jnp.float32),
            pltpu.VMEM((TOK, width), jnp.float32),
            pltpu.VMEM((TOK, width + 4 * N_EXPERTS), jnp.bfloat16),
            *attend_refs,
            *expert_scratch(gate, up, down),
        ],
        compiler_params=pltpu.CompilerParams(
            collective_id=0, has_side_effects=True, vmem_limit_bytes=60 << 20
        ),
        name="layer",
    )(*attend_in, uv_weight, weight, *row_in, gate, up, down)


def on_device(
    residual_in,
    norm_gain,
    q_nope,
    q_rope,
    latent,
    k_rope,
    doc_ids,
    uv_weight,
    out_weight,
    expert_ids,
    gate_levels,
    bin_ids,
    gate_weight,
    up_weight,
    down_weight,
):
    block_len = q_nope.shape[0]
    layer_out, hist = run_layer(
        (q_nope, q_rope, latent, k_rope.T, doc_ids.reshape(1, block_len)),
        uv_weight,
        out_weight,
        (residual_in, norm_gain, expert_ids, gate_levels, bin_ids),
        gate_weight[0],
        up_weight[0],
        down_weight[0],
    )
    layer_out = layer_out.astype(jnp.bfloat16)
    histogram = hist[:, : NBINS // 32].reshape(1, NBINS // N_CTX)
    return (layer_out, histogram)


def solution(mesh):
    return jax.shard_map(
        on_device,
        mesh=mesh,
        in_specs=(
            P(("ctx", "exp"), None),
            P(),
            P("ctx", "exp", None),
            P("ctx", "exp"),
            P("ctx", None),
            P("ctx", None),
            P("ctx"),
            P("exp", None, None),
            P("exp", None),
            P(("ctx", "exp"), None),
            P(("ctx", "exp"), None),
            P(("ctx", "exp"), None),
            P("exp", None, "ctx"),
            P("exp", None, "ctx"),
            P("exp", "ctx", None),
        ),
        out_specs=(P(("ctx", "exp"), None), P("exp", "ctx")),
        check_vma=False,
    )
```

```python
import functools
import math

import jax
import jax.numpy as jnp
from jax import lax
from jax.experimental import pallas as pl
from jax.experimental.pallas import tpu as pltpu
from jax.sharding import PartitionSpec as P

HID = 1024
NBINS = 2048


exponent_scale = 192.0 ** (-0.5) * math.log2(math.e)
norm_eps = 1e-06
masked_score = -1e30

NZ, NX, NY = 8, 4, 2
NQ = NX * NY
NR = NZ * NY
TOK = 8
CAP = 2
N_CTX = 4
N_EXPERTS = 64
ROPE = 64
VDIM = 128
DOC_ROWS = 16
KEY_PIECES = 2
SUBS = 2
MESH = pl.DeviceIdType.MESH


def remote(src, dst, send_sem, recv_sem, target):
    copy = pltpu.make_async_remote_copy(
        src_ref=src,
        dst_ref=dst,
        send_sem=send_sem,
        recv_sem=recv_sem,
        device_id=target,
        device_id_type=MESH,
    )
    copy.start()
    return copy


def greet(targets):
    barrier = pltpu.get_barrier_semaphore()
    for target in targets:
        pl.semaphore_signal(barrier, inc=1, device_id=target, device_id_type=MESH)
    pl.semaphore_wait(barrier, len(targets))


def small(cond):
    return cond.astype(jnp.float32).astype(jnp.bfloat16)


def split3(v):
    first = v.astype(jnp.bfloat16)
    rest = v - first.astype(jnp.float32)
    second = rest.astype(jnp.bfloat16)
    third = (rest - second.astype(jnp.float32)).astype(jnp.bfloat16)
    return first, second, third


def mm(a, b):
    return jnp.dot(a, b, preferred_element_type=jnp.float32)


def mm_t(a, b):
    return lax.dot_general(
        a, b, (((0,), (0,)), ((), ())), preferred_element_type=jnp.float32
    )


def attend_sum_kernel(
    part_a,
    query_ref,
    query_rope_ref,
    latent_ref,
    rope_ref,
    doc_ref,
    uv_hbm,
    weight_hbm,
    out_ref,
    uv_ref,
    weight_ref,
    nope_ref,
    tail_ref,
    keys,
    tails,
    top,
    denominator,
    accum,
    values_ref,
    partial_ref,
    a_first,
    a_slots,
    b_first,
    b_slots,
    a_push,
    a_got,
    b_mid,
    b_other,
    b_push,
    b_got,
    k_send_sem,
    k_recv_sem,
    t_send_sem,
    t_recv_sem,
    a_send_sem,
    a_recv_sem,
    b_send_sem,
    b_recv_sem,
    ap_send_sem,
    ap_recv_sem,
    bp_send_sem,
    bp_recv_sem,
    bc_send_sem,
    bc_recv_sem,
    load_sem,
):
    loads = [
        pltpu.make_async_copy(uv_hbm, uv_ref, load_sem.at[0]),
        pltpu.make_async_copy(weight_hbm, weight_ref, load_sem.at[1]),
    ]
    for load in loads:
        load.start()
    width = weight_ref.shape[1]
    wide_a, wide_b = part_a // (2 * SUBS), (width - part_a) // (2 * SUBS)
    me = lax.axis_index("exp")
    z, x, y = me // NQ, (me // NY) % NX, me % NY
    q = x * NY + y

    def at(z_at, x_at, y_at):
        return {"exp": (z_at * NX + x_at) * NY + y_at}

    q_peers = [(q + j) % NQ for j in range(NQ)]
    z_peers = [(z + j) % NZ for j in range(NZ)]
    y_other = at(z, x, 1 - y)
    z_next = [at((z + 1) % NZ, x, y), at((z + NZ - 1) % NZ, x, y)]
    x_next = [at(z, (x + 1) % NX, y), at(z, (x + NX - 1) % NX, y)]
    ctx = lax.axis_index("ctx")
    y_lo, core = ctx // 2, ctx % 2
    mate = {"ctx": y_lo * 2 + 1 - core, "exp": me}
    across = {"ctx": (1 - y_lo) * 2 + core, "exp": me}
    greet(
        [at(z, p // NY, p % NY) for p in q_peers[1:]]
        + [at(p, x, y) for p in z_peers[1:]]
        + [mate, across, {"ctx": 3 - ctx, "exp": me}]
    )

    block_len, lat = latent_ref.shape
    piece = block_len // KEY_PIECES
    for i in range(KEY_PIECES):
        tail_ref[i, :ROPE] = rope_ref[:, i * piece : (i + 1) * piece]
        tail_ref[i, ROPE:] = jnp.broadcast_to(
            doc_ref[:, i * piece : (i + 1) * piece].astype(jnp.float32),
            (DOC_ROWS, piece),
        ).astype(jnp.bfloat16)

    class KeyCopy:
        def __init__(self, back, i, forward, target):
            self.copies = [
                pltpu.make_async_remote_copy(
                    src_ref=src,
                    dst_ref=dst.at[i, back],
                    send_sem=send_sem.at[back, i],
                    recv_sem=recv_sem.at[back, i],
                    device_id=target,
                    device_id_type=MESH,
                )
                for src, dst, send_sem, recv_sem in (
                    (
                        keys.at[i, 1]
                        if forward
                        else latent_ref.at[i * piece : (i + 1) * piece],
                        keys,
                        k_send_sem,
                        k_recv_sem,
                    ),
                    (
                        tails.at[i, 1] if forward else tail_ref.at[i],
                        tails,
                        t_send_sem,
                        t_recv_sem,
                    ),
                )
            ]

        def start(self):
            for copy in self.copies:
                copy.start()

        def wait_recv(self):
            for copy in self.copies:
                copy.wait_recv()

        def wait_send(self):
            for copy in self.copies:
                copy.wait_send()

    for i in range(KEY_PIECES):

        @pl.when(y_lo == 0)
        def _():
            KeyCopy(1, i, False, across).start()

    for i in range(KEY_PIECES):

        @pl.when(core == 0)
        def _():
            KeyCopy(0, i, False, mate).start()

    def nt(a, b):
        return lax.dot_general(
            a, b, (((1,), (1,)), ((), ())), preferred_element_type=jnp.float32
        )

    heads = uv_ref.shape[0]
    part = block_len // 8

    def unpack(i, carry):
        here = pl.ds(pl.multiple_of(i * part, part), part)
        for head in range(heads):
            nope_ref[head, here] = query_ref[here, head]
        return carry

    lax.fori_loop(0, 8, unpack, 0)
    doc_pick = small(lax.broadcasted_iota(jnp.int32, (DOC_ROWS, 128), 0) == 0)
    query_docs = jnp.concatenate(
        [mm_t(tail_ref[i, ROPE:], doc_pick)[:, :1] for i in range(KEY_PIECES)], axis=0
    )

    def fold(block, tail, offset=None):
        first = offset == 0
        allowed = query_docs == tail[ROPE : ROPE + 1].astype(jnp.float32)
        if offset is not None:
            shape = (block_len, block.shape[0])
            query_at = lax.broadcasted_iota(jnp.int32, shape, 0)
            key_at = lax.broadcasted_iota(jnp.int32, shape, 1) + offset
            allowed = allowed & (key_at <= query_at)
        for head in range(heads):
            nope = nope_ref[head]
            rope = query_rope_ref[:, head * ROPE : (head + 1) * ROPE]
            raw = nt(nope, block) + mm(rope, tail[:ROPE])
            scores = jnp.where(allowed, raw, masked_score)
            peak = jnp.max(scores, axis=1, keepdims=True)
            if not first:
                old = top[head][:, :1]
                peak = jnp.maximum(old, peak)
                fade = jnp.exp2((old - peak) * exponent_scale)
            probs = jnp.exp2((scores - peak) * exponent_scale)
            mass = jnp.sum(probs, axis=1, keepdims=True)
            mixed = mm(probs.astype(jnp.bfloat16), block)
            if not first:
                mass = mass + denominator[head][:, :1] * fade
                mixed = mixed + accum[head] * fade
            top[head] = jnp.broadcast_to(peak, top.shape[1:])
            denominator[head] = jnp.broadcast_to(mass, denominator.shape[1:])
            accum[head] = mixed

    own_tail = jnp.concatenate([tail_ref[i] for i in range(KEY_PIECES)], axis=1)
    fold(latent_ref[...], own_tail, 0)

    def fold_pair(blocks):
        block = jnp.concatenate([keys[i, back] for i, back in blocks], axis=0)
        tail = jnp.concatenate([tails[i, back] for i, back in blocks], axis=1)
        fold(block, tail)

    def near_arrived(i):
        KeyCopy(0, i, False, mate).wait_recv()

    def far_arrived(i):
        KeyCopy(1, i, False, across).wait_recv()

    @pl.when(ctx == 1)
    def _():
        near_arrived(0)
        near_arrived(1)
        fold_pair(((0, 0), (1, 0)))

    @pl.when(ctx == 2)
    def _():
        for i in range(KEY_PIECES):
            far_arrived(i)
            near_arrived(i)
            fold_pair(((i, 0), (i, 1)))

    @pl.when(ctx == 3)
    def _():
        far_arrived(0)
        KeyCopy(0, 0, True, mate).start()
        near_arrived(0)
        near_arrived(1)
        fold_pair(((0, 0), (1, 0), (0, 1)))
        far_arrived(1)
        KeyCopy(0, 1, True, mate).start()
        fold(keys[1, 1], tails[1, 1])

    for load in loads:
        load.wait()
    for head in range(heads):
        context = (accum[head] / denominator[head][:, :1]).astype(jnp.bfloat16)
        values_ref[:, :, :, head * VDIM : (head + 1) * VDIM] = (
            mm(context, uv_ref[head])
            .astype(jnp.bfloat16)
            .reshape(NZ, NX, NY * TOK, VDIM)
        )

    def project(start, stop):
        rows = values_ref[...].reshape(block_len, heads * VDIM)
        for first in range(start, stop, 512):
            shape = (NZ, NX, NY * TOK, 512)
            product = mm(rows, weight_ref[:, first : first + 512])
            partial_ref[:, :, :, first : first + 512] = product.reshape(shape)

    def a_own(way, sub, chunk):
        start = (way * SUBS + sub) * wide_a
        return partial_ref[chunk, :, :, start : start + wide_a].reshape(-1, wide_a)

    def b_own(way, sub, chunk):
        start = part_a + (way * SUBS + sub) * wide_b
        return partial_ref[:, chunk, :, start : start + wide_b].reshape(-1, wide_b)

    a_flight, b_flight, pushes = {}, {}, []

    def ring_step(step, here, count, own_of, first, slots, sems, onward, flight):
        for sub in range(SUBS):
            for way in range(2):
                sign = -1 if way == 0 else 1
                own = own_of(way, sub, (here + sign * (1 + step) + 2 * count) % count)
                if step == 0:
                    src = first.at[way, sub]
                    first[way, sub] = own.astype(jnp.bfloat16)
                else:
                    src = slots.at[way, sub, step - 1]
                    flight[way, sub, step - 1].wait_recv()
                    slots[way, sub, step - 1] = (
                        slots[way, sub, step - 1].astype(jnp.float32) + own
                    ).astype(jnp.bfloat16)
                flight[way, sub, step] = remote(
                    src,
                    slots.at[way, sub, step],
                    sems[0].at[way, sub, step],
                    sems[1].at[way, sub, step],
                    onward[way],
                )

    def a_step(step):
        ring_step(
            step, z, NZ, a_own, a_first, a_slots,
            (a_send_sem, a_recv_sem), z_next, a_flight,
        )

    def b_step(step):
        ring_step(
            step, x, NX, b_own, b_first, b_slots,
            (b_send_sem, b_recv_sem), x_next, b_flight,
        )

    def a_push_out():
        for sub in range(SUBS):
            for way in range(2):
                own = a_own(way, sub, z)
                a_flight[way, sub, NZ - 2].wait_recv()
                own = own + a_slots[way, sub, NZ - 2].astype(jnp.float32)
                start = (way * SUBS + sub) * wide_a
                a_push[:, :, start : start + wide_a] = own.reshape(
                    NQ, TOK, wide_a
                ).astype(jnp.bfloat16)
        for j in range(1, NQ):
            p = q_peers[j]
            pushes.append(
                remote(
                    a_push.at[p],
                    a_got.at[j - 1],
                    ap_send_sem.at[j - 1],
                    ap_recv_sem.at[j - 1],
                    at(z, p // NY, p % NY),
                )
            )

    b_cross = []

    def b_cross_out():
        for sub in range(SUBS):
            for way in range(2):
                k = way * SUBS + sub
                own = b_own(way, sub, x)
                b_flight[way, sub, NX - 2].wait_recv()
                own = own + b_slots[way, sub, NX - 2].astype(jnp.float32)
                own = own.reshape(NZ, NY, TOK, wide_b)
                for y_at in range(NY):
                    b_mid[k, y_at] = own[:, y_at].astype(jnp.bfloat16)
                b_cross.append(
                    (
                        k,
                        remote(
                            b_mid.at[k, 1 - y],
                            b_other.at[k],
                            bc_send_sem.at[k],
                            bc_recv_sem.at[k],
                            y_other,
                        ),
                    )
                )

    def b_push_out():
        for k, copy in b_cross:
            copy.wait_recv()
            own = b_mid[k, y].astype(jnp.float32) + b_other[k].astype(jnp.float32)
            b_push[:, :, k * wide_b : (k + 1) * wide_b] = own.astype(jnp.bfloat16)
        for j in (4, 3, 5, 2, 6, 1, 7):
            p = z_peers[j]
            pushes.append(
                remote(
                    b_push.at[p],
                    b_got.at[j - 1],
                    bp_send_sem.at[j - 1],
                    bp_recv_sem.at[j - 1],
                    at(p, x, y),
                )
            )

    project(0, part_a)
    a_step(0)
    project(part_a, width)
    b_step(0)
    a_step(1)
    a_step(2)
    b_step(1)
    a_step(3)
    b_step(2)
    a_step(4)
    b_cross_out()
    a_step(5)
    b_push_out()
    a_step(6)
    a_push_out()
    for copy in pushes:
        copy.wait_recv()
    total = b_push[z].astype(jnp.float32)
    for j in range(NZ - 1):
        total = total + b_got[j].astype(jnp.float32)
    out_ref[:, part_a:] = total
    total = a_push[q].astype(jnp.float32)
    for j in range(NQ - 1):
        total = total + a_got[j].astype(jnp.float32)
    out_ref[:, :part_a] = total
    crossed = [copy for _, copy in b_cross]
    for copy in [*a_flight.values(), *b_flight.values(), *crossed, *pushes]:
        copy.wait_send()
    for i in range(KEY_PIECES):

        @pl.when(y_lo == 0)
        def _():
            KeyCopy(1, i, False, across).wait_send()

        @pl.when((core == 0) | (y_lo == 1))
        def _():
            KeyCopy(0, i, False, mate).wait_send()


def attend_scratch(latent, uv_weight, weight, part_a):
    heads, lat = uv_weight.shape[:2]
    rows = latent.shape[0]
    width = weight.shape[1]
    part_b = width - part_a
    wide_a, wide_b = part_a // (2 * SUBS), part_b // (2 * SUBS)
    bf16 = jnp.bfloat16
    dma = pltpu.SemaphoreType.DMA
    return [
            pltpu.VMEM(uv_weight.shape, bf16),
            pltpu.VMEM(weight.shape, bf16),
            pltpu.VMEM((heads, rows, lat), bf16),
            pltpu.VMEM((KEY_PIECES, ROPE + DOC_ROWS, rows // KEY_PIECES), bf16),
            pltpu.VMEM((KEY_PIECES, 2, rows // KEY_PIECES, lat), bf16),
            pltpu.VMEM((KEY_PIECES, 2, ROPE + DOC_ROWS, rows // KEY_PIECES), bf16),
            pltpu.VMEM((heads, rows, 128), jnp.float32),
            pltpu.VMEM((heads, rows, 128), jnp.float32),
            pltpu.VMEM((heads, rows, lat), jnp.float32),
            pltpu.VMEM((NZ, NX, NY * TOK, heads * VDIM), bf16),
            pltpu.VMEM((NZ, NX, NY * TOK, width), jnp.float32),
            pltpu.VMEM((2, SUBS, NQ * TOK, wide_a), bf16),
            pltpu.VMEM((2, SUBS, NZ - 1, NQ * TOK, wide_a), bf16),
            pltpu.VMEM((2, SUBS, NR * TOK, wide_b), bf16),
            pltpu.VMEM((2, SUBS, NX - 1, NR * TOK, wide_b), bf16),
            pltpu.VMEM((NQ, TOK, part_a), bf16),
            pltpu.VMEM((NQ - 1, TOK, part_a), bf16),
            pltpu.VMEM((2 * SUBS, NY, NZ, TOK, wide_b), bf16),
            pltpu.VMEM((2 * SUBS, NZ, TOK, wide_b), bf16),
            pltpu.VMEM((NZ, TOK, part_b), bf16),
            pltpu.VMEM((NZ - 1, TOK, part_b), bf16),
            dma((2, KEY_PIECES)),
            dma((2, KEY_PIECES)),
            dma((2, KEY_PIECES)),
            dma((2, KEY_PIECES)),
            dma((2, SUBS, NZ - 1)),
            dma((2, SUBS, NZ - 1)),
            dma((2, SUBS, NX - 1)),
            dma((2, SUBS, NX - 1)),
            dma((NQ - 1,)),
            dma((NQ - 1,)),
            dma((NZ - 1,)),
            dma((NZ - 1,)),
            dma((2 * SUBS,)),
            dma((2 * SUBS,)),
            dma((2,)),
    ]


def expert_loads(gate_hbm, up_hbm, down_hbm, gate_ref, up_ref, down_ref, load_sem):
    return [
        pltpu.make_async_copy(gate_hbm, gate_ref, load_sem.at[0]),
        pltpu.make_async_copy(up_hbm, up_ref, load_sem.at[1]),
        pltpu.make_async_copy(down_hbm, down_ref, load_sem.at[2]),
    ]


def experts_kernel(
    rows_ref,
    gate_hbm,
    up_hbm,
    down_hbm,
    out_ref,
    hist_ref,
    gate_ref,
    up_ref,
    down_ref,
    near,
    weigh,
    slots,
    inbox,
    kept,
    to_mate,
    from_mate,
    back,
    returned,
    to_y,
    from_y,
    own,
    to_z,
    from_z,
    hist_out,
    hist_in,
    load_sem,
    z_send,
    z_recv,
    y_send,
    y_recv,
    q_send,
    q_recv,
    m_send,
    m_recv,
    o_send,
    o_recv,
    b_send,
    b_recv,
    ys_send,
    ys_recv,
    zs_send,
    zs_recv,
    h_send,
    h_recv,
):
    width = down_hbm.shape[1]
    sent = width + 2 * N_EXPERTS
    half_rows, half_slots = NZ * TOK, NQ * NZ * CAP
    piece = NZ * CAP
    ctx, me = lax.axis_index("ctx"), lax.axis_index("exp")
    y_lo, core = ctx // 2, ctx % 2
    z, q = me // NQ, me % NQ

    def z_peer(z_at):
        return {"ctx": ctx, "exp": z_at * NQ + q}

    def q_peer(q_at):
        return {"ctx": ctx, "exp": z * NQ + q_at}

    y_peer = {"ctx": (1 - y_lo) * 2 + core, "exp": me}
    mate = {"ctx": y_lo * 2 + 1 - core, "exp": me}

    def c_peer(j):
        return {"ctx": (ctx + j) % N_CTX, "exp": me}

    loads = expert_loads(
        gate_hbm, up_hbm, down_hbm, gate_ref, up_ref, down_ref, load_sem
    )
    pending = []

    order = (4, 3, 5, 2, 6, 1, 7)
    near[y_lo, z] = rows_ref[...]
    hops = NZ // 2
    middle = rows_ref.shape[1] // 2
    onward = (z_peer((z + 1) % NZ), z_peer((z + NZ - 1) % NZ))
    ring = {}

    def pass_on(way, step, src, dst):
        ring[way, step] = remote(
            src, dst, z_send.at[way, step], z_recv.at[way, step], onward[way]
        )
        pending.append(ring[way, step])

    crossings = []

    def cross(src, dst):
        n = len(crossings)
        crossings.append(remote(src, dst, y_send.at[n], y_recv.at[n], y_peer))

    for way in range(2):
        pass_on(way, 0, rows_ref, near.at[y_lo, z])
    cross(rows_ref, near.at[y_lo, z])
    for step in range(1, hops):
        for way in range(2):
            z_from = (z + (NZ - step if way == 0 else step)) % NZ
            ring[way, step - 1].wait_recv()
            held = near.at[y_lo, z_from]
            if step < hops - 1:
                pass_on(way, step, held, held)
            else:
                side = pl.ds(way * middle, middle)
                part = near.at[y_lo, z_from, :, side]
                pass_on(way, step, part, part)
            cross(held, held)
    for way in range(2):
        ring[way, hops - 1].wait_recv()
    held = near.at[y_lo, (z + hops) % NZ]
    cross(held, held)
    pending += crossings

    lane = lax.broadcasted_iota(jnp.int32, (2 * N_EXPERTS, half_slots), 0)
    wanted = z * NQ + (
        lax.broadcasted_iota(jnp.int32, (2 * N_EXPERTS, half_slots), 1) // piece
    )
    pick_level, pick_rank = small(lane == wanted), small(lane == wanted + N_EXPERTS)
    row = lax.broadcasted_iota(jnp.int32, (half_rows, half_slots), 0)
    col = lax.broadcasted_iota(jnp.int32, (half_rows, half_slots), 1)
    same_source = (row // TOK) == ((col // CAP) % NZ)
    slot_rank = (col % CAP).astype(jnp.float32)

    q_order = (1, 2, 3, 4, 5, 6, 7)
    slot_flight = {}
    for half in range(2):
        if half == 1:
            for copy in crossings:
                copy.wait_recv()
        y_at = y_lo if half == 0 else 1 - y_lo
        held = (
            near[y_at]
            .astype(jnp.float32)
            .reshape(half_rows, sent + 2 * N_EXPERTS)
            .astype(jnp.bfloat16)
        )
        route = held[:, sent:]
        level, rank = mm(route, pick_level), mm(route, pick_rank)
        chosen = (level > 0.5) & (rank == slot_rank) & same_source
        weigh[half] = jnp.where(chosen, level, 0.0).astype(jnp.bfloat16)
        picked = mm_t(small(chosen), held[:, :sent])
        slots[half] = picked.astype(jnp.bfloat16).reshape(NQ, piece, sent)
        for j in q_order:
            p = (q + j) % NQ
            slot_flight[half, j] = remote(
                slots.at[half, p],
                inbox.at[half, 0, q],
                q_send.at[half, j],
                q_recv.at[half, j],
                q_peer(p),
            )
        inbox[half, 0, q] = slots[half, q]
    pending += slot_flight.values()

    bin_lane = lax.broadcasted_iota(jnp.int32, (2 * half_slots, 2 * N_EXPERTS), 1)
    bins_at = bin_lane.astype(jnp.float32)

    def run_block(half):
        block = inbox[half].reshape(2 * half_slots, sent)
        x = block[:, :width]
        gate_part, up_part = mm(x, gate_ref[...]), mm(x, up_ref[...])
        activation = gate_part / (1.0 + jnp.exp(-gate_part)) * up_part
        energy = jnp.sum(activation * activation, axis=1, keepdims=True) * (1.0 / HID)
        tail = block[:, width:].astype(jnp.float32)
        high = jnp.sum(jnp.where(bin_lane == me, tail, 0.0), axis=1, keepdims=True)
        low = jnp.sum(
            jnp.where(bin_lane == me + N_EXPERTS, tail, 0.0), axis=1, keepdims=True
        )
        at_high = jnp.where(high == bins_at, energy, 0.0)
        at_low = small(low == bins_at)
        first, second, third = split3(at_high)
        hist = mm_t(first, at_low) + mm_t(second, at_low) + mm_t(third, at_low)
        return activation.astype(jnp.bfloat16), hist

    back_flight = {}

    def run_half(half):
        flight = []
        for j in (0,) + q_order:
            q_from = (q + NQ - j) % NQ
            if j:
                slot_flight[half, j].wait_recv()
            flight.append(
                remote(
                    inbox.at[half, 0, q_from],
                    inbox.at[half, 1, q_from],
                    m_send.at[half, j],
                    m_recv.at[half, j],
                    mate,
                )
            )
        for copy in flight:
            copy.wait_recv()
        if half == 0:
            for load in loads:
                load.wait()
        hidden, hist = run_block(half)
        to_mate[half] = (
            mm(hidden[half_slots:], down_ref[...])
            .astype(jnp.bfloat16)
            .reshape(NQ, piece, width)
        )
        swap = remote(
            to_mate.at[half], from_mate.at[half], o_send.at[half], o_recv.at[half], mate
        )
        kept[...] = mm(hidden[:half_slots], down_ref[...])
        swap.wait_recv()
        total = kept[...] + from_mate[half].reshape(half_slots, width).astype(
            jnp.float32
        )
        back[half] = total.astype(jnp.bfloat16).reshape(NQ, piece, width)
        for j in q_order:
            p = (q + j) % NQ
            back_flight[half, j] = remote(
                back.at[half, p],
                returned.at[half, q],
                b_send.at[half, j],
                b_recv.at[half, j],
                q_peer(p),
            )
        returned[half, q] = back[half, q]
        pending.extend(flight + [swap])
        return hist

    hist = run_half(0)
    more = run_half(1)

    hist_out[...] = (hist + more)[: N_CTX * 8].reshape(N_CTX, 8, 2 * N_EXPERTS)
    hist_flight = [
        remote(
            hist_out.at[(ctx + j) % N_CTX],
            hist_in.at[j - 1],
            h_send.at[j - 1],
            h_recv.at[j - 1],
            c_peer(j),
        )
        for j in range(1, N_CTX)
    ]
    pending += hist_flight

    pending += back_flight.values()

    def mixed(half):
        for j in q_order:
            back_flight[half, j].wait_recv()
        return mm(weigh[half], returned[half].reshape(half_slots, width))

    own[...] = mixed(0).reshape(NZ, TOK, width)
    to_y[...] = mixed(1).reshape(NZ, TOK, width).astype(jnp.bfloat16)
    y_flight = {}
    for j in order + (0,):
        z_to = (z + j) % NZ
        y_flight[j] = remote(
            to_y.at[z_to], from_y.at[z_to], ys_send.at[j], ys_recv.at[j], y_peer
        )
    pending += y_flight.values()
    z_flight = []
    for j in order + (0,):
        z_to = (z + j) % NZ
        y_flight[j].wait_recv()
        to_z[z_to] = (own[z_to] + from_y[z_to].astype(jnp.float32)).astype(jnp.bfloat16)
        if j:
            z_flight.append(
                remote(
                    to_z.at[z_to],
                    from_z.at[j - 1],
                    zs_send.at[j - 1],
                    zs_recv.at[j - 1],
                    z_peer(z_to),
                )
            )
    pending += z_flight
    for copy in hist_flight:
        copy.wait_recv()
    hist = hist_out[ctx]
    for j in range(N_CTX - 1):
        hist = hist + hist_in[j]
    hist_ref[...] = hist
    for copy in z_flight:
        copy.wait_recv()
    total = to_z[z].astype(jnp.float32)
    for j in range(NZ - 1):
        total = total + from_z[j].astype(jnp.float32)
    out_ref[...] = total
    for copy in pending:
        copy.wait_send()


def expert_scratch(gate, up, down):
    width = down.shape[1]
    sent = width + 2 * N_EXPERTS
    half_slots, piece = NQ * NZ * CAP, NZ * CAP
    bf16, f32 = jnp.bfloat16, jnp.float32
    dma = pltpu.SemaphoreType.DMA
    return [
            pltpu.VMEM(gate.shape, bf16),
            pltpu.VMEM(up.shape, bf16),
            pltpu.VMEM(down.shape, bf16),
            pltpu.VMEM((2, NZ, TOK, sent + 2 * N_EXPERTS), bf16),
            pltpu.VMEM((2, NZ * TOK, half_slots), bf16),
            pltpu.VMEM((2, NQ, piece, sent), bf16),
            pltpu.VMEM((2, 2, NQ, piece, sent), bf16),
            pltpu.VMEM((half_slots, width), f32),
            pltpu.VMEM((2, NQ, piece, width), bf16),
            pltpu.VMEM((2, NQ, piece, width), bf16),
            pltpu.VMEM((2, NQ, piece, width), bf16),
            pltpu.VMEM((2, NQ, piece, width), bf16),
            pltpu.VMEM((NZ, TOK, width), bf16),
            pltpu.VMEM((NZ, TOK, width), bf16),
            pltpu.VMEM((NZ, TOK, width), f32),
            pltpu.VMEM((NZ, TOK, width), bf16),
            pltpu.VMEM((NZ - 1, TOK, width), bf16),
            pltpu.VMEM((N_CTX, 8, 2 * N_EXPERTS), f32),
            pltpu.VMEM((N_CTX - 1, 8, 2 * N_EXPERTS), f32),
            dma((3,)),
            dma((2, NZ // 2)),
            dma((2, NZ // 2)),
            dma((NZ,)),
            dma((NZ,)),
            dma((2, NQ)),
            dma((2, NQ)),
            dma((2, NQ)),
            dma((2, NQ)),
            dma((2,)),
            dma((2,)),
            dma((2, NQ)),
            dma((2, NQ)),
            dma((NZ,)),
            dma((NZ,)),
            dma((NZ - 1,)),
            dma((NZ - 1,)),
            dma((N_CTX - 1,)),
            dma((N_CTX - 1,)),
    ]


def fill_lanes(ids_ref, levels_ref, bins_ref, rows_ref, width):
    expert = lax.broadcasted_iota(jnp.int32, (TOK, N_EXPERTS), 1)
    none = jnp.zeros((TOK, N_EXPERTS), jnp.int32)
    high, low, level, named = none, none, none, none
    for k in range(ids_ref.shape[1]):
        here = ids_ref[:, k : k + 1] == expert
        bins = bins_ref[:, k : k + 1]
        high = high + jnp.where(here, bins >> 6, 0)
        low = low + jnp.where(here, bins & 63, 0)
        level = level + jnp.where(here, levels_ref[:, k : k + 1], 0)
        named = named + jnp.where(here, 1, 0)
    row = lax.broadcasted_iota(jnp.int32, (TOK, N_EXPERTS), 0)
    rank = none
    for t in range(TOK - 1):
        rank = rank + jnp.where(row > t, named[t : t + 1], 0)
    for i, lanes in enumerate((high, low, level, rank)):
        rows_ref[:, width + i * N_EXPERTS : width + (i + 1) * N_EXPERTS] = lanes.astype(
            jnp.float32
        ).astype(jnp.bfloat16)


def layer_kernel(part_a, attend_count, *refs):
    attend_in, (residual, gain, ids, levels, bins), weights = (
        refs[:7],
        refs[7:12],
        refs[12:15],
    )
    layer_out, hist_out = refs[15:17]
    attended, mixture, rows = refs[17:20]
    attend_refs = refs[20 : 20 + attend_count]
    expert_refs = refs[20 + attend_count :]
    for load in expert_loads(*weights, *expert_refs[:3], expert_refs[19]):
        load.start()
    width = residual.shape[1]
    fill_lanes(ids, levels, bins, rows, width)
    attend_sum_kernel(part_a, *attend_in, attended, *attend_refs)
    state = residual[...].astype(jnp.float32) + attended[...]
    attended[...] = state
    mean = jnp.mean(state * state, axis=1, keepdims=True)
    rows[:, :width] = (state * lax.rsqrt(mean + norm_eps) * gain[...][None]).astype(
        jnp.bfloat16
    )
    experts_kernel(rows, *weights, mixture, hist_out, *expert_refs)
    total = jnp.sum(levels[...].astype(jnp.float32), axis=1, keepdims=True)
    layer_out[...] = attended[...] + mixture[...] / total


def run_layer(attend_in, uv_weight, weight, row_in, gate, up, down, part_a=2048):
    width = weight.shape[1]
    vmem = pl.BlockSpec(memory_space=pltpu.VMEM)
    hbm = pl.BlockSpec(memory_space=pltpu.HBM)
    attend_refs = attend_scratch(attend_in[2], uv_weight, weight, part_a)
    return pl.pallas_call(
        functools.partial(layer_kernel, part_a, len(attend_refs)),
        out_shape=(
            jax.ShapeDtypeStruct((TOK, width), jnp.float32),
            jax.ShapeDtypeStruct((8, 2 * N_EXPERTS), jnp.float32),
        ),
        in_specs=[vmem] * 5 + [hbm] * 2 + [vmem] * 5 + [hbm] * 3,
        out_specs=(vmem, vmem),
        scratch_shapes=[
            pltpu.VMEM((TOK, width), jnp.float32),
            pltpu.VMEM((TOK, width), jnp.float32),
            pltpu.VMEM((TOK, width + 4 * N_EXPERTS), jnp.bfloat16),
            *attend_refs,
            *expert_scratch(gate, up, down),
        ],
        compiler_params=pltpu.CompilerParams(
            collective_id=0, has_side_effects=True, vmem_limit_bytes=60 << 20
        ),
        name="layer",
    )(*attend_in, uv_weight, weight, *row_in, gate, up, down)


def on_device(
    residual_in,
    norm_gain,
    q_nope,
    q_rope,
    latent,
    k_rope,
    doc_ids,
    uv_weight,
    out_weight,
    expert_ids,
    gate_levels,
    bin_ids,
    gate_weight,
    up_weight,
    down_weight,
):
    block_len = q_nope.shape[0]
    layer_out, hist = run_layer(
        (q_nope, q_rope, latent, k_rope.T, doc_ids.reshape(1, block_len)),
        uv_weight,
        out_weight,
        (residual_in, norm_gain, expert_ids, gate_levels, bin_ids),
        gate_weight[0],
        up_weight[0],
        down_weight[0],
    )
    layer_out = layer_out.astype(jnp.bfloat16)
    histogram = hist[:, : NBINS // 32].reshape(1, NBINS // N_CTX)
    return (layer_out, histogram)


def solution(mesh):
    return jax.shard_map(
        on_device,
        mesh=mesh,
        in_specs=(
            P(("ctx", "exp"), None),
            P(),
            P("ctx", "exp", None),
            P("ctx", "exp"),
            P("ctx", None),
            P("ctx", None),
            P("ctx"),
            P("exp", None, None),
            P("exp", None),
            P(("ctx", "exp"), None),
            P(("ctx", "exp"), None),
            P(("ctx", "exp"), None),
            P("exp", None, "ctx"),
            P("exp", None, "ctx"),
            P("exp", "ctx", None),
        ),
        out_specs=(P(("ctx", "exp"), None), P("exp", "ctx")),
        check_vma=False,
    )
```
